32 devices in a mesh: chan: 4 (over y, x), strip: 8 (over z, core).
Axes of the slice: x: 2, y: 2, z: 4, core: 2. Of those that a mesh axis runs over, the one named last changes fastest.
Arguments:
- wave_field: float32 [2, 16, 1536, 1536], P(None, 'chan', 'strip'), may hold values from -6 to 6
- radial_op: float32 [1536, 1536], replicated, may hold values from -1 to 1, as said below
- coupling: float32 [2, 16, 8], replicated, may hold values from -4 to 4
- couple: int32 [16, 8], replicated, may hold values from 0 to 15
- partner: int32 [16], replicated, may hold values from 0 to 15, as said below
- extent: int32 [16], replicated, may hold values from 384 to 1536, as said below
Outputs:
- first_step: float32 [2, 16, 1536, 1536], P(None, None, 'strip', 'chan')
- second_step: float32 [2, 16, 1536, 1536], P(None, None, 'strip', 'chan')
The draws below stay inside these ranges and needn't reach their ends.
Inputs may be any that keep to these rules, and one draw needn't show every extreme that they name: radial_op is symmetric. partner pairs the channels: partner(partner(c)) == c and partner(c) != c. Each extent is a multiple of 96; some channel has extent 1536 and some 1536 // 4.
All inputs are finite; a program needn't handle non-finite values.
Results may differ from the reference program's by a relative error of at most 0.0003.
Values sent between devices are 32-bit elements; how exact they have to be, the bound alone decides.
A program may use at most 256 MiB of HBM per device.

```python
import jax
import jax.numpy as jnp
from jax import lax

NR = 1536
CH = 16
MULT = 8


def draw_radial_op(key, part):
    noise = jnp.clip(jax.random.normal(key, (NR, NR), jnp.float32), -6.0, 6.0)
    sym = (noise + noise.T) * (0.35 / jnp.sqrt(2.0 * NR))
    diagonal = jax.random.uniform(jax.random.fold_in(key, 1), (NR,), jnp.float32, -0.5, 0.5)
    return sym + jnp.diag(diagonal)


def draw_partner(key, part):
    order = jax.random.permutation(key, CH).astype(jnp.int32)
    paired = jnp.zeros((CH,), jnp.int32)
    paired = paired.at[order[0::2]].set(order[1::2])
    paired = paired.at[order[1::2]].set(order[0::2])
    return paired


def draw_extent(key, part):
    steps = jax.random.randint(key, (CH,), 0, 13).astype(jnp.int32)
    order = jax.random.permutation(jax.random.fold_in(key, 1), CH).astype(jnp.int32)
    steps = steps.at[order[0]].set(0)
    steps = steps.at[order[1]].set(12)
    return (NR - steps * (NR // 16)).astype(jnp.int32)


def with_ends(array, key, least, largest):
    longest = array.shape.index(max(array.shape))
    spots = []
    for shift in (0, 1):
        where = [jax.random.randint(jax.random.fold_in(key, axis), (), 0, length) for axis, length in enumerate(array.shape)]
        where[longest] = (where[longest] + shift) % array.shape[longest]
        spots.append(tuple(where))
    return array.at[spots[0]].set(least).at[spots[1]].set(largest)


def block_scale(stream_key, shape, pieces, smallest, largest):
    def one(axis_at, blocks):
        steps = jax.random.uniform(jax.random.fold_in(jax.random.fold_in(stream_key, 6), axis_at), (blocks,), jnp.float32, smallest / len(pieces), largest / len(pieces))
        return jnp.repeat(jnp.exp(steps), shape[axis_at] // blocks).reshape((-1,) + (1,) * (len(shape) - axis_at - 1))

    factor_of = one(*pieces[0])
    for cut in pieces[1:]:
        factor_of = factor_of * one(*cut)
    return factor_of


def centred(key, dims, spread, most, cuts=(), dtype=jnp.bfloat16):
    values = jax.random.normal(key, dims, jnp.float32) * spread
    if len(cuts) > 0:
        values = block_scale(key, dims, cuts, -0.22, 0.18) * values
    return jnp.clip(values, min=-most, max=most).astype(dtype)


def setup_inputs(seed: int = 0) -> dict:
    arg_keys = jax.random.split(jax.random.key(seed), 7)
    return {
        "wave_field": centred(arg_keys[0], (2, CH, NR, NR), 1.0, 6.0, ((1, 4), (2, 8)), jnp.float32),
        "radial_op": draw_radial_op(jax.random.fold_in(arg_keys[6], 71), 0),
        "coupling": centred(arg_keys[2], (2, CH, MULT), 0.3, 4.0, (), jnp.float32),
        "couple": with_ends(jax.random.randint(arg_keys[3], (CH, MULT), 0, CH), jax.random.fold_in(arg_keys[3], 1), 0, CH - 1).astype(jnp.int32),
        "partner": draw_partner(jax.random.fold_in(arg_keys[6], 71), 0),
        "extent": draw_extent(jax.random.fold_in(arg_keys[6], 71), 0),
    }


def potentials(row_pos, col_pos, count, orders):
    spacing = 8.0 / count
    first = row_pos.astype(jnp.float32) * spacing
    second = col_pos.astype(jnp.float32) * spacing
    lesser = jnp.minimum(first[:, None], second[None, :])
    greater = jnp.maximum(first[:, None], second[None, :])
    root = jnp.sqrt(greater * greater + 1.0)
    result = []
    for order in range(orders):
        result.append(lesser ** order / root ** (order + 1))
    return result

def reference(wave_field, radial_op, coupling, couple, partner, extent):
    positions = jnp.arange(NR).astype(jnp.int32)
    pots = potentials(positions, positions, NR, MULT)

    def apply(field):
        image = jnp.einsum('ak,pckb->pcab', radial_op, field, precision=lax.Precision.HIGHEST)

        def single(channel):
            total = image[:, channel] + jnp.swapaxes(image[:, partner[channel]], 1, 2)
            real_part = total[0]
            imag_part = total[1]
            for order in range(MULT):
                source = field[:, couple[channel, order]]
                c_real = coupling[0, channel, order]
                c_imag = coupling[1, channel, order]
                real_part = real_part + pots[order] * (c_real * source[0] - c_imag * source[1])
                imag_part = imag_part + pots[order] * (c_real * source[1] + c_imag * source[0])
            live = (positions[:, None] < extent[channel]) & (positions[None, :] < extent[channel])
            return jnp.where(live[None], jnp.stack([real_part, imag_part]), 0.0)
        return jnp.moveaxis(lax.map(single, jnp.arange(CH).astype(jnp.int32)), 0, 1)
    first_step = apply(wave_field)
    second_step = 2.0 * apply(first_step) - wave_field
    return (first_step, second_step)
```

```python
import functools

import jax
import jax.numpy as jnp
from jax import lax
from jax.experimental import pallas as pl
from jax.experimental.pallas import tpu as pltpu
from jax.sharding import PartitionSpec as P


def potentials(row_pos, col_pos, count, orders):
    spacing = 8.0 / count
    first = row_pos.astype(jnp.float32) * spacing
    second = col_pos.astype(jnp.float32) * spacing
    lesser = jnp.minimum(first[:, None], second[None, :])
    greater = jnp.maximum(first[:, None], second[None, :])
    root = jnp.sqrt(greater * greater + 1.0)
    result = []
    for order in range(orders):
        result.append(lesser**order / root ** (order + 1))
    return result


def couple_terms(field, image_rows, mirrored, coupling, couple, partner, pots, live):
    total = image_rows + jnp.take(mirrored, partner, axis=1)
    real_part = total[0]
    imag_part = total[1]
    for order in range(len(pots)):
        source = jnp.take(field, couple[:, order], axis=1)
        c_real = coupling[0, :, order][:, None, None]
        c_imag = coupling[1, :, order][:, None, None]
        real_part = real_part + pots[order] * (c_real * source[0] - c_imag * source[1])
        imag_part = imag_part + pots[order] * (c_real * source[1] + c_imag * source[0])
    return jnp.where(live[None], jnp.stack([real_part, imag_part]), 0.0)


def radial_product(radial_op, block):
    return jnp.einsum("ak,pckb->pcab", radial_op, block, precision=lax.Precision.HIGHEST)


def spread_columns(field):
    strips = lax.axis_size("strip")
    local_chans = field.shape[1]
    local_rows = field.shape[2]
    grid = field.shape[3]
    piece = grid // (strips * strips)
    shaped = field.reshape(2, local_chans, local_rows, strips, strips, piece)
    return jnp.transpose(shaped, (0, 1, 2, 4, 3, 5)).reshape(2, local_chans, local_rows, grid)


def spread_tiles(image):
    chans = lax.axis_size("chan")
    strips = lax.axis_size("strip")
    local_chans = image.shape[1]
    grid = image.shape[2]
    width = image.shape[3]
    piece = grid // (strips * strips)
    ratio = strips // chans
    block = grid // chans
    direct_send = image.reshape(2, local_chans, strips, width, chans, ratio * piece)
    direct_send = jnp.transpose(direct_send, (0, 1, 4, 2, 3, 5)).reshape(
        2, local_chans, chans * strips, width, ratio * piece
    )
    mirror_send = image.reshape(2, local_chans, chans, block, strips, piece)
    mirror_send = jnp.transpose(mirror_send, (0, 1, 2, 4, 3, 5)).reshape(
        2, local_chans, chans * strips, block, piece
    )
    direct_got, mirror_got = (
        lax.all_to_all(direct_send, ("chan", "strip"), split_axis=2, concat_axis=2, tiled=True),
        lax.all_to_all(mirror_send, ("chan", "strip"), split_axis=2, concat_axis=2, tiled=True),
    )
    direct_got = direct_got.reshape(2, local_chans, chans, strips, width, ratio, piece)
    direct_tiles = jnp.transpose(direct_got, (0, 2, 1, 4, 5, 3, 6)).reshape(
        2, chans * local_chans, width, block
    )
    mirror_got = mirror_got.reshape(2, local_chans, chans, strips, block, piece)
    mirror_tiles = jnp.transpose(mirror_got, (0, 2, 1, 3, 5, 4)).reshape(
        2, chans * local_chans, width, block
    )
    return (direct_tiles, mirror_tiles)


def general(wave_field, radial_op, coupling, couple, partner, extent):
    chans = lax.axis_size("chan")
    grid = wave_field.shape[3]
    strip_rows = wave_field.shape[2]
    chan_cols = grid // chans
    row_pos = lax.axis_index("strip") * strip_rows + jnp.arange(strip_rows)
    col_pos = lax.axis_index("chan") * chan_cols + jnp.arange(chan_cols)
    pots = potentials(row_pos, col_pos, grid, coupling.shape[2])
    live = (row_pos[None, :, None] < extent[:, None, None]) & (
        col_pos[None, None, :] < extent[:, None, None]
    )

    def radial(block):
        return radial_product(radial_op, block)

    def product_columns(field_rows):
        return radial(lax.all_to_all(field_rows, "strip", split_axis=3, concat_axis=2, tiled=True))

    field_tiles = lax.all_to_all(wave_field, "chan", split_axis=3, concat_axis=1, tiled=True)
    rows_tiles, mirror_tiles = spread_tiles(product_columns(spread_columns(wave_field)))
    first_step = couple_terms(
        field_tiles, rows_tiles, mirror_tiles, coupling, couple, partner, pots, live
    )
    image = product_columns(
        spread_columns(lax.all_to_all(first_step, "chan", split_axis=1, concat_axis=3, tiled=True))
    )
    rows_tiles, mirror_tiles = spread_tiles(image)
    applied = couple_terms(
        first_step, rows_tiles, mirror_tiles, coupling, couple, partner, pots, live
    )
    second_step = 2.0 * applied - field_tiles
    return (first_step, second_step)


MESH = pl.DeviceIdType.MESH
ANY = pl.BlockSpec(memory_space=pl.ANY)


def rem(value, count):
    return lax.rem(value, count)


def greet(others):
    barrier = pltpu.get_barrier_semaphore()
    for other in others:
        pl.semaphore_signal(barrier, inc=1, device_id=other, device_id_type=MESH)
    pl.semaphore_wait(barrier, len(others))


def remote(source, target, send, recv, device):
    return pltpu.make_async_remote_copy(
        src_ref=source,
        dst_ref=target,
        send_sem=send,
        recv_sem=recv,
        device_id=device,
        device_id_type=MESH,
    )


def columns(block, width):
    return pl.ds(pl.multiple_of(block * width, 128), width)


def lines(block, height):
    return pl.ds(pl.multiple_of(block * height, 8), height)


def split(read, high, low, count, step):
    def one(n, carry):
        at = pl.ds(pl.multiple_of(n * step, step), step)
        value = read(at)
        top = value.astype(jnp.bfloat16)
        high[at, :] = top
        low[at, :] = (value - top.astype(jnp.float32)).astype(jnp.bfloat16)
        return carry

    lax.fori_loop(0, count // step, one, 0)


def load_operator(radial, turned, rh, rl, sems):
    per, width, grid = turned.shape
    loads = [
        pltpu.make_async_copy(radial.at[pl.ds(n * width, width), :], turned.at[n], sems.at[n])
        for n in range(grid // width)
    ]
    return loads


def split_operator(loads, turned, rh, rl):
    width = turned.shape[1]
    for n, load in enumerate(loads):
        load.wait()
        split(
            lambda at, n=n: turned[n, at, :],
            rh.at[pl.ds(n * width, width), :],
            rl.at[pl.ds(n * width, width), :],
            width,
            32,
        )


def product(j, y, img, turned, rh, rl, yh, yl):
    grid = y.shape[1]
    step = 256
    split(lambda at: y[j, at, :], yh, yl, grid, 64)

    def one(n, carry):
        at = pl.ds(pl.multiple_of(n * step, step), step)
        top = rh[at, :]
        total = jnp.dot(top, yh[...], preferred_element_type=jnp.float32)
        total = total + jnp.dot(top, yl[...], preferred_element_type=jnp.float32)
        total = total + jnp.dot(rl[at, :], yh[...], preferred_element_type=jnp.float32)
        img[j, at, :] = total
        turned[j, :, at] = total.T
        return carry

    lax.fori_loop(0, grid // step, one, 0)


def far_order(strips):
    half = strips // 2
    return sorted(range(1, strips), key=lambda d: (abs(d - half), d))


def chunks(per, body):
    def one(j, carry):
        body(j)
        return carry

    lax.fori_loop(0, per, one, 0)


class Spread:
    def __init__(self, c, s, chans, strips, img, turned, w, mt, dd, sems):
        self.c, self.s, self.chans, self.strips = c, s, chans, strips
        self.img, self.turned, self.w, self.mt, self.dd = img, turned, w, mt, dd
        self.zs, self.zr, self.ms, self.mr, self.fs, self.fr, self.ls = sems
        self.rows = w.shape[2]
        self.width = w.shape[3]
        self.member = rem(s, 2)
        group = s // 2
        self.ring = [(c, rem(s + d, strips)) for d in range(1, strips)]
        self.plane = [
            (rem(c + r, chans), group * 2 + rem(self.member + e, 2))
            for r in range(chans)
            for e in range(2)
        ]

    def hop(self, j, d):
        t = self.ring[d - 1][1]
        return remote(
            self.img.at[j, lines(t, self.rows), :],
            self.w.at[j, self.s],
            self.zs.at[j, d],
            self.zr.at[j, d],
            self.ring[d - 1],
        )

    def mirror(self, j, k):
        slot = self.member * self.chans + self.c
        to = self.plane[k][0]
        m = rem(self.member + k % 2, 2)
        part = self.turned.at[j, lines(m, self.rows), columns(to, self.width)]
        if k == 0:
            return pltpu.make_async_copy(part, self.mt.at[slot, j], self.ls.at[j, 2])
        return remote(
            part, self.mt.at[slot, j], self.ms.at[j, k], self.mr.at[j, k], self.plane[k]
        )

    def forward(self, source, j, u):
        to = u // 2
        p = rem(u, 2)
        away = rem(to - self.c + self.chans, self.chans)
        target = self.dd.at[p * self.chans + self.c, j]

        @pl.when(away == 0)
        def _():
            pltpu.make_async_copy(source, target, self.ls.at[j, p]).start()

        @pl.when(away != 0)
        def _():
            k = away * 2 + p
            remote(source, target, self.fs.at[j, k], self.fr.at[j, k], (to, self.s)).start()

    def start(self, j):
        for d in far_order(self.strips):
            self.hop(j, d).start()
        for k in reversed(range(2 * self.chans)):
            self.mirror(j, k).start()

    def relay(self, j):
        self.forward(self.img.at[j, lines(self.s, self.rows), :], j, self.s)
        for d in far_order(self.strips)[::-1]:
            self.hop(j, d).wait_recv()
            u = rem(self.s - d + self.strips, self.strips)
            self.forward(self.w.at[j, u], j, u)

    def finish(self, j):
        for d in range(1, self.strips):
            self.hop(j, d).wait_send()
        for k in range(2 * self.chans):
            self.mirror(j, k).wait()
        for p in range(2):
            own = self.dd.at[p * self.chans + self.c, j]
            pltpu.make_async_copy(self.w.at[j, 0], own, self.ls.at[j, p]).wait()
            for r in range(1, self.chans):
                k = r * 2 + p
                sender = rem(self.c - r + self.chans, self.chans)
                remote(
                    self.w.at[j, 0],
                    self.dd.at[p * self.chans + sender, j],
                    self.fs.at[j, k],
                    self.fr.at[j, k],
                    (rem(self.c + r, self.chans), self.s),
                ).wait()


def first_kernel(
    chans, strips, x, radial, f, mt, dd, y, img, turned, w, rh, rl, yh, yl,
    gs, gr, gl, cs, cr, cl, rs, zs, zr, ms, mr, fs, fr, ls,
):
    c = lax.axis_index("chan")
    s = lax.axis_index("strip")
    per, _, width = y.shape
    rows = x.shape[1]
    spread = Spread(c, s, chans, strips, img, turned, w, mt, dd, (zs, zr, ms, mr, fs, fr, ls))
    greet(spread.ring + spread.plane[2:])

    def gather(j, d):
        t = spread.ring[d - 1][1]
        return remote(
            x.at[rem(t, 2) * per + j, :, columns(t // 2, width)],
            y.at[j, lines(s, rows), :],
            gs.at[j, d],
            gr.at[j, d],
            spread.ring[d - 1],
        )

    def keep(j):
        return pltpu.make_async_copy(
            x.at[rem(s, 2) * per + j, :, columns(s // 2, width)],
            y.at[j, lines(s, rows), :],
            gl.at[j],
        )

    def field(p, r):
        to = rem(c + r, chans)
        part = x.at[pl.ds(p * per, per), :, columns(to, width)]
        target = f.at[p * chans + c]
        if r == 0:
            return pltpu.make_async_copy(part, target, cl.at[p])
        return remote(part, target, cs.at[r * 2 + p], cr.at[r * 2 + p], (to, s))

    def begin(j):
        for d in far_order(strips):
            gather(j, d).start()
        keep(j).start()

    fields = [field(p, r) for r in range(chans) for p in range(2)]
    loads = load_operator(radial, turned, rh, rl, rs)
    chunks(per, begin)
    for load in loads:
        load.start()
    for copy in fields:
        copy.start()
    split_operator(loads, turned, rh, rl)

    def work(j):
        keep(j).wait()
        for d in range(1, strips):
            gather(j, d).wait_recv()
        product(j, y, img, turned, rh, rl, yh, yl)
        spread.start(j)

    chunks(per, work)
    chunks(per, spread.relay)

    def finish(j):
        for d in range(1, strips):
            gather(j, d).wait_send()
        spread.finish(j)

    for copy in fields:
        copy.wait()
    chunks(per, finish)


def second_kernel(
    chans, strips, v, radial, b, mt, dd, y, img, turned, w, rh, rl, yh, yl,
    bs, br, gs, gr, gl, rs, zs, zr, ms, mr, fs, fr, ls,
):
    c = lax.axis_index("chan")
    s = lax.axis_index("strip")
    per = y.shape[0]
    rows = v.shape[2]
    spread = Spread(c, s, chans, strips, img, turned, w, mt, dd, (zs, zr, ms, mr, fs, fr, ls))
    greet(spread.ring + spread.plane[2:])

    def back(j, r, p):
        to = rem(c + r, chans)
        k = r * 2 + p
        return remote(
            v.at[p * chans + to, j], b.at[p * chans + c, j], bs.at[j, k], br.at[j, k], (to, s)
        )

    def forward(source, j, block, p):
        t = block * 2 + p
        away = rem(t - s + strips, strips)
        target = y.at[j, lines(s, rows), :]

        @pl.when(away == 0)
        def _():
            pltpu.make_async_copy(source, target, gl.at[j]).start()

        @pl.when(away != 0)
        def _():
            remote(source, target, gs.at[j, away], gr.at[j, away], (c, t)).start()

    def begin(j):
        for r in reversed(range(1, chans)):
            for p in range(2):
                back(j, r, p).start()

    def relay(j):
        for p in range(2):
            forward(v.at[p * chans + c, j], j, c, p)
        for r in reversed(range(1, chans)):
            sender = rem(c - r + chans, chans)
            for p in range(2):
                back(j, r, p).wait_recv()
                forward(b.at[p * chans + sender, j], j, sender, p)

    loads = load_operator(radial, turned, rh, rl, rs)
    chunks(per, begin)
    for load in loads:
        load.start()
    chunks(per, relay)
    split_operator(loads, turned, rh, rl)

    def arrive(j, d):
        u = rem(s - d + strips, strips)
        return remote(
            v.at[0, 0],
            y.at[j, lines(u, rows), :],
            gs.at[j, d],
            gr.at[j, d],
            spread.ring[d - 1],
        )

    def work(j):
        pltpu.make_async_copy(v.at[0, 0], y.at[j, lines(s, rows), :], gl.at[j]).wait()
        for d in range(1, strips):
            arrive(j, d).wait_recv()
        product(j, y, img, turned, rh, rl, yh, yl)
        spread.start(j)

    chunks(per, work)
    chunks(per, spread.relay)

    def finish(j):
        for r in range(1, chans):
            for p in range(2):
                back(j, r, p).wait_send()
        for d in range(1, strips):
            arrive(j, d).wait_send()
        spread.finish(j)

    chunks(per, finish)


def exchange(kernel, ident, outs, buffers, sems, *operands):
    chans = lax.axis_size("chan")
    strips = lax.axis_size("strip")
    return pl.pallas_call(
        functools.partial(kernel, chans, strips),
        out_shape=[jax.ShapeDtypeStruct(shape, jnp.float32) for shape in outs],
        in_specs=[ANY] * len(operands),
        out_specs=[ANY] * len(outs),
        scratch_shapes=[pltpu.VMEM(*buffer) for buffer in buffers]
        + [pltpu.SemaphoreType.DMA(n) for n in sems],
        compiler_params=pltpu.CompilerParams(
            collective_id=ident, has_side_effects=True, vmem_limit_bytes=60 * 2**20
        ),
    )(*operands)


def couple_kernel(count, last, ints, reals, *refs):
    if last:
        field, direct, mirror, base, out, pots = refs
    else:
        field, direct, mirror, out, pots = refs
    channels, height, width = field.shape[1:]
    orders = pots.shape[0]
    spacing = 8.0 / count
    row = ints[0] + pl.program_id(0) * height
    row = row + lax.broadcasted_iota(jnp.int32, (height, width), 0)
    col = ints[1] + lax.broadcasted_iota(jnp.int32, (height, width), 1)
    first = row.astype(jnp.float32) * spacing
    second = col.astype(jnp.float32) * spacing
    greater = jnp.maximum(first, second)
    root = jnp.sqrt(greater * greater + 1.0)
    ratio = jnp.minimum(first, second) / root
    pot = 1.0 / root
    for order in range(orders):
        pots[order] = pot
        pot = pot * ratio
    reach = jnp.maximum(row, col)

    def channel(c, carry):
        other = ints[2 + c]
        real_part = direct[0, c] + mirror[0, other]
        imag_part = direct[1, c] + mirror[1, other]
        for order in range(orders):
            k = ints[2 + 2 * channels + c * orders + order]
            c_real = reals[c * orders + order]
            c_imag = reals[channels * orders + c * orders + order]
            pot = pots[order]
            s_real = pot * field[0, k]
            s_imag = pot * field[1, k]
            real_part = real_part + (c_real * s_real - c_imag * s_imag)
            imag_part = imag_part + (c_real * s_imag + c_imag * s_real)
        live = reach < ints[2 + channels + c]
        real_part = jnp.where(live, real_part, 0.0)
        imag_part = jnp.where(live, imag_part, 0.0)
        if last:
            real_part = 2.0 * real_part - base[0, c]
            imag_part = 2.0 * imag_part - base[1, c]
        out[0, c] = real_part
        out[1, c] = imag_part
        return carry

    lax.fori_loop(0, channels, channel, 0)


def couple_tiles(count, ints, reals, orders, arrays):
    last = len(arrays) == 4
    shape = arrays[0].shape
    height = 16
    block = pl.BlockSpec((2, shape[1], height, shape[3]), lambda n: (0, 0, n, 0))
    smem = pl.BlockSpec(memory_space=pltpu.SMEM)
    return pl.pallas_call(
        functools.partial(couple_kernel, count, last),
        grid=(shape[2] // height,),
        out_shape=jax.ShapeDtypeStruct(shape, jnp.float32),
        in_specs=[smem, smem] + [block] * len(arrays),
        out_specs=block,
        scratch_shapes=[pltpu.VMEM((orders, height, shape[3]), jnp.float32)],
    )(ints, reals, *arrays)


def local(wave_field, radial_op, coupling, couple, partner, extent):
    chans = lax.axis_size("chan")
    strips = lax.axis_size("strip")
    per, rows, grid = wave_field.shape[1:]
    width = grid // chans
    orders = coupling.shape[2]
    tiles = (2 * chans, per, rows, width)
    whole = (2, chans * per, rows, width)
    starts = jnp.stack([lax.axis_index("strip") * rows, lax.axis_index("chan") * width])
    ints = jnp.concatenate([starts.astype(jnp.int32), partner, extent, couple.reshape(-1)])
    reals = coupling.reshape(-1)
    buffers = [
        ((per, grid, width), jnp.float32),
        ((per, grid, width), jnp.float32),
        ((per, width, grid), jnp.float32),
        ((per, strips, rows, width), jnp.float32),
        ((grid, grid), jnp.bfloat16),
        ((grid, grid), jnp.bfloat16),
        ((grid, width), jnp.bfloat16),
        ((grid, width), jnp.bfloat16),
    ]
    ring = (per, strips)
    plane = (per, 2 * chans)
    spread = [(chans,), ring, ring, plane, plane, plane, plane, (per, 3)]
    field, mirror, direct = exchange(
        first_kernel,
        0,
        [tiles, tiles, tiles],
        buffers,
        [ring, ring, (per,), (2 * chans,), (2 * chans,), (2,)] + spread,
        wave_field.reshape(2 * per, rows, grid),
        radial_op,
    )
    field = field.reshape(whole)
    first_step = couple_tiles(
        grid, ints, reals, orders, (field, direct.reshape(whole), mirror.reshape(whole))
    )
    _, mirror, direct = exchange(
        second_kernel,
        1,
        [tiles, tiles, tiles],
        buffers,
        [plane, plane, ring, ring, (per,)] + spread,
        first_step.reshape(tiles),
        radial_op,
    )
    second_step = couple_tiles(
        grid, ints, reals, orders, (first_step, direct.reshape(whole), mirror.reshape(whole), field)
    )
    return (first_step, second_step)


def dispatch(wave_field, *rest):
    chans = lax.axis_size("chan")
    strips = lax.axis_size("strip")
    width = wave_field.shape[3] // chans
    grid = wave_field.shape[3]
    per_fits = wave_field.shape[1] == chans
    if strips == 2 * chans and width % 128 == 0 and grid % 256 == 0 and wave_field.shape[2] % 16 == 0 and per_fits:
        return local(wave_field, *rest)
    return general(wave_field, *rest)


def solution(mesh):
    placed = (P(None, "chan", "strip", None), P(), P(), P(), P(), P())
    return jax.shard_map(
        dispatch,
        mesh=mesh,
        in_specs=placed,
        out_specs=(P(None, None, "strip", "chan"), P(None, None, "strip", "chan")),
        check_vma=False,
    )
```

```python
import functools

import jax
import jax.numpy as jnp
from jax import lax
from jax.experimental import pallas as pl
from jax.experimental.pallas import tpu as pltpu
from jax.sharding import PartitionSpec as P


def potentials(row_pos, col_pos, count, orders):
    spacing = 8.0 / count
    first = row_pos.astype(jnp.float32) * spacing
    second = col_pos.astype(jnp.float32) * spacing
    lesser = jnp.minimum(first[:, None], second[None, :])
    greater = jnp.maximum(first[:, None], second[None, :])
    root = jnp.sqrt(greater * greater + 1.0)
    result = []
    for order in range(orders):
        result.append(lesser**order / root ** (order + 1))
    return result


def couple_terms(field, image_rows, mirrored, coupling, couple, partner, pots, live):
    total = image_rows + jnp.take(mirrored, partner, axis=1)
    real_part = total[0]
    imag_part = total[1]
    for order in range(len(pots)):
        source = jnp.take(field, couple[:, order], axis=1)
        c_real = coupling[0, :, order][:, None, None]
        c_imag = coupling[1, :, order][:, None, None]
        real_part = real_part + pots[order] * (c_real * source[0] - c_imag * source[1])
        imag_part = imag_part + pots[order] * (c_real * source[1] + c_imag * source[0])
    return jnp.where(live[None], jnp.stack([real_part, imag_part]), 0.0)


def radial_product(radial_op, block):
    return jnp.einsum("ak,pckb->pcab", radial_op, block, precision=lax.Precision.HIGHEST)


def spread_columns(field):
    strips = lax.axis_size("strip")
    local_chans = field.shape[1]
    local_rows = field.shape[2]
    grid = field.shape[3]
    piece = grid // (strips * strips)
    shaped = field.reshape(2, local_chans, local_rows, strips, strips, piece)
    return jnp.transpose(shaped, (0, 1, 2, 4, 3, 5)).reshape(2, local_chans, local_rows, grid)


def spread_tiles(image):
    chans = lax.axis_size("chan")
    strips = lax.axis_size("strip")
    local_chans = image.shape[1]
    grid = image.shape[2]
    width = image.shape[3]
    piece = grid // (strips * strips)
    ratio = strips // chans
    block = grid // chans
    direct_send = image.reshape(2, local_chans, strips, width, chans, ratio * piece)
    direct_send = jnp.transpose(direct_send, (0, 1, 4, 2, 3, 5)).reshape(
        2, local_chans, chans * strips, width, ratio * piece
    )
    mirror_send = image.reshape(2, local_chans, chans, block, strips, piece)
    mirror_send = jnp.transpose(mirror_send, (0, 1, 2, 4, 3, 5)).reshape(
        2, local_chans, chans * strips, block, piece
    )
    direct_got, mirror_got = (
        lax.all_to_all(direct_send, ("chan", "strip"), split_axis=2, concat_axis=2, tiled=True),
        lax.all_to_all(mirror_send, ("chan", "strip"), split_axis=2, concat_axis=2, tiled=True),
    )
    direct_got = direct_got.reshape(2, local_chans, chans, strips, width, ratio, piece)
    direct_tiles = jnp.transpose(direct_got, (0, 2, 1, 4, 5, 3, 6)).reshape(
        2, chans * local_chans, width, block
    )
    mirror_got = mirror_got.reshape(2, local_chans, chans, strips, block, piece)
    mirror_tiles = jnp.transpose(mirror_got, (0, 2, 1, 3, 5, 4)).reshape(
        2, chans * local_chans, width, block
    )
    return (direct_tiles, mirror_tiles)


def general(wave_field, radial_op, coupling, couple, partner, extent):
    chans = lax.axis_size("chan")
    grid = wave_field.shape[3]
    strip_rows = wave_field.shape[2]
    chan_cols = grid // chans
    row_pos = lax.axis_index("strip") * strip_rows + jnp.arange(strip_rows)
    col_pos = lax.axis_index("chan") * chan_cols + jnp.arange(chan_cols)
    pots = potentials(row_pos, col_pos, grid, coupling.shape[2])
    live = (row_pos[None, :, None] < extent[:, None, None]) & (
        col_pos[None, None, :] < extent[:, None, None]
    )

    def radial(block):
        return radial_product(radial_op, block)

    def product_columns(field_rows):
        return radial(lax.all_to_all(field_rows, "strip", split_axis=3, concat_axis=2, tiled=True))

    field_tiles = lax.all_to_all(wave_field, "chan", split_axis=3, concat_axis=1, tiled=True)
    rows_tiles, mirror_tiles = spread_tiles(product_columns(spread_columns(wave_field)))
    first_step = couple_terms(
        field_tiles, rows_tiles, mirror_tiles, coupling, couple, partner, pots, live
    )
    image = product_columns(
        spread_columns(lax.all_to_all(first_step, "chan", split_axis=1, concat_axis=3, tiled=True))
    )
    rows_tiles, mirror_tiles = spread_tiles(image)
    applied = couple_terms(
        first_step, rows_tiles, mirror_tiles, coupling, couple, partner, pots, live
    )
    second_step = 2.0 * applied - field_tiles
    return (first_step, second_step)


MESH = pl.DeviceIdType.MESH
ANY = pl.BlockSpec(memory_space=pl.ANY)


def rem(value, count):
    return lax.rem(value, count)


def greet(others):
    barrier = pltpu.get_barrier_semaphore()
    for other in others:
        pl.semaphore_signal(barrier, inc=1, device_id=other, device_id_type=MESH)
    pl.semaphore_wait(barrier, len(others))


def remote(source, target, send, recv, device):
    return pltpu.make_async_remote_copy(
        src_ref=source,
        dst_ref=target,
        send_sem=send,
        recv_sem=recv,
        device_id=device,
        device_id_type=MESH,
    )


def columns(block, width):
    return pl.ds(pl.multiple_of(block * width, 128), width)


def lines(block, height):
    return pl.ds(pl.multiple_of(block * height, 8), height)


def far_order(strips):
    half = strips // 2
    return sorted(range(1, strips), key=lambda d: (abs(d - half), d))


def chunks(per, body):
    def one(j, carry):
        body(j)
        return carry

    lax.fori_loop(0, per, one, 0)


def pick(j, values):
    chosen = jnp.int32(values[-1])
    for i, value in enumerate(values[:-1]):
        chosen = jnp.where(j == i, jnp.int32(value), chosen)
    return chosen


class Reach:
    def __init__(self, levels, rows, width):
        self.unit = width // 128
        self.width = width
        self.levels = levels
        self.lanes = [-(-level * rows // 128) for level in levels]
        self.parts = sorted({n % self.unit for n in self.lanes} - {0})

    def rows(self, j, strip):
        return strip < pick(j, self.levels)

    def blocks(self, j):
        return pick(j, [-(-n // self.unit) for n in self.lanes])

    def spans(self, j, block, alive, act):
        full = pick(j, [n // self.unit for n in self.lanes])
        rest = pick(j, [n % self.unit for n in self.lanes])

        @pl.when(jnp.logical_and(alive, block < full))
        def _():
            act(self.width)

        for part in self.parts:

            @pl.when(jnp.logical_and(alive, jnp.logical_and(block == full, rest == part)))
            def _():
                act(part * 128)

    def columns_alive(self, j, block):
        return pick(j, self.lanes) * 128 - block * self.width


def split(read, high, low, count, step):
    def one(n, carry):
        start = pl.multiple_of(n * step, step)
        at = pl.ds(start, step)
        value = read(start, at)
        top = value.astype(jnp.bfloat16)
        high[at, :] = top
        low[at, :] = (value - top.astype(jnp.float32)).astype(jnp.bfloat16)
        return carry

    lax.fori_loop(0, count // step, one, 0)


def load_operator(radial, turned, sems):
    per, width, grid = turned.shape
    return [
        pltpu.make_async_copy(radial.at[pl.ds(n * width, width), :], turned.at[n], sems.at[n])
        for n in range(grid // width)
    ]


def split_operator(loads, turned, rh, rl):
    width = turned.shape[1]
    for n, load in enumerate(loads):
        load.wait()
        at = pl.ds(n * width, width)
        split(lambda _, at, n=n: turned[n, at, :], rh.at[at, :], rl.at[at, :], width, 32)


def product(j, y, img, turned, rh, rl, yh, yl, depth, lanes, blocks):
    grid, width = y.shape[1:]
    step = 64
    steps = (depth + width - 1) // width

    def read(start, at):
        row = start + lax.broadcasted_iota(jnp.int32, (step, width), 0)
        col = lax.broadcasted_iota(jnp.int32, (step, width), 1)
        return jnp.where(jnp.logical_and(row < depth, col < lanes), y[j, at, :], 0.0)

    split(read, yh, yl, grid, step)

    def one(n, carry):
        at = pl.ds(pl.multiple_of(n * width, width), width)
        img[j, at, :] = jnp.zeros((width, width), jnp.float32)

        def inner(k, carry):
            mid = pl.ds(pl.multiple_of(k * width, width), width)
            top = rh[at, mid]
            total = jnp.dot(top, yh[mid, :], preferred_element_type=jnp.float32)
            total = total + jnp.dot(top, yl[mid, :], preferred_element_type=jnp.float32)
            total = total + jnp.dot(rl[at, mid], yh[mid, :], preferred_element_type=jnp.float32)
            img[j, at, :] += total
            return carry

        lax.fori_loop(0, steps, inner, 0)
        turned[j, :, at] = img[j, at, :].T
        return carry

    lax.fori_loop(0, blocks, one, 0)


def first_kernel(
    levels, chans, strips, x, radial, f, mt, dd, y, img, turned, w, rh, rl, yh, yl,
    gs, gr, gl, cs, cr, cl, rs, zs, zr, ms, mr, fs, fr, ls,
):
    c = lax.axis_index("chan")
    s = lax.axis_index("strip")
    per, grid, width = y.shape
    rows = x.shape[1]
    group = s // 2
    member = rem(s, 2)
    reach = Reach(levels, rows, width)
    ring = [(c, rem(s + d, strips)) for d in range(1, strips)]
    plane = [
        (rem(c + r, chans), group * 2 + rem(member + q, 2)) for r in range(chans) for q in range(2)
    ]
    greet(ring + plane[2:])

    def gather(j, d):
        t = ring[d - 1][1]
        return remote(
            x.at[rem(t, 2) * per + j, :, columns(t // 2, width)],
            y.at[j, lines(s, rows), :],
            gs.at[j, d],
            gr.at[j, d],
            ring[d - 1],
        )

    def keep(j):
        return pltpu.make_async_copy(
            x.at[member * per + j, :, columns(group, width)], y.at[j, lines(s, rows), :], gl.at[j]
        )

    def field(p, r):
        to = rem(c + r, chans)
        part = x.at[pl.ds(p * per, per), :, columns(to, width)]
        target = f.at[p * chans + c]
        if r == 0:
            return pltpu.make_async_copy(part, target, cl.at[p])
        return remote(part, target, cs.at[r * 2 + p], cr.at[r * 2 + p], (to, s))

    def hop(j, d, lanes):
        t = ring[d - 1][1]
        return remote(
            img.at[j, lines(t, rows), pl.ds(0, lanes)],
            w.at[j, s, :, pl.ds(0, lanes)],
            zs.at[j, d],
            zr.at[j, d],
            ring[d - 1],
        )

    def mirror(j, k):
        slot = member * chans + c
        to = plane[k][0]
        m = rem(member + k % 2, 2)
        part = turned.at[j, lines(m, rows), columns(to, width)]
        if k == 0:
            return pltpu.make_async_copy(part, mt.at[slot, j], ls.at[j, 2])
        return remote(part, mt.at[slot, j], ms.at[j, k], mr.at[j, k], plane[k])

    def forward(source, j, u):
        to = u // 2
        p = rem(u, 2)
        away = rem(to - c + chans, chans)

        def act(lanes):
            part = source.at[:, pl.ds(0, lanes)]
            target = dd.at[p * chans + c, j, :, pl.ds(0, lanes)]

            @pl.when(away == 0)
            def _():
                pltpu.make_async_copy(part, target, ls.at[j, p]).start()

            @pl.when(away != 0)
            def _():
                k = away * 2 + p
                remote(part, target, fs.at[j, k], fr.at[j, k], (to, s)).start()

        reach.spans(j, to, reach.rows(j, s), act)

    def begin(j):
        for d in far_order(strips):
            gather(j, d).start()
        keep(j).start()

    fields = [field(p, r) for r in range(chans) for p in range(2)]
    loads = load_operator(radial, turned, rs)
    chunks(per, begin)
    for load in loads:
        load.start()
    for copy in fields:
        copy.start()
    split_operator(loads, turned, rh, rl)

    def work(j):
        keep(j).wait()
        for d in range(1, strips):
            gather(j, d).wait_recv()
        product(j, y, img, turned, rh, rl, yh, yl, grid, width, chans)
        for d in far_order(strips):
            t = ring[d - 1][1]
            reach.spans(j, group, reach.rows(j, t), lambda lanes: hop(j, d, lanes).start())
        for k in reversed(range(2 * chans)):
            mirror(j, k).start()

    def relay(j):
        forward(img.at[j, lines(s, rows), :], j, s)
        for d in reversed(far_order(strips)):
            u = rem(s - d + strips, strips)
            reach.spans(j, u // 2, reach.rows(j, s), lambda lanes: hop(j, d, lanes).wait_recv())
            forward(w.at[j, u], j, u)

    def finish(j):
        for d in range(1, strips):
            t = ring[d - 1][1]
            gather(j, d).wait_send()
            reach.spans(j, group, reach.rows(j, t), lambda lanes: hop(j, d, lanes).wait_send())
        for k in range(2 * chans):
            mirror(j, k).wait()
        here = reach.rows(j, s)
        for p in range(2):

            def own(lanes):
                part = w.at[j, 0, :, pl.ds(0, lanes)]
                target = dd.at[p * chans + c, j, :, pl.ds(0, lanes)]
                pltpu.make_async_copy(part, target, ls.at[j, p]).wait()

            reach.spans(j, c, here, own)
            for r in range(1, chans):
                k = r * 2 + p

                def passed(lanes):
                    part = w.at[j, 0, :, pl.ds(0, lanes)]
                    target = dd.at[p * chans + c, j, :, pl.ds(0, lanes)]
                    return remote(part, target, fs.at[j, k], fr.at[j, k], (rem(c + r, chans), s))

                reach.spans(j, rem(c + r, chans), here, lambda lanes: passed(lanes).wait_send())
                reach.spans(j, c, here, lambda lanes: passed(lanes).wait_recv())

    chunks(per, work)
    chunks(per, relay)
    for copy in fields:
        copy.wait()
    chunks(per, finish)


def second_kernel(
    levels, chans, strips, v, radial, b, sd, y, img, turned, w, rh, rl, yh, yl, sib,
    bs, br, gs, gr, gl, rs, zs, zr, ms, mr, fs, fr, ls,
):
    c = lax.axis_index("chan")
    s = lax.axis_index("strip")
    per, grid, width = y.shape
    rows = v.shape[2]
    group = s // 2
    member = rem(s, 2)
    reach = Reach(levels, rows, width)
    ring = [(c, rem(s + d, strips)) for d in range(1, strips)]
    plane = [(rem(c + r, chans), s) for r in range(1, chans)]
    twin = (c, group * 2 + 1 - member)
    greet(ring + plane)

    def back(j, r, p, lanes):
        to = plane[r - 1][0]
        k = r * 2 + p
        return remote(
            v.at[p * chans + to, j, :, pl.ds(0, lanes)],
            b.at[p * chans + c, j, :, pl.ds(0, lanes)],
            bs.at[j, k],
            br.at[j, k],
            plane[r - 1],
        )

    def arrive(j, d, u, lanes):
        return remote(
            v.at[0, 0, :, pl.ds(0, lanes)],
            y.at[j, lines(u, rows), pl.ds(0, lanes)],
            gs.at[j, d],
            gr.at[j, d],
            ring[d - 1],
        )

    def forward(source, j, block, p):
        t = block * 2 + p
        away = rem(t - s + strips, strips)

        def act(lanes):
            part = source.at[:, pl.ds(0, lanes)]
            target = y.at[j, lines(s, rows), pl.ds(0, lanes)]

            @pl.when(away == 0)
            def _():
                pltpu.make_async_copy(part, target, gl.at[j]).start()

            @pl.when(away != 0)
            def _():
                remote(part, target, gs.at[j, away], gr.at[j, away], (c, t)).start()

        reach.spans(j, block, reach.rows(j, s), act)

    def begin(j):
        for r in reversed(range(1, chans)):
            for p in range(2):
                reach.spans(
                    j, c, reach.rows(j, s), lambda lanes: back(j, r, p, lanes).start()
                )

    def pass_on(j):
        for p in range(2):
            forward(v.at[p * chans + c, j], j, c, p)
        for r in reversed(range(1, chans)):
            sender = rem(c - r + chans, chans)
            for p in range(2):
                reach.spans(
                    j, sender, reach.rows(j, s), lambda lanes: back(j, r, p, lanes).wait_recv()
                )
                forward(b.at[p * chans + sender, j], j, sender, p)

    def hop(j, d, lanes):
        t = ring[d - 1][1]
        return remote(
            img.at[j, lines(t, rows), pl.ds(0, lanes)],
            w.at[j, s, :, pl.ds(0, lanes)],
            zs.at[j, d],
            zr.at[j, d],
            ring[d - 1],
        )

    def mirror(j):
        part = turned.at[j, lines(1 - member, rows), :]
        return remote(part, sib.at[j], ms.at[j], mr.at[j], twin)

    def pair(j):
        return j + 1 - 2 * rem(j, 2)

    def busy(j):
        return group < reach.blocks(j)

    def combine(source, j, u):
        block = u // 2
        other = pair(j)
        alive = jnp.logical_and(reach.rows(j, s), block < reach.blocks(j))
        mirrored = jnp.logical_and(alive, busy(other))
        own = rem(u, 2) == member
        at = columns(block, width)

        def add(read):
            def one(n, carry):
                line = pl.ds(pl.multiple_of(n * 32, 32), 32)
                w[j, u, line, :] = source[line, :] + read(n)
                return carry

            lax.fori_loop(0, rows // 32, one, 0)

        @pl.when(jnp.logical_and(mirrored, own))
        def _():
            add(
                lambda n: turned[
                    other, pl.ds(pl.multiple_of(member * rows + n * 32, 32), 32), at
                ]
            )

        @pl.when(jnp.logical_and(mirrored, jnp.logical_not(own)))
        def _():
            add(lambda n: sib[other, pl.ds(pl.multiple_of(n * 32, 32), 32), at])

    def send(j, u):
        to = u // 2
        p = rem(u, 2)
        away = rem(to - c + chans, chans)

        def act(lanes):
            part = w.at[j, u, :, pl.ds(0, lanes)]
            target = sd.at[p * chans + c, j, :, pl.ds(0, lanes)]

            @pl.when(away == 0)
            def _():
                pltpu.make_async_copy(part, target, ls.at[j, p]).start()

            @pl.when(away != 0)
            def _():
                k = away * 2 + p
                remote(part, target, fs.at[j, k], fr.at[j, k], (to, s)).start()

        reach.spans(j, to, reach.rows(j, s), act)

    loads = load_operator(radial, turned, rs)
    chunks(per, begin)
    for load in loads:
        load.start()
    chunks(per, pass_on)
    split_operator(loads, turned, rh, rl)

    def work(j):
        other = pair(j)
        depth = pick(j, levels) * rows

        def kept(lanes):
            target = y.at[j, lines(s, rows), pl.ds(0, lanes)]
            pltpu.make_async_copy(v.at[0, 0, :, pl.ds(0, lanes)], target, gl.at[j]).wait()

        reach.spans(j, group, reach.rows(j, s), kept)
        for d in range(1, strips):
            u = rem(s - d + strips, strips)
            reach.spans(
                j, group, reach.rows(j, u), lambda lanes: arrive(j, d, u, lanes).wait_recv()
            )

        @pl.when(busy(j))
        def _():
            blocks = jnp.maximum(reach.blocks(j), reach.blocks(other))
            lanes = reach.columns_alive(j, group)
            product(j, y, img, turned, rh, rl, yh, yl, depth, lanes, blocks)
            mirror(j).start()

        for d in far_order(strips):
            t = ring[d - 1][1]
            reach.spans(j, group, reach.rows(j, t), lambda lanes: hop(j, d, lanes).start())

    def hear(j):
        @pl.when(busy(j))
        def _():
            mirror(j).wait_recv()

    def relay(j):
        @pl.when(reach.rows(j, s))
        def _():
            @pl.when(busy(j))
            def _():
                own = img.at[j, lines(s, rows), :]

                @pl.when(busy(pair(j)))
                def _():
                    combine(own, j, s)

                @pl.when(jnp.logical_not(busy(pair(j))))
                def _():
                    def one(n, carry):
                        line = pl.ds(pl.multiple_of(n * 32, 32), 32)
                        w[j, s, line, :] = own[line, :]
                        return carry

                    lax.fori_loop(0, rows // 32, one, 0)

        send(j, s)
        for d in reversed(far_order(strips)):
            u = rem(s - d + strips, strips)
            reach.spans(j, u // 2, reach.rows(j, s), lambda lanes: hop(j, d, lanes).wait_recv())
            combine(w.at[j, u], j, u)
            send(j, u)

    def finish(j):
        here = reach.rows(j, s)
        for r in range(1, chans):
            for p in range(2):
                reach.spans(j, c, here, lambda lanes: back(j, r, p, lanes).wait_send())
        for d in range(1, strips):
            t = ring[d - 1][1]
            reach.spans(j, t // 2, here, lambda lanes: arrive(j, d, s, lanes).wait_send())
            reach.spans(j, group, reach.rows(j, t), lambda lanes: hop(j, d, lanes).wait_send())

        @pl.when(busy(j))
        def _():
            mirror(j).wait_send()

        for p in range(2):

            def own(lanes):
                part = w.at[j, 0, :, pl.ds(0, lanes)]
                target = sd.at[p * chans + c, j, :, pl.ds(0, lanes)]
                pltpu.make_async_copy(part, target, ls.at[j, p]).wait()

            reach.spans(j, c, here, own)
            for r in range(1, chans):
                k = r * 2 + p

                def passed(lanes):
                    part = w.at[j, 0, :, pl.ds(0, lanes)]
                    target = sd.at[p * chans + c, j, :, pl.ds(0, lanes)]
                    return remote(part, target, fs.at[j, k], fr.at[j, k], plane[r - 1])

                reach.spans(j, plane[r - 1][0], here, lambda lanes: passed(lanes).wait_send())
                reach.spans(j, c, here, lambda lanes: passed(lanes).wait_recv())

    chunks(per, work)
    chunks(per, hear)
    chunks(per, relay)
    chunks(per, finish)


def exchange(kernel, ident, outs, buffers, sems, *operands):
    chans = lax.axis_size("chan")
    strips = lax.axis_size("strip")
    return pl.pallas_call(
        functools.partial(kernel, chans, strips),
        out_shape=[jax.ShapeDtypeStruct(shape, jnp.float32) for shape in outs],
        in_specs=[ANY] * len(operands),
        out_specs=[ANY] * len(outs),
        scratch_shapes=[pltpu.VMEM(*buffer) for buffer in buffers]
        + [pltpu.SemaphoreType.DMA(n) for n in sems],
        compiler_params=pltpu.CompilerParams(
            collective_id=ident, has_side_effects=True, vmem_limit_bytes=62 * 2**20
        ),
    )(*operands)


def couple_kernel(count, last, ints, reals, *refs):
    if last:
        field, radial, base, out, pots = refs
    else:
        field, direct, mirror, out, dealt, pots = refs
    channels, height, width = field.shape[1:]
    orders = pots.shape[0]
    partners, extents, firsts, seconds, couples = [2 + n * channels for n in range(5)]
    spacing = 8.0 / count
    row = ints[0] + pl.program_id(0) * height
    row = row + lax.broadcasted_iota(jnp.int32, (height, width), 0)
    col = ints[1] + lax.broadcasted_iota(jnp.int32, (height, width), 1)
    first = row.astype(jnp.float32) * spacing
    second = col.astype(jnp.float32) * spacing
    greater = jnp.maximum(first, second)
    root = jnp.sqrt(greater * greater + 1.0)
    ratio = jnp.minimum(first, second) / root
    pot = 1.0 / root
    for order in range(orders):
        pots[order] = pot
        pot = pot * ratio
    reach = jnp.maximum(row, col)

    def channel(c, carry):
        mine = ints[firsts + c]
        dealt_at = ints[seconds + c]
        if last:
            real_part = radial[0, dealt_at]
            imag_part = radial[1, dealt_at]
        else:
            other = ints[firsts + ints[partners + c]]
            real_part = direct[0, mine] + mirror[0, other]
            imag_part = direct[1, mine] + mirror[1, other]
        for order in range(orders):
            k = ints[couples + c * orders + order]
            if not last:
                k = ints[firsts + k]
            c_real = reals[c * orders + order]
            c_imag = reals[channels * orders + c * orders + order]
            pot = pots[order]
            s_real = pot * field[0, k]
            s_imag = pot * field[1, k]
            real_part = real_part + (c_real * s_real - c_imag * s_imag)
            imag_part = imag_part + (c_real * s_imag + c_imag * s_real)
        live = reach < ints[extents + c]
        real_part = jnp.where(live, real_part, 0.0)
        imag_part = jnp.where(live, imag_part, 0.0)
        if last:
            real_part = 2.0 * real_part - base[0, mine]
            imag_part = 2.0 * imag_part - base[1, mine]
        else:
            dealt[0, dealt_at] = real_part
            dealt[1, dealt_at] = imag_part
        out[0, c] = real_part
        out[1, c] = imag_part
        return carry

    lax.fori_loop(0, channels, channel, 0)


def couple_tiles(count, ints, reals, orders, last, arrays):
    shape = arrays[0].shape
    height = 16
    block = pl.BlockSpec((2, shape[1], height, shape[3]), lambda n: (0, 0, n, 0))
    smem = pl.BlockSpec(memory_space=pltpu.SMEM)
    outs = 1 if last else 2
    return pl.pallas_call(
        functools.partial(couple_kernel, count, last),
        grid=(shape[2] // height,),
        out_shape=[jax.ShapeDtypeStruct(shape, jnp.float32)] * outs,
        in_specs=[smem, smem] + [block] * len(arrays),
        out_specs=[block] * outs,
        scratch_shapes=[pltpu.VMEM((orders, height, shape[3]), jnp.float32)],
    )(ints, reals, *arrays)


def deal(partner, extent, chans, per):
    channels = extent.shape[0]
    index = jnp.arange(channels)
    line = index // per
    ahead = (extent[None, :] > extent[:, None]) | (
        (extent[None, :] == extent[:, None]) & (index[None, :] < index[:, None])
    )
    place = jnp.sum(ahead & (line[None, :] == line[:, None]), axis=1)
    first = (line * per + place).astype(jnp.int32)
    others = extent[partner]
    lead = (extent > others) | ((extent == others) & (index < partner))
    most = jnp.maximum(extent, others)
    least = jnp.minimum(extent, others)
    head = jnp.where(lead, index, partner)
    key = most * 4096 + least
    before = lead[None, :] & (
        (key[None, :] > key[:, None])
        | ((key[None, :] == key[:, None]) & (head[None, :] < head[:, None]))
    )
    rank = jnp.sum(before, axis=1)
    spot = (rank // chans) * 2 + jnp.where(lead, 0, 1)
    second = (rank % chans) * per + spot
    slots = jnp.arange(per)
    far_first = jnp.max(jnp.where(place[None, :] == slots[:, None], extent[None, :], 0), axis=1)
    far_second = jnp.max(jnp.where(spot[None, :] == slots[:, None], extent[None, :], 0), axis=1)
    order = jnp.sum(jnp.where(first[None, :] == index[:, None], index[None, :] % per, 0), axis=1)
    return first, second.astype(jnp.int32), far_first, far_second, order


FIRST_LEVELS = ((8, 8, 6, 4), (8, 8, 6, 5), (8, 8, 7, 6), (8, 8, 8, 8))
SECOND_LEVELS = ((8, 8, 6, 4), (8, 6, 7, 6), (8, 8, 7, 5), (8, 8, 8, 8))


def choose(table, rows, far):
    limits = jnp.array(table, jnp.int32) * rows
    fits = jnp.all(limits >= far[None, :], axis=1)
    return jnp.argmax(fits).astype(jnp.int32)


def local(wave_field, radial_op, coupling, couple, partner, extent):
    chans = lax.axis_size("chan")
    strips = lax.axis_size("strip")
    per, rows, grid = wave_field.shape[1:]
    width = grid // chans
    orders = coupling.shape[2]
    tiles = (2 * chans, per, rows, width)
    whole = (2, chans * per, rows, width)
    starts = jnp.stack([lax.axis_index("strip") * rows, lax.axis_index("chan") * width])
    first, second, far_first, far_second, order = deal(partner, extent, chans, per)
    ints = jnp.concatenate(
        [starts.astype(jnp.int32), partner, extent, first, second, couple.reshape(-1)]
    )
    reals = coupling.reshape(-1)
    buffers = [
        ((per, grid, width), jnp.float32),
        ((per, grid, width), jnp.float32),
        ((per, width, grid), jnp.float32),
        ((per, strips, rows, width), jnp.float32),
        ((grid, grid), jnp.bfloat16),
        ((grid, grid), jnp.bfloat16),
        ((grid, width), jnp.bfloat16),
        ((grid, width), jnp.bfloat16),
    ]
    ring = (per, strips)
    plane = (per, 2 * chans)
    mine = lax.dynamic_slice(order, (lax.axis_index("chan") * per,), (per,))
    sorted_field = jnp.take(wave_field, mine, axis=1).reshape(2 * per, rows, grid)

    def first_call(n):
        def call(x):
            return exchange(
                functools.partial(first_kernel, FIRST_LEVELS[n]),
                n,
                [tiles, tiles, tiles],
                buffers,
                [ring, ring, (per,), (2 * chans,), (2 * chans,), (2,), (chans,)]
                + [ring, ring, plane, plane, plane, plane, (per, 3)],
                x,
                radial_op,
            )

        return call

    def second_call(n):
        def call(v):
            return exchange(
                functools.partial(second_kernel, SECOND_LEVELS[n]),
                len(FIRST_LEVELS) + n,
                [tiles, tiles],
                buffers + [((per, rows, grid), jnp.float32)],
                [plane, plane, ring, ring, (per,), (chans,)]
                + [ring, ring, (per,), (per,), plane, plane, (per, 2)],
                v,
                radial_op,
            )

        return call

    field, mirror, direct = lax.switch(
        choose(FIRST_LEVELS, rows, far_first),
        [first_call(n) for n in range(len(FIRST_LEVELS))],
        sorted_field,
    )
    field = field.reshape(whole)
    first_step, dealt = couple_tiles(
        grid, ints, reals, orders, False, (field, direct.reshape(whole), mirror.reshape(whole))
    )
    _, radial = lax.switch(
        choose(SECOND_LEVELS, rows, far_second),
        [second_call(n) for n in range(len(SECOND_LEVELS))],
        dealt.reshape(tiles),
    )
    second_step = couple_tiles(
        grid, ints, reals, orders, True, (first_step, radial.reshape(whole), field)
    )[0]
    return (first_step, second_step)


def dispatch(wave_field, *rest):
    chans = lax.axis_size("chan")
    strips = lax.axis_size("strip")
    per, rows, grid = wave_field.shape[1:]
    width = grid // chans
    aligned = width % 128 == 0 and rows % 64 == 0 and grid % 64 == 0
    if strips == 2 * chans and strips == 8 and per == 4 and aligned:
        return local(wave_field, *rest)
    return general(wave_field, *rest)


def solution(mesh):
    placed = (P(None, "chan", "strip", None), P(), P(), P(), P(), P())
    return jax.shard_map(
        dispatch,
        mesh=mesh,
        in_specs=placed,
        out_specs=(P(None, None, "strip", "chan"), P(None, None, "strip", "chan")),
        check_vma=False,
    )
```

```python
import functools

import jax
import jax.numpy as jnp
from jax import lax
from jax.experimental import pallas as pl
from jax.experimental.pallas import tpu as pltpu
from jax.sharding import PartitionSpec as P


def potentials(row_pos, col_pos, count, orders):
    spacing = 8.0 / count
    first = row_pos.astype(jnp.float32) * spacing
    second = col_pos.astype(jnp.float32) * spacing
    lesser = jnp.minimum(first[:, None], second[None, :])
    greater = jnp.maximum(first[:, None], second[None, :])
    root = jnp.sqrt(greater * greater + 1.0)
    result = []
    for order in range(orders):
        result.append(lesser**order / root ** (order + 1))
    return result


def couple_terms(field, image_rows, mirrored, coupling, couple, partner, pots, live):
    total = image_rows + jnp.take(mirrored, partner, axis=1)
    real_part = total[0]
    imag_part = total[1]
    for order in range(len(pots)):
        source = jnp.take(field, couple[:, order], axis=1)
        c_real = coupling[0, :, order][:, None, None]
        c_imag = coupling[1, :, order][:, None, None]
        real_part = real_part + pots[order] * (c_real * source[0] - c_imag * source[1])
        imag_part = imag_part + pots[order] * (c_real * source[1] + c_imag * source[0])
    return jnp.where(live[None], jnp.stack([real_part, imag_part]), 0.0)


def radial_product(radial_op, block):
    return jnp.einsum("ak,pckb->pcab", radial_op, block, precision=lax.Precision.HIGHEST)


def spread_columns(field):
    strips = lax.axis_size("strip")
    local_chans = field.shape[1]
    local_rows = field.shape[2]
    grid = field.shape[3]
    piece = grid // (strips * strips)
    shaped = field.reshape(2, local_chans, local_rows, strips, strips, piece)
    return jnp.transpose(shaped, (0, 1, 2, 4, 3, 5)).reshape(2, local_chans, local_rows, grid)


def spread_tiles(image):
    chans = lax.axis_size("chan")
    strips = lax.axis_size("strip")
    local_chans = image.shape[1]
    grid = image.shape[2]
    width = image.shape[3]
    piece = grid // (strips * strips)
    ratio = strips // chans
    block = grid // chans
    direct_send = image.reshape(2, local_chans, strips, width, chans, ratio * piece)
    direct_send = jnp.transpose(direct_send, (0, 1, 4, 2, 3, 5)).reshape(
        2, local_chans, chans * strips, width, ratio * piece
    )
    mirror_send = image.reshape(2, local_chans, chans, block, strips, piece)
    mirror_send = jnp.transpose(mirror_send, (0, 1, 2, 4, 3, 5)).reshape(
        2, local_chans, chans * strips, block, piece
    )
    direct_got, mirror_got = (
        lax.all_to_all(direct_send, ("chan", "strip"), split_axis=2, concat_axis=2, tiled=True),
        lax.all_to_all(mirror_send, ("chan", "strip"), split_axis=2, concat_axis=2, tiled=True),
    )
    direct_got = direct_got.reshape(2, local_chans, chans, strips, width, ratio, piece)
    direct_tiles = jnp.transpose(direct_got, (0, 2, 1, 4, 5, 3, 6)).reshape(
        2, chans * local_chans, width, block
    )
    mirror_got = mirror_got.reshape(2, local_chans, chans, strips, block, piece)
    mirror_tiles = jnp.transpose(mirror_got, (0, 2, 1, 3, 5, 4)).reshape(
        2, chans * local_chans, width, block
    )
    return (direct_tiles, mirror_tiles)


def general(wave_field, radial_op, coupling, couple, partner, extent):
    chans = lax.axis_size("chan")
    grid = wave_field.shape[3]
    strip_rows = wave_field.shape[2]
    chan_cols = grid // chans
    row_pos = lax.axis_index("strip") * strip_rows + jnp.arange(strip_rows)
    col_pos = lax.axis_index("chan") * chan_cols + jnp.arange(chan_cols)
    pots = potentials(row_pos, col_pos, grid, coupling.shape[2])
    live = (row_pos[None, :, None] < extent[:, None, None]) & (
        col_pos[None, None, :] < extent[:, None, None]
    )

    def radial(block):
        return radial_product(radial_op, block)

    def product_columns(field_rows):
        return radial(lax.all_to_all(field_rows, "strip", split_axis=3, concat_axis=2, tiled=True))

    field_tiles = lax.all_to_all(wave_field, "chan", split_axis=3, concat_axis=1, tiled=True)
    rows_tiles, mirror_tiles = spread_tiles(product_columns(spread_columns(wave_field)))
    first_step = couple_terms(
        field_tiles, rows_tiles, mirror_tiles, coupling, couple, partner, pots, live
    )
    image = product_columns(
        spread_columns(lax.all_to_all(first_step, "chan", split_axis=1, concat_axis=3, tiled=True))
    )
    rows_tiles, mirror_tiles = spread_tiles(image)
    applied = couple_terms(
        first_step, rows_tiles, mirror_tiles, coupling, couple, partner, pots, live
    )
    second_step = 2.0 * applied - field_tiles
    return (first_step, second_step)


MESH = pl.DeviceIdType.MESH
ANY = pl.BlockSpec(memory_space=pl.ANY)


def rem(value, count):
    return lax.rem(value, count)


def greet(others):
    barrier = pltpu.get_barrier_semaphore()
    for other in others:
        pl.semaphore_signal(barrier, inc=1, device_id=other, device_id_type=MESH)
    pl.semaphore_wait(barrier, len(others))


def remote(source, target, send, recv, device):
    return pltpu.make_async_remote_copy(
        src_ref=source,
        dst_ref=target,
        send_sem=send,
        recv_sem=recv,
        device_id=device,
        device_id_type=MESH,
    )


def columns(block, width):
    return pl.ds(pl.multiple_of(block * width, 128), width)


def lines(block, height):
    return pl.ds(pl.multiple_of(block * height, 8), height)


def each(count, body):
    def one(n, carry):
        body(n)
        return carry

    lax.fori_loop(0, count, one, 0)


def far_first(n, strips):
    return strips // 2 + ((n + 1) // 2) * (2 * rem(n + 1, 2) - 1)


def pick(j, values):
    chosen = jnp.int32(values[-1])
    for i, value in enumerate(values[:-1]):
        chosen = jnp.where(j == i, jnp.int32(value), chosen)
    return chosen


class Reach:
    def __init__(self, levels, rows, width):
        self.unit = width // 128
        self.width = width
        self.levels = levels
        self.lanes = [-(-level * rows // 128) for level in levels]
        self.parts = sorted({n % self.unit for n in self.lanes} - {0})

    def rows(self, j, strip):
        return strip < pick(j, self.levels)

    def blocks(self, j):
        return pick(j, [-(-n // self.unit) for n in self.lanes])

    def spans(self, j, block, alive, act):
        full = pick(j, [n // self.unit for n in self.lanes])
        rest = pick(j, [n % self.unit for n in self.lanes])

        @pl.when(jnp.logical_and(alive, block < full))
        def _():
            act(self.width)

        for part in self.parts:

            @pl.when(jnp.logical_and(alive, jnp.logical_and(block == full, rest == part)))
            def _():
                act(part * 128)

    def columns_alive(self, j, block):
        return pick(j, self.lanes) * 128 - block * self.width


def split(read, high, low, count, step):
    def one(n, carry):
        start = pl.multiple_of(n * step, step)
        at = pl.ds(start, step)
        value = read(start, at)
        top = value.astype(jnp.bfloat16)
        high[at, :] = top
        low[at, :] = (value - top.astype(jnp.float32)).astype(jnp.bfloat16)
        return carry

    lax.fori_loop(0, count // step, one, 0)


def load_operator(radial, turned, sems):
    per, width, grid = turned.shape
    return [
        pltpu.make_async_copy(radial.at[pl.ds(n * width, width), :], turned.at[n], sems.at[n])
        for n in range(grid // width)
    ]


def split_operator(loads, turned, rh, rl):
    width = turned.shape[1]
    for n, load in enumerate(loads):
        load.wait()
        at = pl.ds(n * width, width)
        split(lambda _, at, n=n: turned[n, at, :], rh.at[at, :], rl.at[at, :], width, 32)


def product(j, y, img, turned, rh, rl, yh, yl, depth, lanes, blocks):
    grid, width = y.shape[1:]
    step = 64

    def read(start, at):
        row = start + lax.broadcasted_iota(jnp.int32, (step, width), 0)
        col = lax.broadcasted_iota(jnp.int32, (step, width), 1)
        return jnp.where(jnp.logical_and(row < depth, col < lanes), y[j, at, :], 0.0)

    split(read, yh, yl, grid, step)

    def one(n):
        at = pl.ds(pl.multiple_of(n * 128, 128), 128)
        top = rh[at, :]
        total = jnp.dot(top, yh[...], preferred_element_type=jnp.float32)
        total = total + jnp.dot(top, yl[...], preferred_element_type=jnp.float32)
        total = total + jnp.dot(rl[at, :], yh[...], preferred_element_type=jnp.float32)
        img[j, at, :] = total
        turned[j, :, at] = total.T

    each(blocks * (width // 128), one)


ORDER = (0, 2, 3, 1)


def first_kernel(
    levels, chans, strips, x, radial, f, mt, dd, y, img, turned, w, rh, rl, yh, yl,
    gs, gr, gl, cs, cr, cl, rs, ks, zs, zr, ms, mr, ml, fs, fr, ls,
):
    c = lax.axis_index("chan")
    s = lax.axis_index("strip")
    per, grid, width = y.shape
    rows = x.shape[1]
    group = s // 2
    member = rem(s, 2)
    reach = Reach(levels, rows, width)
    ring = [(c, rem(s + d, strips)) for d in range(1, strips)]
    plane = [(rem(c + r, chans), group * 2 + m) for r in range(1, chans) for m in range(2)]
    greet(ring + plane)

    def gather(j, d):
        t = rem(s + d, strips)
        return remote(
            x.at[rem(t, 2) * per + j, :, columns(t // 2, width)],
            y.at[j, lines(s, rows), :],
            gs.at[j, d],
            gr.at[j, d],
            (c, t),
        )

    def keep(j):
        return pltpu.make_async_copy(
            x.at[member * per + j, :, columns(group, width)], y.at[j, lines(s, rows), :], gl.at[j]
        )

    def field(p, r):
        to = rem(c + r, chans)
        part = x.at[pl.ds(p * per, per), :, columns(to, width)]
        target = f.at[p * chans + c]
        return remote(part, target, cs.at[r * 2 + p], cr.at[r * 2 + p], (to, s))

    def own_field(p):
        part = x.at[pl.ds(p * per, per), :, columns(c, width)]
        return pltpu.make_async_copy(part, f.at[p * chans + c], cl.at[p])

    def hop(j, d, lanes):
        t = rem(s + d, strips)
        return remote(
            img.at[j, lines(t, rows), pl.ds(0, lanes)],
            w.at[j, s, :, pl.ds(0, lanes)],
            zs.at[j, d],
            zr.at[j, d],
            (c, t),
        )

    def own_hop(j):
        return pltpu.make_async_copy(img.at[j, lines(s, rows), :], w.at[j, s], ks.at[j])

    def mirror(j, k):
        to = rem(c + k // 2, chans)
        m = rem(member + rem(k, 2), 2)
        part = turned.at[j, lines(m, rows), columns(to, width)]
        target = mt.at[member * chans + c, j]
        return remote(part, target, ms.at[j, k], mr.at[j, k], (to, group * 2 + m))

    def own_mirror(j):
        part = turned.at[j, lines(member, rows), columns(c, width)]
        return pltpu.make_async_copy(part, mt.at[member * chans + c, j], ml.at[j])

    def forward(j, u):
        to = u // 2
        p = rem(u, 2)
        away = rem(to - c + chans, chans)

        def act(lanes):
            part = w.at[j, u, :, pl.ds(0, lanes)]
            target = dd.at[p * chans + c, j, :, pl.ds(0, lanes)]

            @pl.when(away == 0)
            def _():
                pltpu.make_async_copy(part, target, ls.at[j, p]).start()

            @pl.when(away != 0)
            def _():
                k = away * 2 + p
                remote(part, target, fs.at[j, k], fr.at[j, k], (to, s)).start()

        reach.spans(j, to, reach.rows(j, s), act)

    def begin(j):
        each(strips - 1, lambda n: gather(j, far_first(n, strips)).start())
        keep(j).start()

    loads = load_operator(radial, turned, rs)
    each(per, begin)
    for load in loads:
        load.start()
    each(2 * chans - 2, lambda n: field(rem(n, 2), 1 + n // 2).start())
    each(2, lambda p: own_field(p).start())
    split_operator(loads, turned, rh, rl)

    def launch(j):
        def one(n):
            d = far_first(n, strips)
            alive = reach.rows(j, rem(s + d, strips))
            reach.spans(j, group, alive, lambda lanes: hop(j, d, lanes).start())

        each(strips - 1, one)
        own_hop(j).start()

    def work(j):
        keep(j).wait()
        each(strips - 1, lambda n: gather(j, n + 1).wait_recv())
        product(j, y, img, turned, rh, rl, yh, yl, grid, width, chans)
        each(2 * chans - 1, lambda n: mirror(j, n + 1).start())
        own_mirror(j).start()

        @pl.when(j != ORDER[-1])
        def _():
            launch(j)

    def relay(i):
        j = pick(i, ORDER)
        own_hop(j).wait()

        def one(n):
            u = rem(c + n // 2, chans) * 2 + rem(n, 2)
            d = rem(s - u + strips, strips)
            alive = jnp.logical_and(reach.rows(j, s), u != s)
            reach.spans(j, u // 2, alive, lambda lanes: hop(j, d, lanes).wait_recv())
            forward(j, u)

        each(strips, one)

    def finish(j):
        def sent(n):
            d = n + 1
            gather(j, d).wait_send()
            alive = reach.rows(j, rem(s + d, strips))
            reach.spans(j, group, alive, lambda lanes: hop(j, d, lanes).wait_send())
            mirror(j, d).wait()

        each(strips - 1, sent)
        own_mirror(j).wait()
        here = reach.rows(j, s)

        def passed(k, lanes):
            part = w.at[j, 0, :, pl.ds(0, lanes)]
            target = dd.at[rem(k, 2) * chans + c, j, :, pl.ds(0, lanes)]
            return remote(part, target, fs.at[j, k], fr.at[j, k], (rem(c + k // 2, chans), s))

        def one(n):
            k = n + 2
            to = rem(c + k // 2, chans)
            reach.spans(j, to, here, lambda lanes: passed(k, lanes).wait_send())
            reach.spans(j, c, here, lambda lanes: passed(k, lanes).wait_recv())

        def own(p):
            def act(lanes):
                part = w.at[j, 0, :, pl.ds(0, lanes)]
                target = dd.at[p * chans + c, j, :, pl.ds(0, lanes)]
                pltpu.make_async_copy(part, target, ls.at[j, p]).wait()

            reach.spans(j, c, here, act)

        each(2, own)
        each(2 * chans - 2, one)

    each(per, work)
    launch(ORDER[-1])
    each(per, relay)
    each(2 * chans - 2, lambda n: field(rem(n, 2), 1 + n // 2).wait())
    each(2, lambda p: own_field(p).wait())
    each(per, finish)


def second_kernel(
    levels, chans, strips, v, radial, b, sd, y, img, turned, w, rh, rl, yh, yl, sib,
    bs, br, gs, gr, gl, rs, ks, zs, zr, ms, mr, fs, fr, ls,
):
    c = lax.axis_index("chan")
    s = lax.axis_index("strip")
    per, grid, width = y.shape
    rows = v.shape[2]
    group = s // 2
    member = rem(s, 2)
    reach = Reach(levels, rows, width)
    ring = [(c, rem(s + d, strips)) for d in range(1, strips)]
    plane = [(rem(c + r, chans), s) for r in range(1, chans)]
    twin = (c, group * 2 + 1 - member)
    greet(ring + plane)

    def back(j, k, lanes):
        to = rem(c + k // 2, chans)
        p = rem(k, 2)
        return remote(
            v.at[p * chans + to, j, :, pl.ds(0, lanes)],
            b.at[p * chans + c, j, :, pl.ds(0, lanes)],
            bs.at[j, k],
            br.at[j, k],
            (to, s),
        )

    def arrive(j, d, u, lanes):
        return remote(
            v.at[0, 0, :, pl.ds(0, lanes)],
            y.at[j, lines(u, rows), pl.ds(0, lanes)],
            gs.at[j, d],
            gr.at[j, d],
            (c, rem(s + d, strips)),
        )

    def forward(source, j, block, p):
        t = block * 2 + p
        away = rem(t - s + strips, strips)

        def act(lanes):
            part = source.at[:, pl.ds(0, lanes)]
            target = y.at[j, lines(s, rows), pl.ds(0, lanes)]

            @pl.when(away == 0)
            def _():
                pltpu.make_async_copy(part, target, gl.at[j]).start()

            @pl.when(away != 0)
            def _():
                remote(part, target, gs.at[j, away], gr.at[j, away], (c, t)).start()

        reach.spans(j, block, reach.rows(j, s), act)

    def begin(j):
        def one(n):
            k = 2 * chans - 1 - n
            reach.spans(j, c, reach.rows(j, s), lambda lanes: back(j, k, lanes).start())

        each(2 * chans - 2, one)

    def pass_on(j):
        each(2, lambda p: forward(v.at[p * chans + c, j], j, c, p))

        def one(n):
            k = 2 * chans - 1 - n
            p = rem(k, 2)
            sender = rem(c - k // 2 + chans, chans)
            here = reach.rows(j, s)
            reach.spans(j, sender, here, lambda lanes: back(j, k, lanes).wait_recv())
            forward(b.at[p * chans + sender, j], j, sender, p)

        each(2 * chans - 2, one)

    def hop(j, d, lanes):
        t = rem(s + d, strips)
        return remote(
            img.at[j, lines(t, rows), pl.ds(0, lanes)],
            w.at[j, s, :, pl.ds(0, lanes)],
            zs.at[j, d],
            zr.at[j, d],
            (c, t),
        )

    def own_hop(j):
        return pltpu.make_async_copy(img.at[j, lines(s, rows), :], w.at[j, s], ks.at[j])

    def mirror(j):
        part = turned.at[j, lines(1 - member, rows), :]
        return remote(part, sib.at[j], ms.at[j], mr.at[j], twin)

    def pair(j):
        return j + 1 - 2 * rem(j, 2)

    def busy(j):
        return group < reach.blocks(j)

    def combine(j, u):
        block = u // 2
        other = pair(j)
        alive = jnp.logical_and(reach.rows(j, s), block < reach.blocks(j))
        mirrored = jnp.logical_and(alive, busy(other))
        own = rem(u, 2) == member
        at = columns(block, width)

        def add(read):
            def one(n):
                line = pl.ds(pl.multiple_of(n * 32, 32), 32)
                w[j, u, line, :] = w[j, u, line, :] + read(n)

            each(rows // 32, one)

        @pl.when(jnp.logical_and(mirrored, own))
        def _():
            add(
                lambda n: turned[
                    other, pl.ds(pl.multiple_of(member * rows + n * 32, 32), 32), at
                ]
            )

        @pl.when(jnp.logical_and(mirrored, jnp.logical_not(own)))
        def _():
            add(lambda n: sib[other, pl.ds(pl.multiple_of(n * 32, 32), 32), at])

    def send(j, u):
        to = u // 2
        p = rem(u, 2)
        away = rem(to - c + chans, chans)

        def act(lanes):
            part = w.at[j, u, :, pl.ds(0, lanes)]
            target = sd.at[p * chans + c, j, :, pl.ds(0, lanes)]

            @pl.when(away == 0)
            def _():
                pltpu.make_async_copy(part, target, ls.at[j, p]).start()

            @pl.when(away != 0)
            def _():
                k = away * 2 + p
                remote(part, target, fs.at[j, k], fr.at[j, k], (to, s)).start()

        reach.spans(j, to, reach.rows(j, s), act)

    loads = load_operator(radial, turned, rs)
    each(per, begin)
    for load in loads:
        load.start()
    each(per, pass_on)
    split_operator(loads, turned, rh, rl)

    def launch(j):
        def one(n):
            d = far_first(n, strips)
            alive = reach.rows(j, rem(s + d, strips))
            reach.spans(j, group, alive, lambda lanes: hop(j, d, lanes).start())

        each(strips - 1, one)

        @pl.when(busy(j))
        def _():
            own_hop(j).start()

    def work(j):
        other = pair(j)
        depth = pick(j, levels) * rows

        def kept(lanes):
            target = y.at[j, lines(s, rows), pl.ds(0, lanes)]
            pltpu.make_async_copy(v.at[0, 0, :, pl.ds(0, lanes)], target, gl.at[j]).wait()

        reach.spans(j, group, reach.rows(j, s), kept)

        def arrived(n):
            d = n + 1
            u = rem(s - d + strips, strips)
            alive = reach.rows(j, u)
            reach.spans(j, group, alive, lambda lanes: arrive(j, d, u, lanes).wait_recv())

        each(strips - 1, arrived)

        @pl.when(busy(j))
        def _():
            blocks = jnp.maximum(reach.blocks(j), reach.blocks(other))
            lanes = reach.columns_alive(j, group)
            product(j, y, img, turned, rh, rl, yh, yl, depth, lanes, blocks)
            mirror(j).start()

        @pl.when(j != ORDER[-1])
        def _():
            launch(j)

    def hear(j):
        @pl.when(busy(j))
        def _():
            mirror(j).wait_recv()
            own_hop(j).wait()

    def relay(i):
        j = pick(i, ORDER)

        def one(n):
            u = rem(c + n // 2, chans) * 2 + rem(n, 2)
            d = rem(s - u + strips, strips)
            alive = jnp.logical_and(reach.rows(j, s), u != s)
            reach.spans(j, u // 2, alive, lambda lanes: hop(j, d, lanes).wait_recv())
            combine(j, u)
            send(j, u)

        each(strips, one)

    def finish(j):
        here = reach.rows(j, s)

        def sent(n):
            d = n + 1
            t = rem(s + d, strips)
            reach.spans(j, t // 2, here, lambda lanes: arrive(j, d, s, lanes).wait_send())
            alive = reach.rows(j, t)
            reach.spans(j, group, alive, lambda lanes: hop(j, d, lanes).wait_send())

        each(strips - 1, sent)

        @pl.when(busy(j))
        def _():
            mirror(j).wait_send()

        def passed(k, lanes):
            part = w.at[j, 0, :, pl.ds(0, lanes)]
            target = sd.at[rem(k, 2) * chans + c, j, :, pl.ds(0, lanes)]
            return remote(part, target, fs.at[j, k], fr.at[j, k], (rem(c + k // 2, chans), s))

        def one(n):
            k = n + 2
            to = rem(c + k // 2, chans)
            reach.spans(j, c, here, lambda lanes: back(j, k, lanes).wait_send())
            reach.spans(j, to, here, lambda lanes: passed(k, lanes).wait_send())
            reach.spans(j, c, here, lambda lanes: passed(k, lanes).wait_recv())

        def own(p):
            def act(lanes):
                part = w.at[j, 0, :, pl.ds(0, lanes)]
                target = sd.at[p * chans + c, j, :, pl.ds(0, lanes)]
                pltpu.make_async_copy(part, target, ls.at[j, p]).wait()

            reach.spans(j, c, here, act)

        each(2, own)
        each(2 * chans - 2, one)

    each(per, work)
    launch(ORDER[-1])
    each(per, hear)
    each(per, relay)
    each(per, finish)


def exchange(kernel, ident, outs, buffers, sems, *operands):
    chans = lax.axis_size("chan")
    strips = lax.axis_size("strip")
    return pl.pallas_call(
        functools.partial(kernel, chans, strips),
        out_shape=[jax.ShapeDtypeStruct(shape, jnp.float32) for shape in outs],
        in_specs=[ANY] * len(operands),
        out_specs=[ANY] * len(outs),
        scratch_shapes=[pltpu.VMEM(*buffer) for buffer in buffers]
        + [pltpu.SemaphoreType.DMA(n) for n in sems],
        compiler_params=pltpu.CompilerParams(
            collective_id=ident, has_side_effects=True, vmem_limit_bytes=62 * 2**20
        ),
    )(*operands)


def couple_kernel(count, last, ints, links, reals, *refs):
    if last:
        field, radial, base, out, pots = refs
    else:
        field, direct, mirror, out, dealt, pots = refs
    channels, height, width = field.shape[1:]
    orders = pots.shape[0]
    partners, extents, firsts, seconds = [2 + n * channels for n in range(4)]
    spacing = 8.0 / count
    row = ints[0] + pl.program_id(0) * height
    row = row + lax.broadcasted_iota(jnp.int32, (height, width), 0)
    col = ints[1] + lax.broadcasted_iota(jnp.int32, (height, width), 1)
    first = row.astype(jnp.float32) * spacing
    second = col.astype(jnp.float32) * spacing
    greater = jnp.maximum(first, second)
    root = jnp.sqrt(greater * greater + 1.0)
    ratio = jnp.minimum(first, second) / root
    pot = 1.0 / root
    for order in range(orders):
        pots[order] = pot
        pot = pot * ratio
    reach = jnp.maximum(row, col)

    def channel(c, carry):
        mine = ints[firsts + c]
        dealt_at = ints[seconds + c]
        if last:
            real_part = radial[0, dealt_at]
            imag_part = radial[1, dealt_at]
        else:
            other = ints[firsts + ints[partners + c]]
            real_part = direct[0, mine] + mirror[0, other]
            imag_part = direct[1, mine] + mirror[1, other]
        for order in range(orders):
            k = links[order * channels + c]
            if not last:
                k = ints[firsts + k]
            c_real = reals[order * channels + c]
            c_imag = reals[(orders + order) * channels + c]
            pot = pots[order]
            s_real = pot * field[0, k]
            s_imag = pot * field[1, k]
            real_part = real_part + (c_real * s_real - c_imag * s_imag)
            imag_part = imag_part + (c_real * s_imag + c_imag * s_real)
        live = reach < ints[extents + c]
        real_part = jnp.where(live, real_part, 0.0)
        imag_part = jnp.where(live, imag_part, 0.0)
        if last:
            real_part = 2.0 * real_part - base[0, mine]
            imag_part = 2.0 * imag_part - base[1, mine]
        else:
            dealt[0, dealt_at] = real_part
            dealt[1, dealt_at] = imag_part
        out[0, c] = real_part
        out[1, c] = imag_part
        return carry

    lax.fori_loop(0, channels, channel, 0)


def couple_tiles(count, scalars, orders, last, arrays):
    shape = arrays[0].shape
    height = 16
    block = pl.BlockSpec((2, shape[1], height, shape[3]), lambda n: (0, 0, n, 0))
    smem = pl.BlockSpec(memory_space=pltpu.SMEM)
    outs = 1 if last else 2
    return pl.pallas_call(
        functools.partial(couple_kernel, count, last),
        grid=(shape[2] // height,),
        out_shape=[jax.ShapeDtypeStruct(shape, jnp.float32)] * outs,
        in_specs=[smem] * len(scalars) + [block] * len(arrays),
        out_specs=[block] * outs,
        scratch_shapes=[pltpu.VMEM((orders, height, shape[3]), jnp.float32)],
    )(*scalars, *arrays)


FIRST_LEVELS = ((8, 6, 5, 4), (8, 7, 5, 4), (8, 8, 6, 4), (8, 8, 7, 4), (8, 8, 6, 5), (8, 8, 8, 4), (8, 8, 7, 6), (8, 8, 8, 8))
SECOND_LEVELS = ((8, 6, 6, 4), (8, 8, 6, 4), (8, 7, 6, 5), (8, 7, 7, 4), (8, 6, 7, 6), (8, 8, 7, 5), (8, 8, 8, 6), (8, 8, 8, 8))


def deal_kernel(per, rows, width, partner, extent, ints, order, choice, far, keys):
    channels = extent.shape[0]
    chans = channels // per
    c = lax.axis_index("chan")
    ints[0] = lax.axis_index("strip") * rows
    ints[1] = c * width
    for n in range(2 * per):
        far[n] = 0

    def told(i):
        mine = extent[i]
        other = extent[partner[i]]
        lead = jnp.logical_or(mine > other, jnp.logical_and(mine == other, i < partner[i]))
        return mine, lead, jnp.maximum(mine, other) * 4096 + jnp.minimum(mine, other)

    def key(i):
        _, lead, value = told(i)
        keys[i] = jnp.where(lead, value, -1)

    def one(i):
        mine, lead, value = told(i)
        head = jnp.where(lead, i, partner[i])
        line = i // per
        place = jnp.int32(0)
        rank = jnp.int32(0)
        for n in range(per):
            k = line * per + n
            tie = jnp.logical_and(extent[k] == mine, k < i)
            place = place + jnp.where(jnp.logical_or(extent[k] > mine, tie), 1, 0)
        for k in range(channels):
            tie = jnp.logical_and(keys[k] == value, k < head)
            rank = rank + jnp.where(jnp.logical_or(keys[k] > value, tie), 1, 0)
        spot = (rank // chans) * 2 + jnp.where(lead, 0, 1)
        ints[2 + i] = partner[i]
        ints[2 + channels + i] = mine
        ints[2 + 2 * channels + i] = line * per + place
        ints[2 + 3 * channels + i] = rem(rank, chans) * per + spot
        far[place] = jnp.maximum(far[place], mine)
        far[per + spot] = jnp.maximum(far[per + spot], mine)

        @pl.when(line == c)
        def _():
            order[place] = i - line * per

    each(channels, key)
    each(channels, one)
    for n, table in enumerate((FIRST_LEVELS, SECOND_LEVELS)):
        best = jnp.int32(len(table) - 1)
        for v in reversed(range(len(table) - 1)):
            fits = far[n * per] <= table[v][0] * rows
            for j in range(1, per):
                fits = jnp.logical_and(fits, far[n * per + j] <= table[v][j] * rows)
            best = jnp.where(fits, jnp.int32(v), best)
        choice[n] = best


def deal(partner, extent, per, rows, width):
    channels = extent.shape[0]
    smem = pl.BlockSpec(memory_space=pltpu.SMEM)
    return pl.pallas_call(
        functools.partial(deal_kernel, per, rows, width),
        out_shape=[
            jax.ShapeDtypeStruct((size,), jnp.int32) for size in (2 + 4 * channels, per, 2)
        ],
        in_specs=[smem, smem],
        out_specs=[smem] * 3,
        scratch_shapes=[pltpu.SMEM((2 * per,), jnp.int32), pltpu.SMEM((channels,), jnp.int32)],
    )(partner, extent)


def sort_kernel(order, x, out):
    out[...] = x[...]


def sort_field(order, x):
    parts, per, rows, grid = x.shape
    block = (1, 1, rows, grid)
    return pl.pallas_call(
        sort_kernel,
        grid_spec=pltpu.PrefetchScalarGridSpec(
            num_scalar_prefetch=1,
            grid=(parts, per),
            in_specs=[pl.BlockSpec(block, lambda p, j, order: (p, order[j], 0, 0))],
            out_specs=pl.BlockSpec(block, lambda p, j, order: (p, j, 0, 0)),
        ),
        out_shape=jax.ShapeDtypeStruct(x.shape, x.dtype),
    )(order, x)


def local(wave_field, radial_op, coupling, couple, partner, extent):
    chans = lax.axis_size("chan")
    strips = lax.axis_size("strip")
    per, rows, grid = wave_field.shape[1:]
    width = grid // chans
    orders = coupling.shape[2]
    tiles = (2 * chans, per, rows, width)
    whole = (2, chans * per, rows, width)
    ints, order, choice = deal(partner, extent, per, rows, width)
    scalars = (ints, couple.T.reshape(-1), coupling.transpose(0, 2, 1).reshape(-1))
    buffers = [
        ((per, grid, width), jnp.float32),
        ((per, grid, width), jnp.float32),
        ((per, width, grid), jnp.float32),
        ((per, strips, rows, width), jnp.float32),
        ((grid, grid), jnp.bfloat16),
        ((grid, grid), jnp.bfloat16),
        ((grid, width), jnp.bfloat16),
        ((grid, width), jnp.bfloat16),
    ]
    one = (per,)
    ring = (per, strips)
    plane = (per, 2 * chans)
    sorted_field = sort_field(order, wave_field).reshape(2 * per, rows, grid)

    def first_call(n):
        def call(x):
            return exchange(
                functools.partial(first_kernel, FIRST_LEVELS[n]),
                n,
                [tiles, tiles, tiles],
                buffers,
                [ring, ring, one, (2 * chans,), (2 * chans,), (2,), (chans,)]
                + [one, ring, ring, plane, plane, one, plane, plane, (per, 2)],
                x,
                radial_op,
            )

        return call

    def second_call(n):
        def call(v):
            return exchange(
                functools.partial(second_kernel, SECOND_LEVELS[n]),
                len(FIRST_LEVELS) + n,
                [tiles, tiles],
                buffers + [((per, rows, grid), jnp.float32)],
                [plane, plane, ring, ring, one, (chans,)]
                + [one, ring, ring, one, one, plane, plane, (per, 2)],
                v,
                radial_op,
            )

        return call

    field, mirror, direct = lax.switch(
        choice[0], [first_call(n) for n in range(len(FIRST_LEVELS))], sorted_field
    )
    field = field.reshape(whole)
    first_step, dealt = couple_tiles(
        grid, scalars, orders, False, (field, direct.reshape(whole), mirror.reshape(whole))
    )
    _, radial = lax.switch(
        choice[1], [second_call(n) for n in range(len(SECOND_LEVELS))], dealt.reshape(tiles)
    )
    second_step = couple_tiles(
        grid, scalars, orders, True, (first_step, radial.reshape(whole), field)
    )[0]
    return (first_step, second_step)


def dispatch(wave_field, *rest):
    chans = lax.axis_size("chan")
    strips = lax.axis_size("strip")
    per, rows, grid = wave_field.shape[1:]
    width = grid // chans
    aligned = width % 128 == 0 and rows % 64 == 0 and grid % 64 == 0
    if chans == 4 and strips == 8 and per == 4 and aligned:
        return local(wave_field, *rest)
    return general(wave_field, *rest)


def solution(mesh):
    placed = (P(None, "chan", "strip", None), P(), P(), P(), P(), P())
    return jax.shard_map(
        dispatch,
        mesh=mesh,
        in_specs=placed,
        out_specs=(P(None, None, "strip", "chan"), P(None, None, "strip", "chan")),
        check_vma=False,
    )
```

```python
import functools

import jax
import jax.numpy as jnp
from jax import lax
from jax.experimental import pallas as pl
from jax.experimental.pallas import tpu as pltpu
from jax.sharding import PartitionSpec as P


def potentials(row_pos, col_pos, count, orders):
    spacing = 8.0 / count
    first = row_pos.astype(jnp.float32) * spacing
    second = col_pos.astype(jnp.float32) * spacing
    lesser = jnp.minimum(first[:, None], second[None, :])
    greater = jnp.maximum(first[:, None], second[None, :])
    root = jnp.sqrt(greater * greater + 1.0)
    result = []
    for order in range(orders):
        result.append(lesser**order / root ** (order + 1))
    return result


def couple_terms(field, image_rows, mirrored, coupling, couple, partner, pots, live):
    total = image_rows + jnp.take(mirrored, partner, axis=1)
    real_part = total[0]
    imag_part = total[1]
    for order in range(len(pots)):
        source = jnp.take(field, couple[:, order], axis=1)
        c_real = coupling[0, :, order][:, None, None]
        c_imag = coupling[1, :, order][:, None, None]
        real_part = real_part + pots[order] * (c_real * source[0] - c_imag * source[1])
        imag_part = imag_part + pots[order] * (c_real * source[1] + c_imag * source[0])
    return jnp.where(live[None], jnp.stack([real_part, imag_part]), 0.0)


def radial_product(radial_op, block):
    return jnp.einsum("ak,pckb->pcab", radial_op, block, precision=lax.Precision.HIGHEST)


def spread_columns(field):
    strips = lax.axis_size("strip")
    local_chans = field.shape[1]
    local_rows = field.shape[2]
    grid = field.shape[3]
    piece = grid // (strips * strips)
    shaped = field.reshape(2, local_chans, local_rows, strips, strips, piece)
    return jnp.transpose(shaped, (0, 1, 2, 4, 3, 5)).reshape(2, local_chans, local_rows, grid)


def spread_tiles(image):
    chans = lax.axis_size("chan")
    strips = lax.axis_size("strip")
    local_chans = image.shape[1]
    grid = image.shape[2]
    width = image.shape[3]
    piece = grid // (strips * strips)
    ratio = strips // chans
    block = grid // chans
    direct_send = image.reshape(2, local_chans, strips, width, chans, ratio * piece)
    direct_send = jnp.transpose(direct_send, (0, 1, 4, 2, 3, 5)).reshape(
        2, local_chans, chans * strips, width, ratio * piece
    )
    mirror_send = image.reshape(2, local_chans, chans, block, strips, piece)
    mirror_send = jnp.transpose(mirror_send, (0, 1, 2, 4, 3, 5)).reshape(
        2, local_chans, chans * strips, block, piece
    )
    direct_got, mirror_got = (
        lax.all_to_all(direct_send, ("chan", "strip"), split_axis=2, concat_axis=2, tiled=True),
        lax.all_to_all(mirror_send, ("chan", "strip"), split_axis=2, concat_axis=2, tiled=True),
    )
    direct_got = direct_got.reshape(2, local_chans, chans, strips, width, ratio, piece)
    direct_tiles = jnp.transpose(direct_got, (0, 2, 1, 4, 5, 3, 6)).reshape(
        2, chans * local_chans, width, block
    )
    mirror_got = mirror_got.reshape(2, local_chans, chans, strips, block, piece)
    mirror_tiles = jnp.transpose(mirror_got, (0, 2, 1, 3, 5, 4)).reshape(
        2, chans * local_chans, width, block
    )
    return (direct_tiles, mirror_tiles)


def general(wave_field, radial_op, coupling, couple, partner, extent):
    chans = lax.axis_size("chan")
    grid = wave_field.shape[3]
    strip_rows = wave_field.shape[2]
    chan_cols = grid // chans
    row_pos = lax.axis_index("strip") * strip_rows + jnp.arange(strip_rows)
    col_pos = lax.axis_index("chan") * chan_cols + jnp.arange(chan_cols)
    pots = potentials(row_pos, col_pos, grid, coupling.shape[2])
    live = (row_pos[None, :, None] < extent[:, None, None]) & (
        col_pos[None, None, :] < extent[:, None, None]
    )

    def radial(block):
        return radial_product(radial_op, block)

    def product_columns(field_rows):
        return radial(lax.all_to_all(field_rows, "strip", split_axis=3, concat_axis=2, tiled=True))

    field_tiles = lax.all_to_all(wave_field, "chan", split_axis=3, concat_axis=1, tiled=True)
    rows_tiles, mirror_tiles = spread_tiles(product_columns(spread_columns(wave_field)))
    first_step = couple_terms(
        field_tiles, rows_tiles, mirror_tiles, coupling, couple, partner, pots, live
    )
    image = product_columns(
        spread_columns(lax.all_to_all(first_step, "chan", split_axis=1, concat_axis=3, tiled=True))
    )
    rows_tiles, mirror_tiles = spread_tiles(image)
    applied = couple_terms(
        first_step, rows_tiles, mirror_tiles, coupling, couple, partner, pots, live
    )
    second_step = 2.0 * applied - field_tiles
    return (first_step, second_step)


MESH = pl.DeviceIdType.MESH
ANY = pl.BlockSpec(memory_space=pl.ANY)
SMEM = pl.BlockSpec(memory_space=pltpu.SMEM)


def rem(value, count):
    return lax.rem(value, count)


def greet(others):
    barrier = pltpu.get_barrier_semaphore()
    for other in others:
        pl.semaphore_signal(barrier, inc=1, device_id=other, device_id_type=MESH)
    pl.semaphore_wait(barrier, len(others))


def remote(source, target, send, recv, device):
    return pltpu.make_async_remote_copy(
        src_ref=source,
        dst_ref=target,
        send_sem=send,
        recv_sem=recv,
        device_id=device,
        device_id_type=MESH,
    )


def columns(block, width):
    return pl.ds(pl.multiple_of(block * width, 128), width)


def lines(block, height):
    return pl.ds(pl.multiple_of(block * height, 8), height)


def each(count, body):
    def one(n, carry):
        body(n)
        return carry

    lax.fori_loop(0, count, one, 0)


def far_first(n, strips):
    return strips // 2 + ((n + 1) // 2) * (2 * rem(n + 1, 2) - 1)


def pick(j, values):
    chosen = jnp.int32(values[-1])
    for i, value in enumerate(values[:-1]):
        chosen = jnp.where(j == i, jnp.int32(value), chosen)
    return chosen


class Reach:
    def __init__(self, levels, rows, width):
        self.unit = width // 128
        self.width = width
        self.levels = levels
        self.lanes = [-(-level * rows // 128) for level in levels]
        self.parts = sorted({n % self.unit for n in self.lanes} - {0})

    def rows(self, j, strip):
        return strip < pick(j, self.levels)

    def blocks(self, j):
        return pick(j, [-(-n // self.unit) for n in self.lanes])

    def spans(self, j, block, alive, act):
        full = pick(j, [n // self.unit for n in self.lanes])
        rest = pick(j, [n % self.unit for n in self.lanes])

        @pl.when(jnp.logical_and(alive, block < full))
        def _():
            act(self.width)

        for part in self.parts:

            @pl.when(jnp.logical_and(alive, jnp.logical_and(block == full, rest == part)))
            def _():
                act(part * 128)

    def columns_alive(self, j, block):
        return pick(j, self.lanes) * 128 - block * self.width


def split(read, high, low, count, step):
    def one(n, carry):
        start = pl.multiple_of(n * step, step)
        at = pl.ds(start, step)
        value = read(start, at)
        top = value.astype(jnp.bfloat16)
        high[at, :] = top
        low[at, :] = (value - top.astype(jnp.float32)).astype(jnp.bfloat16)
        return carry

    lax.fori_loop(0, count // step, one, 0)


def load_operator(radial, turned, sems):
    per, width, grid = turned.shape
    return [
        pltpu.make_async_copy(radial.at[pl.ds(n * width, width), :], turned.at[n], sems.at[n])
        for n in range(grid // width)
    ]


def split_operator(loads, turned, rh, rl):
    width = turned.shape[1]
    for n, load in enumerate(loads):
        load.wait()
        at = pl.ds(n * width, width)
        split(lambda _, at, n=n: turned[n, at, :], rh.at[at, :], rl.at[at, :], width, 32)


def product(j, y, img, turned, rh, rl, yh, yl, depth, lanes, blocks):
    grid, width = y.shape[1:]
    step = 64

    def read(start, at):
        row = start + lax.broadcasted_iota(jnp.int32, (step, width), 0)
        col = lax.broadcasted_iota(jnp.int32, (step, width), 1)
        return jnp.where(jnp.logical_and(row < depth, col < lanes), y[j, at, :], 0.0)

    split(read, yh, yl, grid, step)

    def one(n):
        at = pl.ds(pl.multiple_of(n * 128, 128), 128)
        top = rh[at, :]
        total = jnp.dot(top, yh[...], preferred_element_type=jnp.float32)
        total = total + jnp.dot(top, yl[...], preferred_element_type=jnp.float32)
        total = total + jnp.dot(rl[at, :], yh[...], preferred_element_type=jnp.float32)
        img[j, at, :] = total
        turned[j, :, at] = total.T

    each(blocks * (width // 128), one)


FIRST_ORDER = (3, 2, 0, 1)
ORDER = (0, 2, 3, 1)


def first_kernel(
    levels, chans, strips, x, radial, f, mt, dd, y, img, turned, w, rh, rl, yh, yl,
    gs, gr, gl, cs, cr, cl, rs, ks, zs, zr, ms, mr, ml, fs, fr, ls,
):
    c = lax.axis_index("chan")
    s = lax.axis_index("strip")
    per, grid, width = y.shape
    rows = x.shape[1]
    group = s // 2
    member = rem(s, 2)
    reach = Reach(levels, rows, width)
    ring = [(c, rem(s + d, strips)) for d in range(1, strips)]
    plane = [(rem(c + r, chans), group * 2 + m) for r in range(1, chans) for m in range(2)]
    greet(ring + plane)

    def gather(j, d):
        t = rem(s + d, strips)
        return remote(
            x.at[rem(t, 2) * per + j, :, columns(t // 2, width)],
            y.at[j, lines(s, rows), :],
            gs.at[j, d],
            gr.at[j, d],
            (c, t),
        )

    def keep(j):
        return pltpu.make_async_copy(
            x.at[member * per + j, :, columns(group, width)], y.at[j, lines(s, rows), :], gl.at[j]
        )

    def field(p, r):
        to = rem(c + r, chans)
        part = x.at[pl.ds(p * per, per), :, columns(to, width)]
        target = f.at[p * chans + c]
        return remote(part, target, cs.at[r * 2 + p], cr.at[r * 2 + p], (to, s))

    def own_field(p):
        part = x.at[pl.ds(p * per, per), :, columns(c, width)]
        return pltpu.make_async_copy(part, f.at[p * chans + c], cl.at[p])

    def hop(j, d, lanes):
        t = rem(s + d, strips)
        return remote(
            img.at[j, lines(t, rows), pl.ds(0, lanes)],
            w.at[j, s, :, pl.ds(0, lanes)],
            zs.at[j, d],
            zr.at[j, d],
            (c, t),
        )

    def own_hop(j):
        return pltpu.make_async_copy(img.at[j, lines(s, rows), :], w.at[j, s], ks.at[j])

    def mirror(j, k):
        to = rem(c + k // 2, chans)
        m = rem(member + rem(k, 2), 2)
        part = turned.at[j, lines(m, rows), columns(to, width)]
        target = mt.at[member * chans + c, j]
        return remote(part, target, ms.at[j, k], mr.at[j, k], (to, group * 2 + m))

    def own_mirror(j):
        part = turned.at[j, lines(member, rows), columns(c, width)]
        return pltpu.make_async_copy(part, mt.at[member * chans + c, j], ml.at[j])

    def forward(j, u):
        to = u // 2
        p = rem(u, 2)
        away = rem(to - c + chans, chans)

        def act(lanes):
            part = w.at[j, u, :, pl.ds(0, lanes)]
            target = dd.at[p * chans + c, j, :, pl.ds(0, lanes)]

            @pl.when(away == 0)
            def _():
                pltpu.make_async_copy(part, target, ls.at[j, p]).start()

            @pl.when(away != 0)
            def _():
                k = away * 2 + p
                remote(part, target, fs.at[j, k], fr.at[j, k], (to, s)).start()

        reach.spans(j, to, reach.rows(j, s), act)

    def begin(j):
        each(strips - 1, lambda n: gather(j, far_first(n, strips)).start())
        keep(j).start()

    loads = load_operator(radial, turned, rs)
    each(2, lambda i: begin(pick(i, FIRST_ORDER)))
    for load in loads:
        load.start()
    each(2 * chans - 2, lambda n: field(rem(n, 2), 1 + n // 2).start())
    each(2, lambda p: own_field(p).start())
    split_operator(loads, turned, rh, rl)

    def launch(j):
        def one(n):
            d = far_first(n, strips)
            alive = reach.rows(j, rem(s + d, strips))
            reach.spans(j, group, alive, lambda lanes: hop(j, d, lanes).start())

        each(strips - 1, one)
        own_hop(j).start()

    def relay(i):
        j = pick(i, FIRST_ORDER)
        own_hop(j).wait()

        def one(n):
            u = rem(c + n // 2, chans) * 2 + rem(n, 2)
            d = rem(s - u + strips, strips)
            alive = jnp.logical_and(reach.rows(j, s), u != s)
            reach.spans(j, u // 2, alive, lambda lanes: hop(j, d, lanes).wait_recv())
            forward(j, u)

        each(strips, one)

    def work(i):
        j = pick(i, FIRST_ORDER)
        keep(j).wait()
        each(strips - 1, lambda n: gather(j, n + 1).wait_recv())
        product(j, y, img, turned, rh, rl, yh, yl, grid, width, chans)
        each(2 * chans - 1, lambda n: mirror(j, n + 1).start())
        own_mirror(j).start()

        @pl.when(i < per - 2)
        def _():
            begin(pick(i + 2, FIRST_ORDER))

        launch(j)

        @pl.when(i == 2)
        def _():
            relay(0)

    def finish(j):
        def sent(n):
            d = n + 1
            gather(j, d).wait_send()
            alive = reach.rows(j, rem(s + d, strips))
            reach.spans(j, group, alive, lambda lanes: hop(j, d, lanes).wait_send())
            mirror(j, d).wait()

        each(strips - 1, sent)
        own_mirror(j).wait()
        here = reach.rows(j, s)

        def passed(k, lanes):
            part = w.at[j, 0, :, pl.ds(0, lanes)]
            target = dd.at[rem(k, 2) * chans + c, j, :, pl.ds(0, lanes)]
            return remote(part, target, fs.at[j, k], fr.at[j, k], (rem(c + k // 2, chans), s))

        def one(n):
            k = n + 2
            to = rem(c + k // 2, chans)
            reach.spans(j, to, here, lambda lanes: passed(k, lanes).wait_send())
            reach.spans(j, c, here, lambda lanes: passed(k, lanes).wait_recv())

        def own(p):
            def act(lanes):
                part = w.at[j, 0, :, pl.ds(0, lanes)]
                target = dd.at[p * chans + c, j, :, pl.ds(0, lanes)]
                pltpu.make_async_copy(part, target, ls.at[j, p]).wait()

            reach.spans(j, c, here, act)

        each(2, own)
        each(2 * chans - 2, one)

    each(per, work)
    each(per - 1, lambda i: relay(i + 1))
    each(2 * chans - 2, lambda n: field(rem(n, 2), 1 + n // 2).wait())
    each(2, lambda p: own_field(p).wait())
    each(per, finish)


def second_kernel(
    levels, chans, strips, mates, v, radial, b, sd, y, img, turned, w, rh, rl, yh, yl, sib,
    bs, br, gs, gr, gl, rs, ks, zs, zr, ms, mr, fs, fr, ls,
):
    c = lax.axis_index("chan")
    s = lax.axis_index("strip")
    per, grid, width = y.shape
    rows = v.shape[2]
    group = s // 2
    member = rem(s, 2)
    reach = Reach(levels, rows, width)
    ring = [(c, rem(s + d, strips)) for d in range(1, strips)]
    plane = [(rem(c + r, chans), s) for r in range(1, chans)]
    twin = (c, group * 2 + 1 - member)
    greet(ring + plane)

    def back(j, k, lanes):
        to = rem(c + k // 2, chans)
        p = rem(k, 2)
        return remote(
            v.at[p * chans + to, j, :, pl.ds(0, lanes)],
            b.at[p * chans + c, j, :, pl.ds(0, lanes)],
            bs.at[j, k],
            br.at[j, k],
            (to, s),
        )

    def arrive(j, d, u, lanes):
        return remote(
            v.at[0, 0, :, pl.ds(0, lanes)],
            y.at[j, lines(u, rows), pl.ds(0, lanes)],
            gs.at[j, d],
            gr.at[j, d],
            (c, rem(s + d, strips)),
        )

    def forward(source, j, block, p):
        t = block * 2 + p
        away = rem(t - s + strips, strips)

        def act(lanes):
            part = source.at[:, pl.ds(0, lanes)]
            target = y.at[j, lines(s, rows), pl.ds(0, lanes)]

            @pl.when(away == 0)
            def _():
                pltpu.make_async_copy(part, target, gl.at[j]).start()

            @pl.when(away != 0)
            def _():
                remote(part, target, gs.at[j, away], gr.at[j, away], (c, t)).start()

        reach.spans(j, block, reach.rows(j, s), act)

    def begin(j):
        def one(n):
            k = 2 * chans - 1 - n
            reach.spans(j, c, reach.rows(j, s), lambda lanes: back(j, k, lanes).start())

        each(2 * chans - 2, one)

    def pass_on(j):
        each(2, lambda p: forward(v.at[p * chans + c, j], j, c, p))

        def one(n):
            k = 2 * chans - 1 - n
            p = rem(k, 2)
            sender = rem(c - k // 2 + chans, chans)
            here = reach.rows(j, s)
            reach.spans(j, sender, here, lambda lanes: back(j, k, lanes).wait_recv())
            forward(b.at[p * chans + sender, j], j, sender, p)

        each(2 * chans - 2, one)

    def hop(j, d, lanes):
        t = rem(s + d, strips)
        return remote(
            img.at[j, lines(t, rows), pl.ds(0, lanes)],
            w.at[j, s, :, pl.ds(0, lanes)],
            zs.at[j, d],
            zr.at[j, d],
            (c, t),
        )

    def own_hop(j):
        return pltpu.make_async_copy(img.at[j, lines(s, rows), :], w.at[j, s], ks.at[j])

    def mirror(j):
        part = turned.at[j, lines(1 - member, rows), :]
        return remote(part, sib.at[j], ms.at[j], mr.at[j], twin)

    def busy(j):
        return group < reach.blocks(j)

    def combine(j, u):
        block = u // 2
        other = mates[j]
        mirrored = group < reach.blocks(other)
        alive = jnp.logical_and(reach.rows(j, s), block < reach.blocks(j))
        own = rem(u, 2) == member
        at = columns(block, width)

        def add(read):
            def one(n):
                line = pl.ds(pl.multiple_of(n * 32, 32), 32)
                w[j, u, line, :] = w[j, u, line, :] + jnp.where(mirrored, read(n), 0.0)

            each(rows // 32, one)

        @pl.when(jnp.logical_and(alive, own))
        def _():
            add(
                lambda n: turned[
                    other, pl.ds(pl.multiple_of(member * rows + n * 32, 32), 32), at
                ]
            )

        @pl.when(jnp.logical_and(alive, jnp.logical_not(own)))
        def _():
            add(lambda n: sib[other, pl.ds(pl.multiple_of(n * 32, 32), 32), at])

    def send(j, u):
        to = u // 2
        p = rem(u, 2)
        away = rem(to - c + chans, chans)

        def act(lanes):
            part = w.at[j, u, :, pl.ds(0, lanes)]
            target = sd.at[p * chans + c, j, :, pl.ds(0, lanes)]

            @pl.when(away == 0)
            def _():
                pltpu.make_async_copy(part, target, ls.at[j, p]).start()

            @pl.when(away != 0)
            def _():
                k = away * 2 + p
                remote(part, target, fs.at[j, k], fr.at[j, k], (to, s)).start()

        reach.spans(j, to, reach.rows(j, s), act)

    loads = load_operator(radial, turned, rs)
    each(per, begin)
    for load in loads:
        load.start()
    each(per, pass_on)
    split_operator(loads, turned, rh, rl)

    def launch(j):
        def one(n):
            d = far_first(n, strips)
            alive = reach.rows(j, rem(s + d, strips))
            reach.spans(j, group, alive, lambda lanes: hop(j, d, lanes).start())

        each(strips - 1, one)

        @pl.when(busy(j))
        def _():
            own_hop(j).start()

    def work(j):
        depth = pick(j, levels) * rows

        def kept(lanes):
            target = y.at[j, lines(s, rows), pl.ds(0, lanes)]
            pltpu.make_async_copy(v.at[0, 0, :, pl.ds(0, lanes)], target, gl.at[j]).wait()

        reach.spans(j, group, reach.rows(j, s), kept)

        def arrived(n):
            d = n + 1
            u = rem(s - d + strips, strips)
            alive = reach.rows(j, u)
            reach.spans(j, group, alive, lambda lanes: arrive(j, d, u, lanes).wait_recv())

        each(strips - 1, arrived)

        @pl.when(busy(j))
        def _():
            lanes = reach.columns_alive(j, group)
            product(j, y, img, turned, rh, rl, yh, yl, depth, lanes, chans)
            mirror(j).start()

        @pl.when(j != ORDER[-1])
        def _():
            launch(j)

    def hear(j):
        @pl.when(busy(j))
        def _():
            mirror(j).wait_recv()
            own_hop(j).wait()

    def relay(i):
        j = pick(i, ORDER)

        def one(n):
            u = rem(c + n // 2, chans) * 2 + rem(n, 2)
            d = rem(s - u + strips, strips)
            alive = jnp.logical_and(reach.rows(j, s), u != s)
            reach.spans(j, u // 2, alive, lambda lanes: hop(j, d, lanes).wait_recv())
            combine(j, u)
            send(j, u)

        each(strips, one)

    def finish(j):
        here = reach.rows(j, s)

        def sent(n):
            d = n + 1
            t = rem(s + d, strips)
            reach.spans(j, t // 2, here, lambda lanes: arrive(j, d, s, lanes).wait_send())
            alive = reach.rows(j, t)
            reach.spans(j, group, alive, lambda lanes: hop(j, d, lanes).wait_send())

        each(strips - 1, sent)

        @pl.when(busy(j))
        def _():
            mirror(j).wait_send()

        def passed(k, lanes):
            part = w.at[j, 0, :, pl.ds(0, lanes)]
            target = sd.at[rem(k, 2) * chans + c, j, :, pl.ds(0, lanes)]
            return remote(part, target, fs.at[j, k], fr.at[j, k], (rem(c + k // 2, chans), s))

        def one(n):
            k = n + 2
            to = rem(c + k // 2, chans)
            reach.spans(j, c, here, lambda lanes: back(j, k, lanes).wait_send())
            reach.spans(j, to, here, lambda lanes: passed(k, lanes).wait_send())
            reach.spans(j, c, here, lambda lanes: passed(k, lanes).wait_recv())

        def own(p):
            def act(lanes):
                part = w.at[j, 0, :, pl.ds(0, lanes)]
                target = sd.at[p * chans + c, j, :, pl.ds(0, lanes)]
                pltpu.make_async_copy(part, target, ls.at[j, p]).wait()

            reach.spans(j, c, here, act)

        each(2, own)
        each(2 * chans - 2, one)

    each(per, work)
    launch(ORDER[-1])
    each(per, hear)
    each(per, relay)
    each(per, finish)


def exchange(kernel, ident, outs, buffers, sems, *operands):
    chans = lax.axis_size("chan")
    strips = lax.axis_size("strip")
    return pl.pallas_call(
        functools.partial(kernel, chans, strips),
        out_shape=[jax.ShapeDtypeStruct(shape, jnp.float32) for shape in outs],
        in_specs=[SMEM] * (len(operands) - 2) + [ANY] * 2,
        out_specs=[ANY] * len(outs),
        scratch_shapes=[pltpu.VMEM(*buffer) for buffer in buffers]
        + [pltpu.SemaphoreType.DMA(n) for n in sems],
        compiler_params=pltpu.CompilerParams(
            collective_id=ident, has_side_effects=True, vmem_limit_bytes=62 * 2**20
        ),
    )(*operands)


def couple_kernel(count, last, ints, links, reals, *refs):
    if last:
        field, radial, base, out, pots = refs
    else:
        field, direct, mirror, out, dealt, pots = refs
    channels, height, width = field.shape[1:]
    orders = pots.shape[0]
    partners, extents, firsts, seconds = [2 + n * channels for n in range(4)]
    spacing = 8.0 / count
    row = ints[0] + pl.program_id(0) * height
    row = row + lax.broadcasted_iota(jnp.int32, (height, width), 0)
    col = ints[1] + lax.broadcasted_iota(jnp.int32, (height, width), 1)
    first = row.astype(jnp.float32) * spacing
    second = col.astype(jnp.float32) * spacing
    greater = jnp.maximum(first, second)
    root = jnp.sqrt(greater * greater + 1.0)
    ratio = jnp.minimum(first, second) / root
    pot = 1.0 / root
    for order in range(orders):
        pots[order] = pot
        pot = pot * ratio
    reach = jnp.maximum(row, col)

    def channel(c, carry):
        mine = ints[firsts + c]
        dealt_at = ints[seconds + c]
        if last:
            real_part = radial[0, dealt_at]
            imag_part = radial[1, dealt_at]
        else:
            other = ints[firsts + ints[partners + c]]
            real_part = direct[0, mine] + mirror[0, other]
            imag_part = direct[1, mine] + mirror[1, other]
        for order in range(orders):
            k = links[order, c]
            if not last:
                k = ints[firsts + k]
            c_real = reals[0, order, c]
            c_imag = reals[1, order, c]
            pot = pots[order]
            s_real = pot * field[0, k]
            s_imag = pot * field[1, k]
            real_part = real_part + (c_real * s_real - c_imag * s_imag)
            imag_part = imag_part + (c_real * s_imag + c_imag * s_real)
        live = reach < ints[extents + c]
        real_part = jnp.where(live, real_part, 0.0)
        imag_part = jnp.where(live, imag_part, 0.0)
        if last:
            real_part = 2.0 * real_part - base[0, mine]
            imag_part = 2.0 * imag_part - base[1, mine]
        else:
            dealt[0, dealt_at] = real_part
            dealt[1, dealt_at] = imag_part
        out[0, c] = real_part
        out[1, c] = imag_part
        return carry

    lax.fori_loop(0, channels, channel, 0)


def couple_tiles(count, scalars, orders, last, arrays):
    shape = arrays[0].shape
    height = 16
    block = pl.BlockSpec((2, shape[1], height, shape[3]), lambda n: (0, 0, n, 0))
    outs = 1 if last else 2
    return pl.pallas_call(
        functools.partial(couple_kernel, count, last),
        grid=(shape[2] // height,),
        out_shape=[jax.ShapeDtypeStruct(shape, jnp.float32)] * outs,
        in_specs=[SMEM] * len(scalars) + [block] * len(arrays),
        out_specs=[block] * outs,
        scratch_shapes=[pltpu.VMEM((orders, height, shape[3]), jnp.float32)],
    )(*scalars, *arrays)


FIRST_LEVELS = ((8, 6, 5, 4), (8, 7, 5, 4), (8, 8, 6, 4), (8, 8, 7, 4), (8, 8, 6, 5), (8, 8, 8, 4), (8, 8, 7, 6), (8, 8, 8, 8))
SECOND_LEVELS = ((8, 6, 4, 4), (8, 6, 5, 4), (8, 8, 4, 4), (8, 7, 5, 4), (8, 8, 6, 4), (8, 8, 6, 5), (8, 8, 7, 5), (8, 8, 8, 8))


def deal_kernel(
    per, rows, width, partner, extent, ints, order, mates, choice, choice_next,
    far, keys, lines_of, places,
):
    channels = extent.shape[0]
    chans = channels // per
    c = lax.axis_index("chan")
    ints[0] = lax.axis_index("strip") * rows
    ints[1] = c * width
    for n in range(2 * per):
        far[n] = 0

    def head(i):
        return jnp.minimum(i, partner[i])

    def key(i):
        keys[i] = jnp.where(i < partner[i], extent[i] + extent[partner[i]], -1)

    def place_among(i, same):
        place = jnp.int32(0)
        for k in range(channels):
            tie = jnp.logical_and(extent[k] == extent[i], k < i)
            ahead = jnp.logical_and(same(k), jnp.logical_or(extent[k] > extent[i], tie))
            place = place + jnp.where(ahead, 1, 0)
        return place

    def first(i):
        line = i // per
        place = place_among(i, lambda k: k // per == line)
        ints[2 + 2 * channels + i] = line * per + place
        far[place] = jnp.maximum(far[place], extent[i])

        @pl.when(line == c)
        def _():
            order[place] = i - line * per

        mine = keys[head(i)]
        rank = jnp.int32(0)
        for k in range(channels):
            tie = jnp.logical_and(keys[k] == mine, k < head(i))
            rank = rank + jnp.where(jnp.logical_or(keys[k] > mine, tie), 1, 0)
        lines_of[i] = jnp.where(rank < chans, rank, 2 * chans - 1 - rank)

    def second(i):
        line = lines_of[i]
        place = place_among(i, lambda k: lines_of[k] == line)
        places[i] = place
        ints[2 + i] = partner[i]
        ints[2 + channels + i] = extent[i]
        ints[2 + 3 * channels + i] = line * per + place
        far[per + place] = jnp.maximum(far[per + place], extent[i])

    def match(i):
        @pl.when(lines_of[i] == c)
        def _():
            mates[places[i]] = places[partner[i]]

    each(channels, key)
    each(channels, first)
    each(channels, second)
    each(channels, match)
    for n, (table, out) in enumerate(((FIRST_LEVELS, choice), (SECOND_LEVELS, choice_next))):
        best = jnp.int32(len(table) - 1)
        for v in reversed(range(len(table) - 1)):
            fits = far[n * per] <= table[v][0] * rows
            for j in range(1, per):
                fits = jnp.logical_and(fits, far[n * per + j] <= table[v][j] * rows)
            best = jnp.where(fits, jnp.int32(v), best)
        out[0] = best


def deal(partner, extent, per, rows, width):
    channels = extent.shape[0]
    sizes = (2 + 4 * channels, per, per, 1, 1)
    scratch = (2 * per, channels, channels, channels)
    return pl.pallas_call(
        functools.partial(deal_kernel, per, rows, width),
        out_shape=[jax.ShapeDtypeStruct((size,), jnp.int32) for size in sizes],
        in_specs=[SMEM] * 2,
        out_specs=[SMEM] * len(sizes),
        scratch_shapes=[pltpu.SMEM((size,), jnp.int32) for size in scratch],
    )(partner, extent)


def sort_kernel(order, x, out):
    out[...] = x[...]


def sort_field(order, x):
    parts, per, rows, grid = x.shape
    height = rows // 4
    block = (1, 1, height, grid)
    return pl.pallas_call(
        sort_kernel,
        grid_spec=pltpu.PrefetchScalarGridSpec(
            num_scalar_prefetch=1,
            grid=(parts, per, rows // height),
            in_specs=[pl.BlockSpec(block, lambda p, j, n, order: (p, order[j], n, 0))],
            out_specs=pl.BlockSpec(block, lambda p, j, n, order: (p, j, n, 0)),
        ),
        out_shape=jax.ShapeDtypeStruct(x.shape, x.dtype),
    )(order, x)


def local(wave_field, radial_op, coupling, couple, partner, extent):
    chans = lax.axis_size("chan")
    strips = lax.axis_size("strip")
    per, rows, grid = wave_field.shape[1:]
    width = grid // chans
    orders = coupling.shape[2]
    tiles = (2 * chans, per, rows, width)
    whole = (2, chans * per, rows, width)
    ints, order, mates, choice, choice_next = deal(partner, extent, per, rows, width)
    scalars = (ints, couple.T, coupling.transpose(0, 2, 1))
    buffers = [
        ((per, grid, width), jnp.float32),
        ((per, grid, width), jnp.float32),
        ((per, width, grid), jnp.float32),
        ((per, strips, rows, width), jnp.float32),
        ((grid, grid), jnp.bfloat16),
        ((grid, grid), jnp.bfloat16),
        ((grid, width), jnp.bfloat16),
        ((grid, width), jnp.bfloat16),
    ]
    one = (per,)
    ring = (per, strips)
    plane = (per, 2 * chans)
    sorted_field = sort_field(order, wave_field).reshape(2 * per, rows, grid)

    def first_call(n):
        def call(x):
            return exchange(
                functools.partial(first_kernel, FIRST_LEVELS[n]),
                n,
                [tiles, tiles, tiles],
                buffers,
                [ring, ring, one, (2 * chans,), (2 * chans,), (2,), (chans,)]
                + [one, ring, ring, plane, plane, one, plane, plane, (per, 2)],
                x,
                radial_op,
            )

        return call

    def second_call(n):
        def call(mates, v):
            return exchange(
                functools.partial(second_kernel, SECOND_LEVELS[n]),
                len(FIRST_LEVELS) + n,
                [tiles, tiles],
                buffers + [((per, rows, grid), jnp.float32)],
                [plane, plane, ring, ring, one, (chans,)]
                + [one, ring, ring, one, one, plane, plane, (per, 2)],
                mates,
                v,
                radial_op,
            )

        return call

    field, mirror, direct = lax.switch(
        choice[0], [first_call(n) for n in range(len(FIRST_LEVELS))], sorted_field
    )
    field = field.reshape(whole)
    first_step, dealt = couple_tiles(
        grid, scalars, orders, False, (field, direct.reshape(whole), mirror.reshape(whole))
    )
    _, radial = lax.switch(
        choice_next[0],
        [second_call(n) for n in range(len(SECOND_LEVELS))],
        mates,
        dealt.reshape(tiles),
    )
    second_step = couple_tiles(
        grid, scalars, orders, True, (first_step, radial.reshape(whole), field)
    )[0]
    return (first_step, second_step)


def dispatch(wave_field, *rest):
    chans = lax.axis_size("chan")
    strips = lax.axis_size("strip")
    per, rows, grid = wave_field.shape[1:]
    width = grid // chans
    aligned = width % 128 == 0 and rows % 64 == 0 and grid % 64 == 0
    if chans == 4 and strips == 8 and per == 4 and aligned:
        return local(wave_field, *rest)
    return general(wave_field, *rest)


def solution(mesh):
    placed = (P(None, "chan", "strip", None), P(), P(), P(), P(), P())
    return jax.shard_map(
        dispatch,
        mesh=mesh,
        in_specs=placed,
        out_specs=(P(None, None, "strip", "chan"), P(None, None, "strip", "chan")),
        check_vma=False,
    )
```

```python
import functools

import jax
import jax.numpy as jnp
from jax import lax
from jax.experimental import pallas as pl
from jax.experimental.pallas import tpu as pltpu
from jax.sharding import PartitionSpec as P


def potentials(row_pos, col_pos, count, orders):
    spacing = 8.0 / count
    first = row_pos.astype(jnp.float32) * spacing
    second = col_pos.astype(jnp.float32) * spacing
    lesser = jnp.minimum(first[:, None], second[None, :])
    greater = jnp.maximum(first[:, None], second[None, :])
    root = jnp.sqrt(greater * greater + 1.0)
    result = []
    for order in range(orders):
        result.append(lesser**order / root ** (order + 1))
    return result


def couple_terms(field, image_rows, mirrored, coupling, couple, partner, pots, live):
    total = image_rows + jnp.take(mirrored, partner, axis=1)
    real_part = total[0]
    imag_part = total[1]
    for order in range(len(pots)):
        source = jnp.take(field, couple[:, order], axis=1)
        c_real = coupling[0, :, order][:, None, None]
        c_imag = coupling[1, :, order][:, None, None]
        real_part = real_part + pots[order] * (c_real * source[0] - c_imag * source[1])
        imag_part = imag_part + pots[order] * (c_real * source[1] + c_imag * source[0])
    return jnp.where(live[None], jnp.stack([real_part, imag_part]), 0.0)


def radial_product(radial_op, block):
    return jnp.einsum("ak,pckb->pcab", radial_op, block, precision=lax.Precision.HIGHEST)


def spread_columns(field):
    strips = lax.axis_size("strip")
    local_chans = field.shape[1]
    local_rows = field.shape[2]
    grid = field.shape[3]
    piece = grid // (strips * strips)
    shaped = field.reshape(2, local_chans, local_rows, strips, strips, piece)
    return jnp.transpose(shaped, (0, 1, 2, 4, 3, 5)).reshape(2, local_chans, local_rows, grid)


def spread_tiles(image):
    chans = lax.axis_size("chan")
    strips = lax.axis_size("strip")
    local_chans = image.shape[1]
    grid = image.shape[2]
    width = image.shape[3]
    piece = grid // (strips * strips)
    ratio = strips // chans
    block = grid // chans
    direct_send = image.reshape(2, local_chans, strips, width, chans, ratio * piece)
    direct_send = jnp.transpose(direct_send, (0, 1, 4, 2, 3, 5)).reshape(
        2, local_chans, chans * strips, width, ratio * piece
    )
    mirror_send = image.reshape(2, local_chans, chans, block, strips, piece)
    mirror_send = jnp.transpose(mirror_send, (0, 1, 2, 4, 3, 5)).reshape(
        2, local_chans, chans * strips, block, piece
    )
    direct_got, mirror_got = (
        lax.all_to_all(direct_send, ("chan", "strip"), split_axis=2, concat_axis=2, tiled=True),
        lax.all_to_all(mirror_send, ("chan", "strip"), split_axis=2, concat_axis=2, tiled=True),
    )
    direct_got = direct_got.reshape(2, local_chans, chans, strips, width, ratio, piece)
    direct_tiles = jnp.transpose(direct_got, (0, 2, 1, 4, 5, 3, 6)).reshape(
        2, chans * local_chans, width, block
    )
    mirror_got = mirror_got.reshape(2, local_chans, chans, strips, block, piece)
    mirror_tiles = jnp.transpose(mirror_got, (0, 2, 1, 3, 5, 4)).reshape(
        2, chans * local_chans, width, block
    )
    return (direct_tiles, mirror_tiles)


def general(wave_field, radial_op, coupling, couple, partner, extent):
    chans = lax.axis_size("chan")
    grid = wave_field.shape[3]
    strip_rows = wave_field.shape[2]
    chan_cols = grid // chans
    row_pos = lax.axis_index("strip") * strip_rows + jnp.arange(strip_rows)
    col_pos = lax.axis_index("chan") * chan_cols + jnp.arange(chan_cols)
    pots = potentials(row_pos, col_pos, grid, coupling.shape[2])
    live = (row_pos[None, :, None] < extent[:, None, None]) & (
        col_pos[None, None, :] < extent[:, None, None]
    )

    def radial(block):
        return radial_product(radial_op, block)

    def product_columns(field_rows):
        return radial(lax.all_to_all(field_rows, "strip", split_axis=3, concat_axis=2, tiled=True))

    field_tiles = lax.all_to_all(wave_field, "chan", split_axis=3, concat_axis=1, tiled=True)
    rows_tiles, mirror_tiles = spread_tiles(product_columns(spread_columns(wave_field)))
    first_step = couple_terms(
        field_tiles, rows_tiles, mirror_tiles, coupling, couple, partner, pots, live
    )
    image = product_columns(
        spread_columns(lax.all_to_all(first_step, "chan", split_axis=1, concat_axis=3, tiled=True))
    )
    rows_tiles, mirror_tiles = spread_tiles(image)
    applied = couple_terms(
        first_step, rows_tiles, mirror_tiles, coupling, couple, partner, pots, live
    )
    second_step = 2.0 * applied - field_tiles
    return (first_step, second_step)


MESH = pl.DeviceIdType.MESH
ANY = pl.BlockSpec(memory_space=pl.ANY)
SMEM = pl.BlockSpec(memory_space=pltpu.SMEM)


def rem(value, count):
    return lax.rem(value, count)


def greet(others):
    barrier = pltpu.get_barrier_semaphore()
    for other in others:
        pl.semaphore_signal(barrier, inc=1, device_id=other, device_id_type=MESH)
    pl.semaphore_wait(barrier, len(others))


def remote(source, target, send, recv, device):
    return pltpu.make_async_remote_copy(
        src_ref=source,
        dst_ref=target,
        send_sem=send,
        recv_sem=recv,
        device_id=device,
        device_id_type=MESH,
    )


def columns(block, width):
    return pl.ds(pl.multiple_of(block * width, 128), width)


def lines(block, height):
    return pl.ds(pl.multiple_of(block * height, 8), height)


def each(count, body):
    def one(n, carry):
        body(n)
        return carry

    lax.fori_loop(0, count, one, 0)


def far_first(n, strips):
    return strips // 2 + ((n + 1) // 2) * (2 * rem(n + 1, 2) - 1)


def by_distance(n, group):
    half = group // 2
    near = jnp.where(n < 2, group, group + 1 - 2 * rem(group, 2))
    m = rem(n, 2)
    far = jnp.where(half == 0, 2 + m, 1 - m)
    return jnp.where(n < 4, near * 2 + m, far * 2 + (n - 4) // 2)


def pick(j, values):
    chosen = jnp.int32(values[-1])
    for i, value in enumerate(values[:-1]):
        chosen = jnp.where(j == i, jnp.int32(value), chosen)
    return chosen


class Reach:
    def __init__(self, levels, rows, width):
        self.unit = width // 128
        self.width = width
        self.levels = levels
        self.lanes = [-(-level * rows // 128) for level in levels]
        self.parts = sorted({n % self.unit for n in self.lanes} - {0})

    def rows(self, j, strip):
        return strip < pick(j, self.levels)

    def blocks(self, j):
        return pick(j, [-(-n // self.unit) for n in self.lanes])

    def spans(self, j, block, alive, act):
        full = pick(j, [n // self.unit for n in self.lanes])
        rest = pick(j, [n % self.unit for n in self.lanes])

        @pl.when(jnp.logical_and(alive, block < full))
        def _():
            act(self.width)

        for part in self.parts:

            @pl.when(jnp.logical_and(alive, jnp.logical_and(block == full, rest == part)))
            def _():
                act(part * 128)

    def columns_alive(self, j, block):
        return pick(j, self.lanes) * 128 - block * self.width


def split(read, high, low, count, step):
    def one(n, carry):
        start = pl.multiple_of(n * step, step)
        at = pl.ds(start, step)
        value = read(start, at)
        top = value.astype(jnp.bfloat16)
        high[at, :] = top
        low[at, :] = (value - top.astype(jnp.float32)).astype(jnp.bfloat16)
        return carry

    lax.fori_loop(0, count // step, one, 0)


def load_operator(radial, turned, sems):
    per, width, grid = turned.shape
    return [
        pltpu.make_async_copy(radial.at[pl.ds(n * width, width), :], turned.at[n], sems.at[n])
        for n in range(grid // width)
    ]


def split_operator(loads, turned, rh, rl):
    width = turned.shape[1]
    for n, load in enumerate(loads):
        load.wait()
        at = pl.ds(n * width, width)
        split(lambda _, at, n=n: turned[n, at, :], rh.at[at, :], rl.at[at, :], width, 32)


def product(j, y, img, turned, rh, rl, yh, yl, depth, lanes, blocks):
    grid, width = y.shape[1:]
    step = 64

    def read(start, at):
        row = start + lax.broadcasted_iota(jnp.int32, (step, width), 0)
        col = lax.broadcasted_iota(jnp.int32, (step, width), 1)
        return jnp.where(jnp.logical_and(row < depth, col < lanes), y[j, at, :], 0.0)

    split(read, yh, yl, grid, step)

    def one(n):
        at = pl.ds(pl.multiple_of(n * 128, 128), 128)
        top = rh[at, :]
        total = jnp.dot(top, yh[...], preferred_element_type=jnp.float32)
        total = total + jnp.dot(top, yl[...], preferred_element_type=jnp.float32)
        total = total + jnp.dot(rl[at, :], yh[...], preferred_element_type=jnp.float32)
        img[j, at, :] = total
        turned[j, :, at] = total.T

    each(blocks * (width // 128), one)


FIRST_ORDER = (3, 2, 0, 1)
ORDER = (0, 2, 3, 1)


def first_kernel(
    levels, chans, strips, x, radial, f, mt, dd, y, img, turned, w, rh, rl, yh, yl,
    gs, gr, gl, cs, cr, cl, rs, ks, zs, zr, ms, mr, ml, fs, fr, ls,
):
    c = lax.axis_index("chan")
    s = lax.axis_index("strip")
    per, grid, width = y.shape
    rows = x.shape[1]
    group = s // 2
    member = rem(s, 2)
    reach = Reach(levels, rows, width)
    ring = [(c, rem(s + d, strips)) for d in range(1, strips)]
    plane = [(rem(c + r, chans), group * 2 + m) for r in range(1, chans) for m in range(2)]
    greet(ring + plane)

    def gather(j, d):
        t = rem(s + d, strips)
        return remote(
            x.at[rem(t, 2) * per + j, :, columns(t // 2, width)],
            y.at[j, lines(s, rows), :],
            gs.at[j, d],
            gr.at[j, d],
            (c, t),
        )

    def keep(j):
        return pltpu.make_async_copy(
            x.at[member * per + j, :, columns(group, width)], y.at[j, lines(s, rows), :], gl.at[j]
        )

    def field(p, r):
        to = rem(c + r, chans)
        part = x.at[pl.ds(p * per, per), :, columns(to, width)]
        target = f.at[p * chans + c]
        return remote(part, target, cs.at[r * 2 + p], cr.at[r * 2 + p], (to, s))

    def own_field(p):
        part = x.at[pl.ds(p * per, per), :, columns(c, width)]
        return pltpu.make_async_copy(part, f.at[p * chans + c], cl.at[p])

    def hop(j, d, lanes):
        t = rem(s + d, strips)
        return remote(
            img.at[j, lines(t, rows), pl.ds(0, lanes)],
            w.at[j, s, :, pl.ds(0, lanes)],
            zs.at[j, d],
            zr.at[j, d],
            (c, t),
        )

    def own_hop(j):
        return pltpu.make_async_copy(img.at[j, lines(s, rows), :], w.at[j, s], ks.at[j])

    def mirror(j, k):
        to = rem(c + k // 2, chans)
        m = rem(member + rem(k, 2), 2)
        part = turned.at[j, lines(m, rows), columns(to, width)]
        target = mt.at[member * chans + c, j]
        return remote(part, target, ms.at[j, k], mr.at[j, k], (to, group * 2 + m))

    def own_mirror(j):
        part = turned.at[j, lines(member, rows), columns(c, width)]
        return pltpu.make_async_copy(part, mt.at[member * chans + c, j], ml.at[j])

    def forward(j, u):
        to = u // 2
        p = rem(u, 2)
        away = rem(to - c + chans, chans)

        def act(lanes):
            part = w.at[j, u, :, pl.ds(0, lanes)]
            target = dd.at[p * chans + c, j, :, pl.ds(0, lanes)]

            @pl.when(away == 0)
            def _():
                pltpu.make_async_copy(part, target, ls.at[j, p]).start()

            @pl.when(away != 0)
            def _():
                k = away * 2 + p
                remote(part, target, fs.at[j, k], fr.at[j, k], (to, s)).start()

        reach.spans(j, to, reach.rows(j, s), act)

    def begin(j):
        each(strips - 1, lambda n: gather(j, far_first(n, strips)).start())
        keep(j).start()

    loads = load_operator(radial, turned, rs)
    each(2, lambda i: begin(pick(i, FIRST_ORDER)))
    for load in loads:
        load.start()
    each(2 * chans - 2, lambda n: field(rem(n, 2), 1 + n // 2).start())
    each(2, lambda p: own_field(p).start())
    split_operator(loads, turned, rh, rl)

    def launch(j):
        def one(n):
            d = far_first(n, strips)
            alive = reach.rows(j, rem(s + d, strips))
            reach.spans(j, group, alive, lambda lanes: hop(j, d, lanes).start())

        each(strips - 1, one)
        own_hop(j).start()

    def relay(i):
        j = pick(i, FIRST_ORDER)
        own_hop(j).wait()

        def one(n):
            u = by_distance(n, group)
            d = rem(s - u + strips, strips)
            alive = jnp.logical_and(reach.rows(j, s), u != s)
            reach.spans(j, u // 2, alive, lambda lanes: hop(j, d, lanes).wait_recv())
            forward(j, u)

        each(strips, one)

    def work(i):
        j = pick(i, FIRST_ORDER)
        keep(j).wait()
        each(strips - 1, lambda n: gather(j, n + 1).wait_recv())
        product(j, y, img, turned, rh, rl, yh, yl, grid, width, chans)
        each(2 * chans - 1, lambda n: mirror(j, n + 1).start())
        own_mirror(j).start()

        @pl.when(i < per - 2)
        def _():
            begin(pick(i + 2, FIRST_ORDER))

        launch(j)

        @pl.when(i == 2)
        def _():
            relay(0)

    def finish(j):
        def sent(n):
            d = n + 1
            gather(j, d).wait_send()
            alive = reach.rows(j, rem(s + d, strips))
            reach.spans(j, group, alive, lambda lanes: hop(j, d, lanes).wait_send())
            mirror(j, d).wait()

        each(strips - 1, sent)
        own_mirror(j).wait()
        here = reach.rows(j, s)

        def passed(k, lanes):
            part = w.at[j, 0, :, pl.ds(0, lanes)]
            target = dd.at[rem(k, 2) * chans + c, j, :, pl.ds(0, lanes)]
            return remote(part, target, fs.at[j, k], fr.at[j, k], (rem(c + k // 2, chans), s))

        def one(n):
            k = n + 2
            to = rem(c + k // 2, chans)
            reach.spans(j, to, here, lambda lanes: passed(k, lanes).wait_send())
            reach.spans(j, c, here, lambda lanes: passed(k, lanes).wait_recv())

        def own(p):
            def act(lanes):
                part = w.at[j, 0, :, pl.ds(0, lanes)]
                target = dd.at[p * chans + c, j, :, pl.ds(0, lanes)]
                pltpu.make_async_copy(part, target, ls.at[j, p]).wait()

            reach.spans(j, c, here, act)

        each(2, own)
        each(2 * chans - 2, one)

    each(per, work)
    each(per - 1, lambda i: relay(i + 1))
    each(2 * chans - 2, lambda n: field(rem(n, 2), 1 + n // 2).wait())
    each(2, lambda p: own_field(p).wait())
    each(per, finish)


def second_kernel(
    levels, chans, strips, mates, v, radial, b, sd, y, img, turned, w, rh, rl, yh, yl, sib,
    bs, br, gs, gr, gl, rs, ks, zs, zr, ms, mr, fs, fr, ls,
):
    c = lax.axis_index("chan")
    s = lax.axis_index("strip")
    per, grid, width = y.shape
    rows = v.shape[2]
    group = s // 2
    member = rem(s, 2)
    reach = Reach(levels, rows, width)
    ring = [(c, rem(s + d, strips)) for d in range(1, strips)]
    plane = [(rem(c + r, chans), s) for r in range(1, chans)]
    twin = (c, group * 2 + 1 - member)
    greet(ring + plane)

    def back(j, k, lanes):
        to = rem(c + k // 2, chans)
        p = rem(k, 2)
        return remote(
            v.at[p * chans + to, j, :, pl.ds(0, lanes)],
            b.at[p * chans + c, j, :, pl.ds(0, lanes)],
            bs.at[j, k],
            br.at[j, k],
            (to, s),
        )

    def arrive(j, d, u, lanes):
        return remote(
            v.at[0, 0, :, pl.ds(0, lanes)],
            y.at[j, lines(u, rows), pl.ds(0, lanes)],
            gs.at[j, d],
            gr.at[j, d],
            (c, rem(s + d, strips)),
        )

    def forward(source, j, block, p):
        t = block * 2 + p
        away = rem(t - s + strips, strips)

        def act(lanes):
            part = source.at[:, pl.ds(0, lanes)]
            target = y.at[j, lines(s, rows), pl.ds(0, lanes)]

            @pl.when(away == 0)
            def _():
                pltpu.make_async_copy(part, target, gl.at[j]).start()

            @pl.when(away != 0)
            def _():
                remote(part, target, gs.at[j, away], gr.at[j, away], (c, t)).start()

        reach.spans(j, block, reach.rows(j, s), act)

    def begin(j):
        def one(n):
            k = 2 * chans - 1 - n
            reach.spans(j, c, reach.rows(j, s), lambda lanes: back(j, k, lanes).start())

        each(2 * chans - 2, one)

    def pass_on(j):
        each(2, lambda p: forward(v.at[p * chans + c, j], j, c, p))

        def one(n):
            k = 2 * chans - 1 - n
            p = rem(k, 2)
            sender = rem(c - k // 2 + chans, chans)
            here = reach.rows(j, s)
            reach.spans(j, sender, here, lambda lanes: back(j, k, lanes).wait_recv())
            forward(b.at[p * chans + sender, j], j, sender, p)

        each(2 * chans - 2, one)

    def hop(j, d, lanes):
        t = rem(s + d, strips)
        return remote(
            img.at[j, lines(t, rows), pl.ds(0, lanes)],
            w.at[j, s, :, pl.ds(0, lanes)],
            zs.at[j, d],
            zr.at[j, d],
            (c, t),
        )

    def own_hop(j):
        return pltpu.make_async_copy(img.at[j, lines(s, rows), :], w.at[j, s], ks.at[j])

    def mirror(j):
        part = turned.at[j, lines(1 - member, rows), :]
        return remote(part, sib.at[j], ms.at[j], mr.at[j], twin)

    def busy(j):
        return group < reach.blocks(j)

    def combine(j, u):
        block = u // 2
        other = mates[j]
        mirrored = group < reach.blocks(other)
        alive = jnp.logical_and(reach.rows(j, s), block < reach.blocks(j))
        own = rem(u, 2) == member
        at = columns(block, width)

        def add(read):
            def one(n):
                line = pl.ds(pl.multiple_of(n * 32, 32), 32)
                w[j, u, line, :] = w[j, u, line, :] + jnp.where(mirrored, read(n), 0.0)

            each(rows // 32, one)

        @pl.when(jnp.logical_and(alive, own))
        def _():
            add(
                lambda n: turned[
                    other, pl.ds(pl.multiple_of(member * rows + n * 32, 32), 32), at
                ]
            )

        @pl.when(jnp.logical_and(alive, jnp.logical_not(own)))
        def _():
            add(lambda n: sib[other, pl.ds(pl.multiple_of(n * 32, 32), 32), at])

    def send(j, u):
        to = u // 2
        p = rem(u, 2)
        away = rem(to - c + chans, chans)

        def act(lanes):
            part = w.at[j, u, :, pl.ds(0, lanes)]
            target = sd.at[p * chans + c, j, :, pl.ds(0, lanes)]

            @pl.when(away == 0)
            def _():
                pltpu.make_async_copy(part, target, ls.at[j, p]).start()

            @pl.when(away != 0)
            def _():
                k = away * 2 + p
                remote(part, target, fs.at[j, k], fr.at[j, k], (to, s)).start()

        reach.spans(j, to, reach.rows(j, s), act)

    loads = load_operator(radial, turned, rs)
    each(per, begin)
    for load in loads:
        load.start()
    each(per, pass_on)
    split_operator(loads, turned, rh, rl)

    def launch(j):
        def one(n):
            d = far_first(n, strips)
            alive = reach.rows(j, rem(s + d, strips))
            reach.spans(j, group, alive, lambda lanes: hop(j, d, lanes).start())

        each(strips - 1, one)

    def work(j):
        depth = pick(j, levels) * rows

        def kept(lanes):
            target = y.at[j, lines(s, rows), pl.ds(0, lanes)]
            pltpu.make_async_copy(v.at[0, 0, :, pl.ds(0, lanes)], target, gl.at[j]).wait()

        reach.spans(j, group, reach.rows(j, s), kept)

        def arrived(n):
            d = n + 1
            u = rem(s - d + strips, strips)
            alive = reach.rows(j, u)
            reach.spans(j, group, alive, lambda lanes: arrive(j, d, u, lanes).wait_recv())

        each(strips - 1, arrived)

        @pl.when(busy(j))
        def _():
            lanes = reach.columns_alive(j, group)
            product(j, y, img, turned, rh, rl, yh, yl, depth, lanes, chans)
            mirror(j).start()
            own_hop(j).start()

        @pl.when(j == ORDER[0])
        def _():
            launch(j)

    def hear(j):
        @pl.when(busy(j))
        def _():
            mirror(j).wait_recv()
            own_hop(j).wait()

    def relay(i):
        j = pick(i, ORDER)

        def one(n):
            u = by_distance(n, group)
            d = rem(s - u + strips, strips)
            alive = jnp.logical_and(reach.rows(j, s), u != s)
            reach.spans(j, u // 2, alive, lambda lanes: hop(j, d, lanes).wait_recv())
            combine(j, u)
            send(j, u)

        each(strips, one)

    def finish(j):
        here = reach.rows(j, s)

        def sent(n):
            d = n + 1
            t = rem(s + d, strips)
            reach.spans(j, t // 2, here, lambda lanes: arrive(j, d, s, lanes).wait_send())
            alive = reach.rows(j, t)
            reach.spans(j, group, alive, lambda lanes: hop(j, d, lanes).wait_send())

        each(strips - 1, sent)

        @pl.when(busy(j))
        def _():
            mirror(j).wait_send()

        def passed(k, lanes):
            part = w.at[j, 0, :, pl.ds(0, lanes)]
            target = sd.at[rem(k, 2) * chans + c, j, :, pl.ds(0, lanes)]
            return remote(part, target, fs.at[j, k], fr.at[j, k], (rem(c + k // 2, chans), s))

        def one(n):
            k = n + 2
            to = rem(c + k // 2, chans)
            reach.spans(j, c, here, lambda lanes: back(j, k, lanes).wait_send())
            reach.spans(j, to, here, lambda lanes: passed(k, lanes).wait_send())
            reach.spans(j, c, here, lambda lanes: passed(k, lanes).wait_recv())

        def own(p):
            def act(lanes):
                part = w.at[j, 0, :, pl.ds(0, lanes)]
                target = sd.at[p * chans + c, j, :, pl.ds(0, lanes)]
                pltpu.make_async_copy(part, target, ls.at[j, p]).wait()

            reach.spans(j, c, here, act)

        each(2, own)
        each(2 * chans - 2, one)

    def step(i):
        @pl.when(i < per - 1)
        def _():
            launch(pick(i + 1, ORDER))

        relay(i)

    each(per, work)
    each(per, hear)
    each(per, step)
    each(per, finish)


def exchange(kernel, ident, outs, buffers, sems, *operands):
    chans = lax.axis_size("chan")
    strips = lax.axis_size("strip")
    return pl.pallas_call(
        functools.partial(kernel, chans, strips),
        out_shape=[jax.ShapeDtypeStruct(shape, jnp.float32) for shape in outs],
        in_specs=[SMEM] * (len(operands) - 2) + [ANY] * 2,
        out_specs=[ANY] * len(outs),
        scratch_shapes=[pltpu.VMEM(*buffer) for buffer in buffers]
        + [pltpu.SemaphoreType.DMA(n) for n in sems],
        compiler_params=pltpu.CompilerParams(
            collective_id=ident, has_side_effects=True, vmem_limit_bytes=62 * 2**20
        ),
    )(*operands)


def couple_kernel(count, last, ints, links, reals, *refs):
    if last:
        field, radial, base, out, pots = refs
    else:
        field, direct, mirror, out, dealt, pots = refs
    channels, height, width = field.shape[1:]
    orders = pots.shape[0]
    partners, extents, firsts, seconds = [2 + n * channels for n in range(4)]
    spacing = 8.0 / count
    row = ints[0] + pl.program_id(0) * height
    row = row + lax.broadcasted_iota(jnp.int32, (height, width), 0)
    col = ints[1] + lax.broadcasted_iota(jnp.int32, (height, width), 1)
    first = row.astype(jnp.float32) * spacing
    second = col.astype(jnp.float32) * spacing
    greater = jnp.maximum(first, second)
    root = jnp.sqrt(greater * greater + 1.0)
    ratio = jnp.minimum(first, second) / root
    pot = 1.0 / root
    for order in range(orders):
        pots[order] = pot
        pot = pot * ratio
    reach = jnp.maximum(row, col)

    def channel(c, carry):
        mine = ints[firsts + c]
        dealt_at = ints[seconds + c]
        if last:
            real_part = radial[0, dealt_at]
            imag_part = radial[1, dealt_at]
        else:
            other = ints[firsts + ints[partners + c]]
            real_part = direct[0, mine] + mirror[0, other]
            imag_part = direct[1, mine] + mirror[1, other]
        for order in range(orders):
            k = links[order, c]
            if not last:
                k = ints[firsts + k]
            c_real = reals[0, order, c]
            c_imag = reals[1, order, c]
            pot = pots[order]
            s_real = pot * field[0, k]
            s_imag = pot * field[1, k]
            real_part = real_part + (c_real * s_real - c_imag * s_imag)
            imag_part = imag_part + (c_real * s_imag + c_imag * s_real)
        live = reach < ints[extents + c]
        real_part = jnp.where(live, real_part, 0.0)
        imag_part = jnp.where(live, imag_part, 0.0)
        if last:
            real_part = 2.0 * real_part - base[0, mine]
            imag_part = 2.0 * imag_part - base[1, mine]
        else:
            dealt[0, dealt_at] = real_part
            dealt[1, dealt_at] = imag_part
        out[0, c] = real_part
        out[1, c] = imag_part
        return carry

    lax.fori_loop(0, channels, channel, 0)


def couple_tiles(count, scalars, orders, last, arrays):
    shape = arrays[0].shape
    height = 16
    block = pl.BlockSpec((2, shape[1], height, shape[3]), lambda n: (0, 0, n, 0))
    outs = 1 if last else 2
    return pl.pallas_call(
        functools.partial(couple_kernel, count, last),
        grid=(shape[2] // height,),
        out_shape=[jax.ShapeDtypeStruct(shape, jnp.float32)] * outs,
        in_specs=[SMEM] * len(scalars) + [block] * len(arrays),
        out_specs=[block] * outs,
        scratch_shapes=[pltpu.VMEM((orders, height, shape[3]), jnp.float32)],
    )(*scalars, *arrays)


FIRST_LEVELS = ((8, 6, 5, 4), (8, 7, 5, 4), (8, 8, 6, 4), (8, 8, 7, 4), (8, 8, 6, 5), (8, 8, 8, 4), (8, 8, 7, 6), (8, 8, 8, 8))
SECOND_LEVELS = ((8, 6, 4, 4), (8, 6, 5, 4), (8, 8, 4, 4), (8, 7, 5, 4), (8, 8, 6, 4), (8, 8, 6, 5), (8, 8, 7, 5), (8, 8, 8, 8))


def deal_kernel(
    per, rows, width, partner, extent, ints, order, mates, choice, choice_next,
    far, keys, lines_of, places,
):
    channels = extent.shape[0]
    chans = channels // per
    c = lax.axis_index("chan")
    ints[0] = lax.axis_index("strip") * rows
    ints[1] = c * width
    for n in range(2 * per):
        far[n] = 0

    def head(i):
        return jnp.minimum(i, partner[i])

    def key(i):
        keys[i] = jnp.where(i < partner[i], extent[i] + extent[partner[i]], -1)

    def place_among(i, same):
        place = jnp.int32(0)
        for k in range(channels):
            tie = jnp.logical_and(extent[k] == extent[i], k < i)
            ahead = jnp.logical_and(same(k), jnp.logical_or(extent[k] > extent[i], tie))
            place = place + jnp.where(ahead, 1, 0)
        return place

    def first(i):
        line = i // per
        place = place_among(i, lambda k: k // per == line)
        ints[2 + 2 * channels + i] = line * per + place
        far[place] = jnp.maximum(far[place], extent[i])

        @pl.when(line == c)
        def _():
            order[place] = i - line * per

        mine = keys[head(i)]
        rank = jnp.int32(0)
        for k in range(channels):
            tie = jnp.logical_and(keys[k] == mine, k < head(i))
            rank = rank + jnp.where(jnp.logical_or(keys[k] > mine, tie), 1, 0)
        lines_of[i] = jnp.where(rank < chans, rank, 2 * chans - 1 - rank)

    def second(i):
        line = lines_of[i]
        place = place_among(i, lambda k: lines_of[k] == line)
        places[i] = place
        ints[2 + i] = partner[i]
        ints[2 + channels + i] = extent[i]
        ints[2 + 3 * channels + i] = line * per + place
        far[per + place] = jnp.maximum(far[per + place], extent[i])

    def match(i):
        @pl.when(lines_of[i] == c)
        def _():
            mates[places[i]] = places[partner[i]]

    each(channels, key)
    each(channels, first)
    each(channels, second)
    each(channels, match)
    for n, (table, out) in enumerate(((FIRST_LEVELS, choice), (SECOND_LEVELS, choice_next))):
        best = jnp.int32(len(table) - 1)
        for v in reversed(range(len(table) - 1)):
            fits = far[n * per] <= table[v][0] * rows
            for j in range(1, per):
                fits = jnp.logical_and(fits, far[n * per + j] <= table[v][j] * rows)
            best = jnp.where(fits, jnp.int32(v), best)
        out[0] = best


def deal(partner, extent, per, rows, width):
    channels = extent.shape[0]
    sizes = (2 + 4 * channels, per, per, 1, 1)
    scratch = (2 * per, channels, channels, channels)
    return pl.pallas_call(
        functools.partial(deal_kernel, per, rows, width),
        out_shape=[jax.ShapeDtypeStruct((size,), jnp.int32) for size in sizes],
        in_specs=[SMEM] * 2,
        out_specs=[SMEM] * len(sizes),
        scratch_shapes=[pltpu.SMEM((size,), jnp.int32) for size in scratch],
    )(partner, extent)


def sort_kernel(order, x, out, held, loads, stores):
    parts, per = held.shape[:2]
    pieces = [(p, j) for j in range(per) for p in range(parts)]

    def load(p, j):
        return pltpu.make_async_copy(x.at[p, order[j]], held.at[p, j], loads.at[p, j])

    def store(p, j):
        return pltpu.make_async_copy(held.at[p, j], out.at[p, j], stores.at[p, j])

    for p, j in pieces:
        load(p, j).start()
    for p, j in pieces:
        load(p, j).wait()
        store(p, j).start()
    for p, j in pieces:
        store(p, j).wait()


def sort_field(order, x):
    parts, per = x.shape[:2]
    return pl.pallas_call(
        sort_kernel,
        out_shape=jax.ShapeDtypeStruct(x.shape, x.dtype),
        in_specs=[SMEM, ANY],
        out_specs=ANY,
        scratch_shapes=[
            pltpu.VMEM(x.shape, x.dtype),
            pltpu.SemaphoreType.DMA((parts, per)),
            pltpu.SemaphoreType.DMA((parts, per)),
        ],
    )(order, x)


def local(wave_field, radial_op, coupling, couple, partner, extent):
    chans = lax.axis_size("chan")
    strips = lax.axis_size("strip")
    per, rows, grid = wave_field.shape[1:]
    width = grid // chans
    orders = coupling.shape[2]
    tiles = (2 * chans, per, rows, width)
    whole = (2, chans * per, rows, width)
    ints, order, mates, choice, choice_next = deal(partner, extent, per, rows, width)
    scalars = (ints, couple.T, coupling.transpose(0, 2, 1))
    buffers = [
        ((per, grid, width), jnp.float32),
        ((per, grid, width), jnp.float32),
        ((per, width, grid), jnp.float32),
        ((per, strips, rows, width), jnp.float32),
        ((grid, grid), jnp.bfloat16),
        ((grid, grid), jnp.bfloat16),
        ((grid, width), jnp.bfloat16),
        ((grid, width), jnp.bfloat16),
    ]
    one = (per,)
    ring = (per, strips)
    plane = (per, 2 * chans)
    sorted_field = sort_field(order, wave_field).reshape(2 * per, rows, grid)

    def first_call(n):
        def call(x):
            return exchange(
                functools.partial(first_kernel, FIRST_LEVELS[n]),
                n,
                [tiles, tiles, tiles],
                buffers,
                [ring, ring, one, (2 * chans,), (2 * chans,), (2,), (chans,)]
                + [one, ring, ring, plane, plane, one, plane, plane, (per, 2)],
                x,
                radial_op,
            )

        return call

    def second_call(n):
        def call(mates, v):
            return exchange(
                functools.partial(second_kernel, SECOND_LEVELS[n]),
                len(FIRST_LEVELS) + n,
                [tiles, tiles],
                buffers + [((per, rows, grid), jnp.float32)],
                [plane, plane, ring, ring, one, (chans,)]
                + [one, ring, ring, one, one, plane, plane, (per, 2)],
                mates,
                v,
                radial_op,
            )

        return call

    field, mirror, direct = lax.switch(
        choice[0], [first_call(n) for n in range(len(FIRST_LEVELS))], sorted_field
    )
    field = field.reshape(whole)
    first_step, dealt = couple_tiles(
        grid, scalars, orders, False, (field, direct.reshape(whole), mirror.reshape(whole))
    )
    _, radial = lax.switch(
        choice_next[0],
        [second_call(n) for n in range(len(SECOND_LEVELS))],
        mates,
        dealt.reshape(tiles),
    )
    second_step = couple_tiles(
        grid, scalars, orders, True, (first_step, radial.reshape(whole), field)
    )[0]
    return (first_step, second_step)


def dispatch(wave_field, *rest):
    chans = lax.axis_size("chan")
    strips = lax.axis_size("strip")
    per, rows, grid = wave_field.shape[1:]
    width = grid // chans
    aligned = width % 128 == 0 and rows % 64 == 0 and grid % 64 == 0
    if chans == 4 and strips == 8 and per == 4 and aligned:
        return local(wave_field, *rest)
    return general(wave_field, *rest)


def solution(mesh):
    placed = (P(None, "chan", "strip", None), P(), P(), P(), P(), P())
    return jax.shard_map(
        dispatch,
        mesh=mesh,
        in_specs=placed,
        out_specs=(P(None, None, "strip", "chan"), P(None, None, "strip", "chan")),
        check_vma=False,
    )
```

```python
import functools

import jax
import jax.numpy as jnp
from jax import lax
from jax.experimental import pallas as pl
from jax.experimental.pallas import tpu as pltpu
from jax.sharding import PartitionSpec as P


def potentials(row_pos, col_pos, count, orders):
    spacing = 8.0 / count
    first = row_pos.astype(jnp.float32) * spacing
    second = col_pos.astype(jnp.float32) * spacing
    lesser = jnp.minimum(first[:, None], second[None, :])
    greater = jnp.maximum(first[:, None], second[None, :])
    root = jnp.sqrt(greater * greater + 1.0)
    result = []
    for order in range(orders):
        result.append(lesser**order / root ** (order + 1))
    return result


def couple_terms(field, image_rows, mirrored, coupling, couple, partner, pots, live):
    total = image_rows + jnp.take(mirrored, partner, axis=1)
    real_part = total[0]
    imag_part = total[1]
    for order in range(len(pots)):
        source = jnp.take(field, couple[:, order], axis=1)
        c_real = coupling[0, :, order][:, None, None]
        c_imag = coupling[1, :, order][:, None, None]
        real_part = real_part + pots[order] * (c_real * source[0] - c_imag * source[1])
        imag_part = imag_part + pots[order] * (c_real * source[1] + c_imag * source[0])
    return jnp.where(live[None], jnp.stack([real_part, imag_part]), 0.0)


def radial_product(radial_op, block):
    return jnp.einsum("ak,pckb->pcab", radial_op, block, precision=lax.Precision.HIGHEST)


def spread_columns(field):
    strips = lax.axis_size("strip")
    local_chans = field.shape[1]
    local_rows = field.shape[2]
    grid = field.shape[3]
    piece = grid // (strips * strips)
    shaped = field.reshape(2, local_chans, local_rows, strips, strips, piece)
    return jnp.transpose(shaped, (0, 1, 2, 4, 3, 5)).reshape(2, local_chans, local_rows, grid)


def spread_tiles(image):
    chans = lax.axis_size("chan")
    strips = lax.axis_size("strip")
    local_chans = image.shape[1]
    grid = image.shape[2]
    width = image.shape[3]
    piece = grid // (strips * strips)
    ratio = strips // chans
    block = grid // chans
    direct_send = image.reshape(2, local_chans, strips, width, chans, ratio * piece)
    direct_send = jnp.transpose(direct_send, (0, 1, 4, 2, 3, 5)).reshape(
        2, local_chans, chans * strips, width, ratio * piece
    )
    mirror_send = image.reshape(2, local_chans, chans, block, strips, piece)
    mirror_send = jnp.transpose(mirror_send, (0, 1, 2, 4, 3, 5)).reshape(
        2, local_chans, chans * strips, block, piece
    )
    direct_got, mirror_got = (
        lax.all_to_all(direct_send, ("chan", "strip"), split_axis=2, concat_axis=2, tiled=True),
        lax.all_to_all(mirror_send, ("chan", "strip"), split_axis=2, concat_axis=2, tiled=True),
    )
    direct_got = direct_got.reshape(2, local_chans, chans, strips, width, ratio, piece)
    direct_tiles = jnp.transpose(direct_got, (0, 2, 1, 4, 5, 3, 6)).reshape(
        2, chans * local_chans, width, block
    )
    mirror_got = mirror_got.reshape(2, local_chans, chans, strips, block, piece)
    mirror_tiles = jnp.transpose(mirror_got, (0, 2, 1, 3, 5, 4)).reshape(
        2, chans * local_chans, width, block
    )
    return (direct_tiles, mirror_tiles)


def general(wave_field, radial_op, coupling, couple, partner, extent):
    chans = lax.axis_size("chan")
    grid = wave_field.shape[3]
    strip_rows = wave_field.shape[2]
    chan_cols = grid // chans
    row_pos = lax.axis_index("strip") * strip_rows + jnp.arange(strip_rows)
    col_pos = lax.axis_index("chan") * chan_cols + jnp.arange(chan_cols)
    pots = potentials(row_pos, col_pos, grid, coupling.shape[2])
    live = (row_pos[None, :, None] < extent[:, None, None]) & (
        col_pos[None, None, :] < extent[:, None, None]
    )

    def radial(block):
        return radial_product(radial_op, block)

    def product_columns(field_rows):
        return radial(lax.all_to_all(field_rows, "strip", split_axis=3, concat_axis=2, tiled=True))

    field_tiles = lax.all_to_all(wave_field, "chan", split_axis=3, concat_axis=1, tiled=True)
    rows_tiles, mirror_tiles = spread_tiles(product_columns(spread_columns(wave_field)))
    first_step = couple_terms(
        field_tiles, rows_tiles, mirror_tiles, coupling, couple, partner, pots, live
    )
    image = product_columns(
        spread_columns(lax.all_to_all(first_step, "chan", split_axis=1, concat_axis=3, tiled=True))
    )
    rows_tiles, mirror_tiles = spread_tiles(image)
    applied = couple_terms(
        first_step, rows_tiles, mirror_tiles, coupling, couple, partner, pots, live
    )
    second_step = 2.0 * applied - field_tiles
    return (first_step, second_step)


MESH = pl.DeviceIdType.MESH
ANY = pl.BlockSpec(memory_space=pl.ANY)
SMEM = pl.BlockSpec(memory_space=pltpu.SMEM)


def rem(value, count):
    return lax.rem(value, count)


def greet(others):
    barrier = pltpu.get_barrier_semaphore()
    for other in others:
        pl.semaphore_signal(barrier, inc=1, device_id=other, device_id_type=MESH)
    pl.semaphore_wait(barrier, len(others))


def remote(source, target, send, recv, device):
    return pltpu.make_async_remote_copy(
        src_ref=source,
        dst_ref=target,
        send_sem=send,
        recv_sem=recv,
        device_id=device,
        device_id_type=MESH,
    )


def columns(block, width):
    return pl.ds(pl.multiple_of(block * width, 128), width)


def lines(block, height):
    return pl.ds(pl.multiple_of(block * height, 8), height)


def each(count, body):
    def one(n, carry):
        body(n)
        return carry

    lax.fori_loop(0, count, one, 0)


def far_first(n, strips):
    return strips // 2 + ((n + 1) // 2) * (2 * rem(n + 1, 2) - 1)


def by_distance(n, group):
    half = group // 2
    near = jnp.where(n < 2, group, group + 1 - 2 * rem(group, 2))
    m = rem(n, 2)
    far = jnp.where(half == 0, 2 + m, 1 - m)
    return jnp.where(n < 4, near * 2 + m, far * 2 + (n - 4) // 2)


def pick(j, values):
    chosen = jnp.int32(values[-1])
    for i, value in enumerate(values[:-1]):
        chosen = jnp.where(j == i, jnp.int32(value), chosen)
    return chosen


class Reach:
    def __init__(self, levels, rows, width):
        self.unit = width // 128
        self.width = width
        self.levels = levels
        self.lanes = [-(-level * rows // 128) for level in levels]
        self.parts = sorted({n % self.unit for n in self.lanes} - {0})

    def rows(self, j, strip):
        return strip < pick(j, self.levels)

    def blocks(self, j):
        return pick(j, [-(-n // self.unit) for n in self.lanes])

    def spans(self, j, block, alive, act):
        full = pick(j, [n // self.unit for n in self.lanes])
        rest = pick(j, [n % self.unit for n in self.lanes])

        @pl.when(jnp.logical_and(alive, block < full))
        def _():
            act(self.width)

        for part in self.parts:

            @pl.when(jnp.logical_and(alive, jnp.logical_and(block == full, rest == part)))
            def _():
                act(part * 128)

    def columns_alive(self, j, block):
        return pick(j, self.lanes) * 128 - block * self.width


def split(read, high, low, count, step):
    def one(n, carry):
        start = pl.multiple_of(n * step, step)
        at = pl.ds(start, step)
        value = read(start, at)
        top = value.astype(jnp.bfloat16)
        high[at, :] = top
        low[at, :] = (value - top.astype(jnp.float32)).astype(jnp.bfloat16)
        return carry

    lax.fori_loop(0, count // step, one, 0)


def load_operator(radial, turned, sems):
    per, width, grid = turned.shape
    return [
        pltpu.make_async_copy(radial.at[pl.ds(n * width, width), :], turned.at[n], sems.at[n])
        for n in range(grid // width)
    ]


def split_operator(loads, turned, rh, rl):
    width = turned.shape[1]
    for n, load in enumerate(loads):
        load.wait()
        at = pl.ds(n * width, width)
        split(lambda _, at, n=n: turned[n, at, :], rh.at[at, :], rl.at[at, :], width, 32)


def product(j, y, img, turned, rh, rl, yh, yl, depth, lanes, blocks):
    grid, width = y.shape[1:]
    step = 64

    def read(start, at):
        row = start + lax.broadcasted_iota(jnp.int32, (step, width), 0)
        col = lax.broadcasted_iota(jnp.int32, (step, width), 1)
        return jnp.where(jnp.logical_and(row < depth, col < lanes), y[j, at, :], 0.0)

    split(read, yh, yl, grid, step)

    def one(n):
        at = pl.ds(pl.multiple_of(n * 128, 128), 128)
        top = rh[at, :]
        total = jnp.dot(top, yh[...], preferred_element_type=jnp.float32)
        total = total + jnp.dot(top, yl[...], preferred_element_type=jnp.float32)
        total = total + jnp.dot(rl[at, :], yh[...], preferred_element_type=jnp.float32)
        img[j, at, :] = total
        turned[j, :, at] = total.T

    each(blocks * (width // 128), one)


FIRST_ORDER = (3, 2, 0, 1)
ORDER = (0, 2, 3, 1)


def first_kernel(
    levels, chans, strips, x, radial, f, mt, dd, y, img, turned, w, rh, rl, yh, yl,
    gs, gr, gl, cs, cr, cl, rs, ks, zs, zr, ms, mr, ml, fs, fr, ls,
):
    c = lax.axis_index("chan")
    s = lax.axis_index("strip")
    per, grid, width = y.shape
    rows = x.shape[1]
    group = s // 2
    member = rem(s, 2)
    reach = Reach(levels, rows, width)
    ring = [(c, rem(s + d, strips)) for d in range(1, strips)]
    plane = [(rem(c + r, chans), group * 2 + m) for r in range(1, chans) for m in range(2)]
    greet(ring + plane)

    def gather(j, d):
        t = rem(s + d, strips)
        return remote(
            x.at[rem(t, 2) * per + j, :, columns(t // 2, width)],
            y.at[j, lines(s, rows), :],
            gs.at[j, d],
            gr.at[j, d],
            (c, t),
        )

    def keep(j):
        return pltpu.make_async_copy(
            x.at[member * per + j, :, columns(group, width)], y.at[j, lines(s, rows), :], gl.at[j]
        )

    def field(p, r):
        to = rem(c + r, chans)
        part = x.at[pl.ds(p * per, per), :, columns(to, width)]
        target = f.at[p * chans + c]
        return remote(part, target, cs.at[r * 2 + p], cr.at[r * 2 + p], (to, s))

    def own_field(p):
        part = x.at[pl.ds(p * per, per), :, columns(c, width)]
        return pltpu.make_async_copy(part, f.at[p * chans + c], cl.at[p])

    def hop(j, d, lanes):
        t = rem(s + d, strips)
        return remote(
            img.at[j, lines(t, rows), pl.ds(0, lanes)],
            w.at[j, s, :, pl.ds(0, lanes)],
            zs.at[j, d],
            zr.at[j, d],
            (c, t),
        )

    def own_hop(j):
        return pltpu.make_async_copy(img.at[j, lines(s, rows), :], w.at[j, s], ks.at[j])

    def mirror(j, k):
        to = rem(c + k // 2, chans)
        m = rem(member + rem(k, 2), 2)
        part = turned.at[j, lines(m, rows), columns(to, width)]
        target = mt.at[member * chans + c, j]
        return remote(part, target, ms.at[j, k], mr.at[j, k], (to, group * 2 + m))

    def own_mirror(j):
        part = turned.at[j, lines(member, rows), columns(c, width)]
        return pltpu.make_async_copy(part, mt.at[member * chans + c, j], ml.at[j])

    def forward(j, u):
        to = u // 2
        p = rem(u, 2)
        away = rem(to - c + chans, chans)

        def act(lanes):
            part = w.at[j, u, :, pl.ds(0, lanes)]
            target = dd.at[p * chans + c, j, :, pl.ds(0, lanes)]

            @pl.when(away == 0)
            def _():
                pltpu.make_async_copy(part, target, ls.at[j, p]).start()

            @pl.when(away != 0)
            def _():
                k = away * 2 + p
                remote(part, target, fs.at[j, k], fr.at[j, k], (to, s)).start()

        reach.spans(j, to, reach.rows(j, s), act)

    def begin(j):
        each(strips - 1, lambda n: gather(j, far_first(n, strips)).start())
        keep(j).start()

    loads = load_operator(radial, turned, rs)
    each(2, lambda i: begin(pick(i, FIRST_ORDER)))
    for load in loads:
        load.start()
    each(2 * chans - 2, lambda n: field(rem(n, 2), 1 + n // 2).start())
    each(2, lambda p: own_field(p).start())
    split_operator(loads, turned, rh, rl)

    def launch(j):
        def one(n):
            d = far_first(n, strips)
            alive = reach.rows(j, rem(s + d, strips))
            reach.spans(j, group, alive, lambda lanes: hop(j, d, lanes).start())

        each(strips - 1, one)
        own_hop(j).start()

    def relay(i):
        j = pick(i, FIRST_ORDER)
        own_hop(j).wait()

        def one(n):
            u = by_distance(n, group)
            d = rem(s - u + strips, strips)
            alive = jnp.logical_and(reach.rows(j, s), u != s)
            reach.spans(j, u // 2, alive, lambda lanes: hop(j, d, lanes).wait_recv())
            forward(j, u)

        each(strips, one)

    def work(i):
        j = pick(i, FIRST_ORDER)
        keep(j).wait()
        each(strips - 1, lambda n: gather(j, n + 1).wait_recv())
        product(j, y, img, turned, rh, rl, yh, yl, grid, width, chans)
        each(2 * chans - 1, lambda n: mirror(j, n + 1).start())
        own_mirror(j).start()

        @pl.when(i < per - 2)
        def _():
            begin(pick(i + 2, FIRST_ORDER))

        launch(j)

        @pl.when(i == 2)
        def _():
            relay(0)

    def finish(j):
        def sent(n):
            d = n + 1
            gather(j, d).wait_send()
            alive = reach.rows(j, rem(s + d, strips))
            reach.spans(j, group, alive, lambda lanes: hop(j, d, lanes).wait_send())
            mirror(j, d).wait()

        each(strips - 1, sent)
        own_mirror(j).wait()
        here = reach.rows(j, s)

        def passed(k, lanes):
            part = w.at[j, 0, :, pl.ds(0, lanes)]
            target = dd.at[rem(k, 2) * chans + c, j, :, pl.ds(0, lanes)]
            return remote(part, target, fs.at[j, k], fr.at[j, k], (rem(c + k // 2, chans), s))

        def one(n):
            k = n + 2
            to = rem(c + k // 2, chans)
            reach.spans(j, to, here, lambda lanes: passed(k, lanes).wait_send())
            reach.spans(j, c, here, lambda lanes: passed(k, lanes).wait_recv())

        def own(p):
            def act(lanes):
                part = w.at[j, 0, :, pl.ds(0, lanes)]
                target = dd.at[p * chans + c, j, :, pl.ds(0, lanes)]
                pltpu.make_async_copy(part, target, ls.at[j, p]).wait()

            reach.spans(j, c, here, act)

        each(2, own)
        each(2 * chans - 2, one)

    each(per, work)
    each(per - 1, lambda i: relay(i + 1))
    each(2 * chans - 2, lambda n: field(rem(n, 2), 1 + n // 2).wait())
    each(2, lambda p: own_field(p).wait())
    each(per, finish)


def second_kernel(
    levels, chans, strips, mates, v, radial, b, sd, y, img, turned, w, rh, rl, yh, yl, sib,
    bs, br, gs, gr, gl, rs, ks, zs, zr, ms, mr, fs, fr, ls,
):
    c = lax.axis_index("chan")
    s = lax.axis_index("strip")
    per, grid, width = y.shape
    rows = v.shape[2]
    group = s // 2
    member = rem(s, 2)
    reach = Reach(levels, rows, width)
    ring = [(c, rem(s + d, strips)) for d in range(1, strips)]
    plane = [(rem(c + r, chans), s) for r in range(1, chans)]
    twin = (c, group * 2 + 1 - member)
    greet(ring + plane)

    def back(j, k, lanes):
        to = rem(c + k // 2, chans)
        p = rem(k, 2)
        return remote(
            v.at[p * chans + to, j, :, pl.ds(0, lanes)],
            b.at[p * chans + c, j, :, pl.ds(0, lanes)],
            bs.at[j, k],
            br.at[j, k],
            (to, s),
        )

    def arrive(j, d, u, lanes):
        return remote(
            v.at[0, 0, :, pl.ds(0, lanes)],
            y.at[j, lines(u, rows), pl.ds(0, lanes)],
            gs.at[j, d],
            gr.at[j, d],
            (c, rem(s + d, strips)),
        )

    def forward(source, j, block, p):
        t = block * 2 + p
        away = rem(t - s + strips, strips)

        def act(lanes):
            part = source.at[:, pl.ds(0, lanes)]
            target = y.at[j, lines(s, rows), pl.ds(0, lanes)]

            @pl.when(away == 0)
            def _():
                pltpu.make_async_copy(part, target, gl.at[j]).start()

            @pl.when(away != 0)
            def _():
                remote(part, target, gs.at[j, away], gr.at[j, away], (c, t)).start()

        reach.spans(j, block, reach.rows(j, s), act)

    def begin(j):
        def one(n):
            k = 2 * chans - 1 - n
            reach.spans(j, c, reach.rows(j, s), lambda lanes: back(j, k, lanes).start())

        each(2 * chans - 2, one)

    def pass_on(j):
        each(2, lambda p: forward(v.at[p * chans + c, j], j, c, p))

        def one(n):
            k = 2 * chans - 1 - n
            p = rem(k, 2)
            sender = rem(c - k // 2 + chans, chans)
            here = reach.rows(j, s)
            reach.spans(j, sender, here, lambda lanes: back(j, k, lanes).wait_recv())
            forward(b.at[p * chans + sender, j], j, sender, p)

        each(2 * chans - 2, one)

    def hop(j, d, lanes):
        t = rem(s + d, strips)
        return remote(
            img.at[j, lines(t, rows), pl.ds(0, lanes)],
            w.at[j, s, :, pl.ds(0, lanes)],
            zs.at[j, d],
            zr.at[j, d],
            (c, t),
        )

    def own_hop(j):
        return pltpu.make_async_copy(img.at[j, lines(s, rows), :], w.at[j, s], ks.at[j])

    def mirror(j):
        part = turned.at[j, lines(1 - member, rows), :]
        return remote(part, sib.at[j], ms.at[j], mr.at[j], twin)

    def busy(j):
        return group < reach.blocks(j)

    def combine(j, u):
        block = u // 2
        other = mates[j]
        mirrored = group < reach.blocks(other)
        alive = jnp.logical_and(reach.rows(j, s), block < reach.blocks(j))
        own = rem(u, 2) == member
        at = columns(block, width)

        def add(read):
            def one(n):
                line = pl.ds(pl.multiple_of(n * 32, 32), 32)
                w[j, u, line, :] = w[j, u, line, :] + jnp.where(mirrored, read(n), 0.0)

            each(rows // 32, one)

        @pl.when(jnp.logical_and(alive, own))
        def _():
            add(
                lambda n: turned[
                    other, pl.ds(pl.multiple_of(member * rows + n * 32, 32), 32), at
                ]
            )

        @pl.when(jnp.logical_and(alive, jnp.logical_not(own)))
        def _():
            add(lambda n: sib[other, pl.ds(pl.multiple_of(n * 32, 32), 32), at])

    def send(j, u):
        to = u // 2
        p = rem(u, 2)
        away = rem(to - c + chans, chans)

        def act(lanes):
            part = w.at[j, u, :, pl.ds(0, lanes)]
            target = sd.at[p * chans + c, j, :, pl.ds(0, lanes)]

            @pl.when(away == 0)
            def _():
                pltpu.make_async_copy(part, target, ls.at[j, p]).start()

            @pl.when(away != 0)
            def _():
                k = away * 2 + p
                remote(part, target, fs.at[j, k], fr.at[j, k], (to, s)).start()

        reach.spans(j, to, reach.rows(j, s), act)

    loads = load_operator(radial, turned, rs)
    each(per, begin)
    for load in loads:
        load.start()
    each(per, pass_on)
    split_operator(loads, turned, rh, rl)

    def launch(j):
        def one(n):
            d = far_first(n, strips)
            alive = reach.rows(j, rem(s + d, strips))
            reach.spans(j, group, alive, lambda lanes: hop(j, d, lanes).start())

        each(strips - 1, one)

    def work(j):
        depth = pick(j, levels) * rows

        def kept(lanes):
            target = y.at[j, lines(s, rows), pl.ds(0, lanes)]
            pltpu.make_async_copy(v.at[0, 0, :, pl.ds(0, lanes)], target, gl.at[j]).wait()

        reach.spans(j, group, reach.rows(j, s), kept)

        def arrived(n):
            d = n + 1
            u = rem(s - d + strips, strips)
            alive = reach.rows(j, u)
            reach.spans(j, group, alive, lambda lanes: arrive(j, d, u, lanes).wait_recv())

        each(strips - 1, arrived)

        @pl.when(busy(j))
        def _():
            lanes = reach.columns_alive(j, group)
            product(j, y, img, turned, rh, rl, yh, yl, depth, lanes, chans)
            mirror(j).start()
            own_hop(j).start()

        @pl.when(j == ORDER[0])
        def _():
            launch(j)

    def hear(j):
        @pl.when(busy(j))
        def _():
            mirror(j).wait_recv()
            own_hop(j).wait()

    def relay(i):
        j = pick(i, ORDER)

        def one(n):
            u = by_distance(n, group)
            d = rem(s - u + strips, strips)
            alive = jnp.logical_and(reach.rows(j, s), u != s)
            reach.spans(j, u // 2, alive, lambda lanes: hop(j, d, lanes).wait_recv())
            combine(j, u)
            send(j, u)

        each(strips, one)

    def finish(j):
        here = reach.rows(j, s)

        def sent(n):
            d = n + 1
            t = rem(s + d, strips)
            reach.spans(j, t // 2, here, lambda lanes: arrive(j, d, s, lanes).wait_send())
            alive = reach.rows(j, t)
            reach.spans(j, group, alive, lambda lanes: hop(j, d, lanes).wait_send())

        each(strips - 1, sent)

        @pl.when(busy(j))
        def _():
            mirror(j).wait_send()

        def passed(k, lanes):
            part = w.at[j, 0, :, pl.ds(0, lanes)]
            target = sd.at[rem(k, 2) * chans + c, j, :, pl.ds(0, lanes)]
            return remote(part, target, fs.at[j, k], fr.at[j, k], (rem(c + k // 2, chans), s))

        def one(n):
            k = n + 2
            to = rem(c + k // 2, chans)
            reach.spans(j, c, here, lambda lanes: back(j, k, lanes).wait_send())
            reach.spans(j, to, here, lambda lanes: passed(k, lanes).wait_send())
            reach.spans(j, c, here, lambda lanes: passed(k, lanes).wait_recv())

        def own(p):
            def act(lanes):
                part = w.at[j, 0, :, pl.ds(0, lanes)]
                target = sd.at[p * chans + c, j, :, pl.ds(0, lanes)]
                pltpu.make_async_copy(part, target, ls.at[j, p]).wait()

            reach.spans(j, c, here, act)

        each(2, own)
        each(2 * chans - 2, one)

    def step(i):
        @pl.when(i < per - 1)
        def _():
            launch(pick(i + 1, ORDER))

        relay(i)

    each(per, work)
    each(per, hear)
    each(per, step)
    each(per, finish)


def exchange(kernel, ident, outs, buffers, sems, *operands):
    chans = lax.axis_size("chan")
    strips = lax.axis_size("strip")
    return pl.pallas_call(
        functools.partial(kernel, chans, strips),
        out_shape=[jax.ShapeDtypeStruct(shape, jnp.float32) for shape in outs],
        in_specs=[SMEM] * (len(operands) - 2) + [ANY] * 2,
        out_specs=[ANY] * len(outs),
        scratch_shapes=[pltpu.VMEM(*buffer) for buffer in buffers]
        + [pltpu.SemaphoreType.DMA(n) for n in sems],
        compiler_params=pltpu.CompilerParams(
            collective_id=ident, has_side_effects=True, vmem_limit_bytes=62 * 2**20
        ),
    )(*operands)


def couple_kernel(count, last, ints, links, reals, *refs):
    if last:
        field, radial, base, out, pots = refs
    else:
        field, direct, mirror, out, dealt, pots = refs
    channels, height, width = field.shape[1:]
    orders = pots.shape[0]
    partners, extents, firsts, seconds = [2 + n * channels for n in range(4)]
    spacing = 8.0 / count
    row = ints[0] + pl.program_id(0) * height
    row = row + lax.broadcasted_iota(jnp.int32, (height, width), 0)
    col = ints[1] + lax.broadcasted_iota(jnp.int32, (height, width), 1)
    first = row.astype(jnp.float32) * spacing
    second = col.astype(jnp.float32) * spacing
    greater = jnp.maximum(first, second)
    root = jnp.sqrt(greater * greater + 1.0)
    ratio = jnp.minimum(first, second) / root
    pot = 1.0 / root
    for order in range(orders):
        pots[order] = pot
        pot = pot * ratio
    reach = jnp.maximum(row, col)

    def channel(c, carry):
        mine = ints[firsts + c]
        dealt_at = ints[seconds + c]
        if last:
            real_part = radial[0, dealt_at]
            imag_part = radial[1, dealt_at]
        else:
            other = ints[firsts + ints[partners + c]]
            real_part = direct[0, mine] + mirror[0, other]
            imag_part = direct[1, mine] + mirror[1, other]
        for order in range(orders):
            k = links[order, c]
            if not last:
                k = ints[firsts + k]
            c_real = reals[0, order, c]
            c_imag = reals[1, order, c]
            pot = pots[order]
            s_real = pot * field[0, k]
            s_imag = pot * field[1, k]
            real_part = real_part + (c_real * s_real - c_imag * s_imag)
            imag_part = imag_part + (c_real * s_imag + c_imag * s_real)
        live = reach < ints[extents + c]
        real_part = jnp.where(live, real_part, 0.0)
        imag_part = jnp.where(live, imag_part, 0.0)
        if last:
            real_part = 2.0 * real_part - base[0, mine]
            imag_part = 2.0 * imag_part - base[1, mine]
        else:
            dealt[0, dealt_at] = real_part
            dealt[1, dealt_at] = imag_part
        out[0, c] = real_part
        out[1, c] = imag_part
        return carry

    lax.fori_loop(0, channels, channel, 0)


def couple_tiles(count, scalars, orders, last, arrays):
    shape = arrays[0].shape
    height = 32
    block = pl.BlockSpec((2, shape[1], height, shape[3]), lambda n: (0, 0, n, 0))
    outs = 1 if last else 2
    return pl.pallas_call(
        functools.partial(couple_kernel, count, last),
        grid=(shape[2] // height,),
        out_shape=[jax.ShapeDtypeStruct(shape, jnp.float32)] * outs,
        in_specs=[SMEM] * len(scalars) + [block] * len(arrays),
        out_specs=[block] * outs,
        scratch_shapes=[pltpu.VMEM((orders, height, shape[3]), jnp.float32)],
    )(*scalars, *arrays)


FIRST_LEVELS = ((8, 6, 5, 4), (8, 7, 5, 4), (8, 8, 6, 4), (8, 8, 7, 4), (8, 8, 6, 5), (8, 8, 8, 4), (8, 8, 7, 6), (8, 8, 8, 8))
SECOND_LEVELS = ((8, 6, 4, 4), (8, 6, 5, 4), (8, 8, 4, 4), (8, 7, 5, 4), (8, 8, 6, 4), (8, 8, 6, 5), (8, 8, 7, 5), (8, 8, 8, 8))


def deal_kernel(
    per, rows, width, partner, extent, ints, order, mates, choice, choice_next,
    far, keys, lines_of, places,
):
    channels = extent.shape[0]
    chans = channels // per
    c = lax.axis_index("chan")
    ints[0] = lax.axis_index("strip") * rows
    ints[1] = c * width
    for n in range(2 * per):
        far[n] = 0

    def head(i):
        return jnp.minimum(i, partner[i])

    def key(i):
        keys[i] = jnp.where(i < partner[i], extent[i] + extent[partner[i]], -1)

    def before(k, i):
        tie = jnp.logical_and(extent[k] == extent[i], k < i)
        return jnp.logical_or(extent[k] > extent[i], tie)

    def first(i):
        line = i // per
        place = jnp.int32(0)
        for n in range(per):
            place = place + jnp.where(before(line * per + n, i), 1, 0)
        ints[2 + 2 * channels + i] = line * per + place
        far[place] = jnp.maximum(far[place], extent[i])

        @pl.when(line == c)
        def _():
            order[place] = i - line * per

        mine = keys[head(i)]
        rank = jnp.int32(0)
        for k in range(channels):
            tie = jnp.logical_and(keys[k] == mine, k < head(i))
            rank = rank + jnp.where(jnp.logical_or(keys[k] > mine, tie), 1, 0)
        lines_of[i] = jnp.where(rank < chans, rank, 2 * chans - 1 - rank)

    def second(i):
        line = lines_of[i]
        place = jnp.int32(0)
        for k in range(channels):
            ahead = jnp.logical_and(lines_of[k] == line, before(k, i))
            place = place + jnp.where(ahead, 1, 0)
        places[i] = place
        ints[2 + i] = partner[i]
        ints[2 + channels + i] = extent[i]
        ints[2 + 3 * channels + i] = line * per + place
        far[per + place] = jnp.maximum(far[per + place], extent[i])

    def match(i):
        @pl.when(lines_of[i] == c)
        def _():
            mates[places[i]] = places[partner[i]]

    each(channels, key)
    each(channels, first)
    each(channels, second)
    each(channels, match)
    for n, (table, out) in enumerate(((FIRST_LEVELS, choice), (SECOND_LEVELS, choice_next))):
        best = jnp.int32(len(table) - 1)
        for v in reversed(range(len(table) - 1)):
            fits = far[n * per] <= table[v][0] * rows
            for j in range(1, per):
                fits = jnp.logical_and(fits, far[n * per + j] <= table[v][j] * rows)
            best = jnp.where(fits, jnp.int32(v), best)
        out[0] = best


def deal(partner, extent, per, rows, width):
    channels = extent.shape[0]
    sizes = (2 + 4 * channels, per, per, 1, 1)
    scratch = (2 * per, channels, channels, channels)
    return pl.pallas_call(
        functools.partial(deal_kernel, per, rows, width),
        out_shape=[jax.ShapeDtypeStruct((size,), jnp.int32) for size in sizes],
        in_specs=[SMEM] * 2,
        out_specs=[SMEM] * len(sizes),
        scratch_shapes=[pltpu.SMEM((size,), jnp.int32) for size in scratch],
    )(partner, extent)


def sort_kernel(order, x, out, held, loads, stores):
    parts, per = held.shape[:2]
    pieces = [(p, j) for j in range(per) for p in range(parts)]

    def load(p, j):
        return pltpu.make_async_copy(x.at[p, order[j]], held.at[p, j], loads.at[p, j])

    def store(p, j):
        return pltpu.make_async_copy(held.at[p, j], out.at[p, j], stores.at[p, j])

    for p, j in pieces:
        load(p, j).start()
    for p, j in pieces:
        load(p, j).wait()
        store(p, j).start()
    for p, j in pieces:
        store(p, j).wait()


def sort_field(order, x):
    parts, per = x.shape[:2]
    return pl.pallas_call(
        sort_kernel,
        out_shape=jax.ShapeDtypeStruct(x.shape, x.dtype),
        in_specs=[SMEM, ANY],
        out_specs=ANY,
        scratch_shapes=[
            pltpu.VMEM(x.shape, x.dtype),
            pltpu.SemaphoreType.DMA((parts, per)),
            pltpu.SemaphoreType.DMA((parts, per)),
        ],
    )(order, x)


def local(wave_field, radial_op, coupling, couple, partner, extent):
    chans = lax.axis_size("chan")
    strips = lax.axis_size("strip")
    per, rows, grid = wave_field.shape[1:]
    width = grid // chans
    orders = coupling.shape[2]
    tiles = (2 * chans, per, rows, width)
    whole = (2, chans * per, rows, width)
    ints, order, mates, choice, choice_next = deal(partner, extent, per, rows, width)
    scalars = (ints, couple.T, coupling.transpose(0, 2, 1))
    buffers = [
        ((per, grid, width), jnp.float32),
        ((per, grid, width), jnp.float32),
        ((per, width, grid), jnp.float32),
        ((per, strips, rows, width), jnp.float32),
        ((grid, grid), jnp.bfloat16),
        ((grid, grid), jnp.bfloat16),
        ((grid, width), jnp.bfloat16),
        ((grid, width), jnp.bfloat16),
    ]
    one = (per,)
    ring = (per, strips)
    plane = (per, 2 * chans)
    sorted_field = sort_field(order, wave_field).reshape(2 * per, rows, grid)

    def first_call(n):
        def call(x):
            return exchange(
                functools.partial(first_kernel, FIRST_LEVELS[n]),
                n,
                [tiles, tiles, tiles],
                buffers,
                [ring, ring, one, (2 * chans,), (2 * chans,), (2,), (chans,)]
                + [one, ring, ring, plane, plane, one, plane, plane, (per, 2)],
                x,
                radial_op,
            )

        return call

    def second_call(n):
        def call(mates, v):
            return exchange(
                functools.partial(second_kernel, SECOND_LEVELS[n]),
                len(FIRST_LEVELS) + n,
                [tiles, tiles],
                buffers + [((per, rows, grid), jnp.float32)],
                [plane, plane, ring, ring, one, (chans,)]
                + [one, ring, ring, one, one, plane, plane, (per, 2)],
                mates,
                v,
                radial_op,
            )

        return call

    field, mirror, direct = lax.switch(
        choice[0], [first_call(n) for n in range(len(FIRST_LEVELS))], sorted_field
    )
    field = field.reshape(whole)
    first_step, dealt = couple_tiles(
        grid, scalars, orders, False, (field, direct.reshape(whole), mirror.reshape(whole))
    )
    _, radial = lax.switch(
        choice_next[0],
        [second_call(n) for n in range(len(SECOND_LEVELS))],
        mates,
        dealt.reshape(tiles),
    )
    second_step = couple_tiles(
        grid, scalars, orders, True, (first_step, radial.reshape(whole), field)
    )[0]
    return (first_step, second_step)


def dispatch(wave_field, *rest):
    chans = lax.axis_size("chan")
    strips = lax.axis_size("strip")
    per, rows, grid = wave_field.shape[1:]
    width = grid // chans
    aligned = width % 128 == 0 and rows % 64 == 0 and grid % 64 == 0
    if chans == 4 and strips == 8 and per == 4 and aligned:
        return local(wave_field, *rest)
    return general(wave_field, *rest)


def solution(mesh):
    placed = (P(None, "chan", "strip", None), P(), P(), P(), P(), P())
    return jax.shard_map(
        dispatch,
        mesh=mesh,
        in_specs=placed,
        out_specs=(P(None, None, "strip", "chan"), P(None, None, "strip", "chan")),
        check_vma=False,
    )
```

```python
import functools

import jax
import jax.numpy as jnp
from jax import lax
from jax.experimental import pallas as pl
from jax.experimental.pallas import tpu as pltpu
from jax.sharding import PartitionSpec as P


def potentials(row_pos, col_pos, count, orders):
    spacing = 8.0 / count
    first = row_pos.astype(jnp.float32) * spacing
    second = col_pos.astype(jnp.float32) * spacing
    lesser = jnp.minimum(first[:, None], second[None, :])
    greater = jnp.maximum(first[:, None], second[None, :])
    root = jnp.sqrt(greater * greater + 1.0)
    result = []
    for order in range(orders):
        result.append(lesser**order / root ** (order + 1))
    return result


def couple_terms(field, image_rows, mirrored, coupling, couple, partner, pots, live):
    total = image_rows + jnp.take(mirrored, partner, axis=1)
    real_part = total[0]
    imag_part = total[1]
    for order in range(len(pots)):
        source = jnp.take(field, couple[:, order], axis=1)
        c_real = coupling[0, :, order][:, None, None]
        c_imag = coupling[1, :, order][:, None, None]
        real_part = real_part + pots[order] * (c_real * source[0] - c_imag * source[1])
        imag_part = imag_part + pots[order] * (c_real * source[1] + c_imag * source[0])
    return jnp.where(live[None], jnp.stack([real_part, imag_part]), 0.0)


def radial_product(radial_op, block):
    return jnp.einsum("ak,pckb->pcab", radial_op, block, precision=lax.Precision.HIGHEST)


def spread_columns(field):
    strips = lax.axis_size("strip")
    local_chans = field.shape[1]
    local_rows = field.shape[2]
    grid = field.shape[3]
    piece = grid // (strips * strips)
    shaped = field.reshape(2, local_chans, local_rows, strips, strips, piece)
    return jnp.transpose(shaped, (0, 1, 2, 4, 3, 5)).reshape(2, local_chans, local_rows, grid)


def spread_tiles(image):
    chans = lax.axis_size("chan")
    strips = lax.axis_size("strip")
    local_chans = image.shape[1]
    grid = image.shape[2]
    width = image.shape[3]
    piece = grid // (strips * strips)
    ratio = strips // chans
    block = grid // chans
    direct_send = image.reshape(2, local_chans, strips, width, chans, ratio * piece)
    direct_send = jnp.transpose(direct_send, (0, 1, 4, 2, 3, 5)).reshape(
        2, local_chans, chans * strips, width, ratio * piece
    )
    mirror_send = image.reshape(2, local_chans, chans, block, strips, piece)
    mirror_send = jnp.transpose(mirror_send, (0, 1, 2, 4, 3, 5)).reshape(
        2, local_chans, chans * strips, block, piece
    )
    direct_got, mirror_got = (
        lax.all_to_all(direct_send, ("chan", "strip"), split_axis=2, concat_axis=2, tiled=True),
        lax.all_to_all(mirror_send, ("chan", "strip"), split_axis=2, concat_axis=2, tiled=True),
    )
    direct_got = direct_got.reshape(2, local_chans, chans, strips, width, ratio, piece)
    direct_tiles = jnp.transpose(direct_got, (0, 2, 1, 4, 5, 3, 6)).reshape(
        2, chans * local_chans, width, block
    )
    mirror_got = mirror_got.reshape(2, local_chans, chans, strips, block, piece)
    mirror_tiles = jnp.transpose(mirror_got, (0, 2, 1, 3, 5, 4)).reshape(
        2, chans * local_chans, width, block
    )
    return (direct_tiles, mirror_tiles)


def general(wave_field, radial_op, coupling, couple, partner, extent):
    chans = lax.axis_size("chan")
    grid = wave_field.shape[3]
    strip_rows = wave_field.shape[2]
    chan_cols = grid // chans
    row_pos = lax.axis_index("strip") * strip_rows + jnp.arange(strip_rows)
    col_pos = lax.axis_index("chan") * chan_cols + jnp.arange(chan_cols)
    pots = potentials(row_pos, col_pos, grid, coupling.shape[2])
    live = (row_pos[None, :, None] < extent[:, None, None]) & (
        col_pos[None, None, :] < extent[:, None, None]
    )

    def radial(block):
        return radial_product(radial_op, block)

    def product_columns(field_rows):
        return radial(lax.all_to_all(field_rows, "strip", split_axis=3, concat_axis=2, tiled=True))

    field_tiles = lax.all_to_all(wave_field, "chan", split_axis=3, concat_axis=1, tiled=True)
    rows_tiles, mirror_tiles = spread_tiles(product_columns(spread_columns(wave_field)))
    first_step = couple_terms(
        field_tiles, rows_tiles, mirror_tiles, coupling, couple, partner, pots, live
    )
    image = product_columns(
        spread_columns(lax.all_to_all(first_step, "chan", split_axis=1, concat_axis=3, tiled=True))
    )
    rows_tiles, mirror_tiles = spread_tiles(image)
    applied = couple_terms(
        first_step, rows_tiles, mirror_tiles, coupling, couple, partner, pots, live
    )
    second_step = 2.0 * applied - field_tiles
    return (first_step, second_step)


MESH = pl.DeviceIdType.MESH
ANY = pl.BlockSpec(memory_space=pl.ANY)
SMEM = pl.BlockSpec(memory_space=pltpu.SMEM)


def rem(value, count):
    return lax.rem(value, count)


def greet(others):
    barrier = pltpu.get_barrier_semaphore()
    for other in others:
        pl.semaphore_signal(barrier, inc=1, device_id=other, device_id_type=MESH)
    pl.semaphore_wait(barrier, len(others))


def remote(source, target, send, recv, device):
    return pltpu.make_async_remote_copy(
        src_ref=source,
        dst_ref=target,
        send_sem=send,
        recv_sem=recv,
        device_id=device,
        device_id_type=MESH,
    )


def columns(block, width):
    return pl.ds(pl.multiple_of(block * width, 128), width)


def lines(block, height):
    return pl.ds(pl.multiple_of(block * height, 8), height)


def each(count, body):
    def one(n, carry):
        body(n)
        return carry

    lax.fori_loop(0, count, one, 0)


def far_first(n, strips):
    return strips // 2 + ((n + 1) // 2) * (2 * rem(n + 1, 2) - 1)


def by_distance(n, group):
    half = group // 2
    near = jnp.where(n < 2, group, group + 1 - 2 * rem(group, 2))
    m = rem(n, 2)
    far = jnp.where(half == 0, 2 + m, 1 - m)
    return jnp.where(n < 4, near * 2 + m, far * 2 + (n - 4) // 2)


def pick(j, values):
    chosen = jnp.int32(values[-1])
    for i, value in enumerate(values[:-1]):
        chosen = jnp.where(j == i, jnp.int32(value), chosen)
    return chosen


class Reach:
    def __init__(self, levels, rows, width):
        self.unit = width // 128
        self.width = width
        self.levels = levels
        self.lanes = [-(-level * rows // 128) for level in levels]
        self.parts = sorted({n % self.unit for n in self.lanes} - {0})

    def rows(self, j, strip):
        return strip < pick(j, self.levels)

    def blocks(self, j):
        return pick(j, [-(-n // self.unit) for n in self.lanes])

    def spans(self, j, block, alive, act):
        full = pick(j, [n // self.unit for n in self.lanes])
        rest = pick(j, [n % self.unit for n in self.lanes])

        @pl.when(jnp.logical_and(alive, block < full))
        def _():
            act(self.width)

        for part in self.parts:

            @pl.when(jnp.logical_and(alive, jnp.logical_and(block == full, rest == part)))
            def _():
                act(part * 128)

    def columns_alive(self, j, block):
        return pick(j, self.lanes) * 128 - block * self.width


def split(read, high, low, count, step):
    def one(n, carry):
        start = pl.multiple_of(n * step, step)
        at = pl.ds(start, step)
        value = read(start, at)
        top = value.astype(jnp.bfloat16)
        high[at, :] = top
        low[at, :] = (value - top.astype(jnp.float32)).astype(jnp.bfloat16)
        return carry

    lax.fori_loop(0, count // step, one, 0)


def load_operator(radial, turned, sems):
    per, width, grid = turned.shape
    return [
        pltpu.make_async_copy(radial.at[pl.ds(n * width, width), :], turned.at[n], sems.at[n])
        for n in range(grid // width)
    ]


def split_operator(loads, turned, rh, rl):
    width = turned.shape[1]
    for n, load in enumerate(loads):
        load.wait()
        at = pl.ds(n * width, width)
        split(lambda _, at, n=n: turned[n, at, :], rh.at[at, :], rl.at[at, :], width, 32)


def product(j, y, img, turned, rh, rl, yh, yl, depth, lanes, blocks):
    grid, width = y.shape[1:]
    step = 64

    def read(start, at):
        row = start + lax.broadcasted_iota(jnp.int32, (step, width), 0)
        col = lax.broadcasted_iota(jnp.int32, (step, width), 1)
        return jnp.where(jnp.logical_and(row < depth, col < lanes), y[j, at, :], 0.0)

    split(read, yh, yl, grid, step)

    def one(n):
        at = pl.ds(pl.multiple_of(n * 128, 128), 128)
        top = rh[at, :]
        total = jnp.dot(top, yh[...], preferred_element_type=jnp.float32)
        total = total + jnp.dot(top, yl[...], preferred_element_type=jnp.float32)
        total = total + jnp.dot(rl[at, :], yh[...], preferred_element_type=jnp.float32)
        img[j, at, :] = total
        turned[j, :, at] = total.T

    each(blocks * (width // 128), one)


FIRST_ORDER = (3, 2, 0, 1)
ORDER = (0, 2, 3, 1)


def first_kernel(
    levels, chans, strips, x, radial, f, mt, dd, y, img, turned, w, rh, rl, yh, yl,
    gs, gr, gl, cs, cr, cl, rs, ks, zs, zr, ms, mr, ml, fs, fr, ls,
):
    c = lax.axis_index("chan")
    s = lax.axis_index("strip")
    per, grid, width = y.shape
    rows = x.shape[1]
    group = s // 2
    member = rem(s, 2)
    reach = Reach(levels, rows, width)
    ring = [(c, rem(s + d, strips)) for d in range(1, strips)]
    plane = [(rem(c + r, chans), group * 2 + m) for r in range(1, chans) for m in range(2)]
    greet(ring + plane)

    def gather(j, d):
        t = rem(s + d, strips)
        return remote(
            x.at[rem(t, 2) * per + j, :, columns(t // 2, width)],
            y.at[j, lines(s, rows), :],
            gs.at[j, d],
            gr.at[j, d],
            (c, t),
        )

    def keep(j):
        return pltpu.make_async_copy(
            x.at[member * per + j, :, columns(group, width)], y.at[j, lines(s, rows), :], gl.at[j]
        )

    def field(p, r):
        to = rem(c + r, chans)
        part = x.at[pl.ds(p * per, per), :, columns(to, width)]
        target = f.at[p * chans + c]
        return remote(part, target, cs.at[r * 2 + p], cr.at[r * 2 + p], (to, s))

    def own_field(p):
        part = x.at[pl.ds(p * per, per), :, columns(c, width)]
        return pltpu.make_async_copy(part, f.at[p * chans + c], cl.at[p])

    def hop(j, d, lanes):
        t = rem(s + d, strips)
        return remote(
            img.at[j, lines(t, rows), pl.ds(0, lanes)],
            w.at[j, s, :, pl.ds(0, lanes)],
            zs.at[j, d],
            zr.at[j, d],
            (c, t),
        )

    def own_hop(j):
        return pltpu.make_async_copy(img.at[j, lines(s, rows), :], w.at[j, s], ks.at[j])

    def mirror(j, k):
        to = rem(c + k // 2, chans)
        m = rem(member + rem(k, 2), 2)
        part = turned.at[j, lines(m, rows), columns(to, width)]
        target = mt.at[member * chans + c, j]
        return remote(part, target, ms.at[j, k], mr.at[j, k], (to, group * 2 + m))

    def own_mirror(j):
        part = turned.at[j, lines(member, rows), columns(c, width)]
        return pltpu.make_async_copy(part, mt.at[member * chans + c, j], ml.at[j])

    def forward(j, u):
        to = u // 2
        p = rem(u, 2)
        away = rem(to - c + chans, chans)

        def act(lanes):
            part = w.at[j, u, :, pl.ds(0, lanes)]
            target = dd.at[p * chans + c, j, :, pl.ds(0, lanes)]

            @pl.when(away == 0)
            def _():
                pltpu.make_async_copy(part, target, ls.at[j, p]).start()

            @pl.when(away != 0)
            def _():
                k = away * 2 + p
                remote(part, target, fs.at[j, k], fr.at[j, k], (to, s)).start()

        reach.spans(j, to, reach.rows(j, s), act)

    def begin(j):
        each(strips - 1, lambda n: gather(j, far_first(n, strips)).start())
        keep(j).start()

    loads = load_operator(radial, turned, rs)
    each(2, lambda i: begin(pick(i, FIRST_ORDER)))
    for load in loads:
        load.start()
    each(2 * chans - 2, lambda n: field(rem(n, 2), 1 + n // 2).start())
    each(2, lambda p: own_field(p).start())
    split_operator(loads, turned, rh, rl)

    def launch(j):
        def one(n):
            d = far_first(n, strips)
            alive = reach.rows(j, rem(s + d, strips))
            reach.spans(j, group, alive, lambda lanes: hop(j, d, lanes).start())

        each(strips - 1, one)
        own_hop(j).start()

    def relay(i):
        j = pick(i, FIRST_ORDER)
        own_hop(j).wait()

        def one(n):
            u = by_distance(n, group)
            d = rem(s - u + strips, strips)
            alive = jnp.logical_and(reach.rows(j, s), u != s)
            reach.spans(j, u // 2, alive, lambda lanes: hop(j, d, lanes).wait_recv())
            forward(j, u)

        each(strips, one)

    def work(i):
        j = pick(i, FIRST_ORDER)
        keep(j).wait()
        each(strips - 1, lambda n: gather(j, n + 1).wait_recv())
        product(j, y, img, turned, rh, rl, yh, yl, grid, width, chans)
        each(2 * chans - 1, lambda n: mirror(j, n + 1).start())
        own_mirror(j).start()

        @pl.when(i < per - 2)
        def _():
            begin(pick(i + 2, FIRST_ORDER))

        launch(j)

        @pl.when(i == 2)
        def _():
            relay(0)

    def finish(j):
        def sent(n):
            d = n + 1
            gather(j, d).wait_send()
            alive = reach.rows(j, rem(s + d, strips))
            reach.spans(j, group, alive, lambda lanes: hop(j, d, lanes).wait_send())
            mirror(j, d).wait()

        each(strips - 1, sent)
        own_mirror(j).wait()
        here = reach.rows(j, s)

        def passed(k, lanes):
            part = w.at[j, 0, :, pl.ds(0, lanes)]
            target = dd.at[rem(k, 2) * chans + c, j, :, pl.ds(0, lanes)]
            return remote(part, target, fs.at[j, k], fr.at[j, k], (rem(c + k // 2, chans), s))

        def one(n):
            k = n + 2
            to = rem(c + k // 2, chans)
            reach.spans(j, to, here, lambda lanes: passed(k, lanes).wait_send())
            reach.spans(j, c, here, lambda lanes: passed(k, lanes).wait_recv())

        def own(p):
            def act(lanes):
                part = w.at[j, 0, :, pl.ds(0, lanes)]
                target = dd.at[p * chans + c, j, :, pl.ds(0, lanes)]
                pltpu.make_async_copy(part, target, ls.at[j, p]).wait()

            reach.spans(j, c, here, act)

        each(2, own)
        each(2 * chans - 2, one)

    each(per, work)
    each(per - 1, lambda i: relay(i + 1))
    each(2 * chans - 2, lambda n: field(rem(n, 2), 1 + n // 2).wait())
    each(2, lambda p: own_field(p).wait())
    each(per, finish)


def second_kernel(
    levels, chans, strips, mates, v, radial, b, sd, y, img, turned, w, rh, rl, yh, yl, sib,
    bs, br, gs, gr, gl, rs, ks, zs, zr, ms, mr, fs, fr, ls,
):
    c = lax.axis_index("chan")
    s = lax.axis_index("strip")
    per, grid, width = y.shape
    rows = v.shape[2]
    group = s // 2
    member = rem(s, 2)
    reach = Reach(levels, rows, width)
    ring = [(c, rem(s + d, strips)) for d in range(1, strips)]
    plane = [(rem(c + r, chans), s) for r in range(1, chans)]
    twin = (c, group * 2 + 1 - member)
    greet(ring + plane)

    def back(j, k, lanes):
        to = rem(c + k // 2, chans)
        p = rem(k, 2)
        return remote(
            v.at[p * chans + to, j, :, pl.ds(0, lanes)],
            b.at[p * chans + c, j, :, pl.ds(0, lanes)],
            bs.at[j, k],
            br.at[j, k],
            (to, s),
        )

    def arrive(j, d, u, lanes):
        return remote(
            v.at[0, 0, :, pl.ds(0, lanes)],
            y.at[j, lines(u, rows), pl.ds(0, lanes)],
            gs.at[j, d],
            gr.at[j, d],
            (c, rem(s + d, strips)),
        )

    def forward(source, j, block, p):
        t = block * 2 + p
        away = rem(t - s + strips, strips)

        def act(lanes):
            part = source.at[:, pl.ds(0, lanes)]
            target = y.at[j, lines(s, rows), pl.ds(0, lanes)]

            @pl.when(away == 0)
            def _():
                pltpu.make_async_copy(part, target, gl.at[j]).start()

            @pl.when(away != 0)
            def _():
                remote(part, target, gs.at[j, away], gr.at[j, away], (c, t)).start()

        reach.spans(j, block, reach.rows(j, s), act)

    def begin(j):
        def one(n):
            k = 2 * chans - 1 - n
            reach.spans(j, c, reach.rows(j, s), lambda lanes: back(j, k, lanes).start())

        each(2 * chans - 2, one)

    def pass_on(j):
        each(2, lambda p: forward(v.at[p * chans + c, j], j, c, p))

        def one(n):
            k = 2 * chans - 1 - n
            p = rem(k, 2)
            sender = rem(c - k // 2 + chans, chans)
            here = reach.rows(j, s)
            reach.spans(j, sender, here, lambda lanes: back(j, k, lanes).wait_recv())
            forward(b.at[p * chans + sender, j], j, sender, p)

        each(2 * chans - 2, one)

    def hop(j, d, lanes):
        t = rem(s + d, strips)
        return remote(
            img.at[j, lines(t, rows), pl.ds(0, lanes)],
            w.at[j, s, :, pl.ds(0, lanes)],
            zs.at[j, d],
            zr.at[j, d],
            (c, t),
        )

    def own_hop(j):
        return pltpu.make_async_copy(img.at[j, lines(s, rows), :], w.at[j, s], ks.at[j])

    def mirror(j):
        part = turned.at[j, lines(1 - member, rows), :]
        return remote(part, sib.at[j], ms.at[j], mr.at[j], twin)

    def busy(j):
        return group < reach.blocks(j)

    def combine(j, u):
        block = u // 2
        other = mates[j]
        mirrored = group < reach.blocks(other)
        alive = jnp.logical_and(reach.rows(j, s), block < reach.blocks(j))
        own = rem(u, 2) == member
        at = columns(block, width)

        def add(read):
            def one(n):
                line = pl.ds(pl.multiple_of(n * 32, 32), 32)
                w[j, u, line, :] = w[j, u, line, :] + jnp.where(mirrored, read(n), 0.0)

            each(rows // 32, one)

        @pl.when(jnp.logical_and(alive, own))
        def _():
            add(
                lambda n: turned[
                    other, pl.ds(pl.multiple_of(member * rows + n * 32, 32), 32), at
                ]
            )

        @pl.when(jnp.logical_and(alive, jnp.logical_not(own)))
        def _():
            add(lambda n: sib[other, pl.ds(pl.multiple_of(n * 32, 32), 32), at])

    def send(j, u):
        to = u // 2
        p = rem(u, 2)
        away = rem(to - c + chans, chans)

        def act(lanes):
            part = w.at[j, u, :, pl.ds(0, lanes)]
            target = sd.at[p * chans + c, j, :, pl.ds(0, lanes)]

            @pl.when(away == 0)
            def _():
                pltpu.make_async_copy(part, target, ls.at[j, p]).start()

            @pl.when(away != 0)
            def _():
                k = away * 2 + p
                remote(part, target, fs.at[j, k], fr.at[j, k], (to, s)).start()

        reach.spans(j, to, reach.rows(j, s), act)

    loads = load_operator(radial, turned, rs)
    each(per, begin)
    for load in loads:
        load.start()
    each(per, pass_on)
    split_operator(loads, turned, rh, rl)

    def launch(j):
        def one(n):
            d = far_first(n, strips)
            alive = reach.rows(j, rem(s + d, strips))
            reach.spans(j, group, alive, lambda lanes: hop(j, d, lanes).start())

        each(strips - 1, one)

    def work(j):
        depth = pick(j, levels) * rows

        def kept(lanes):
            target = y.at[j, lines(s, rows), pl.ds(0, lanes)]
            pltpu.make_async_copy(v.at[0, 0, :, pl.ds(0, lanes)], target, gl.at[j]).wait()

        reach.spans(j, group, reach.rows(j, s), kept)

        def arrived(n):
            d = n + 1
            u = rem(s - d + strips, strips)
            alive = reach.rows(j, u)
            reach.spans(j, group, alive, lambda lanes: arrive(j, d, u, lanes).wait_recv())

        each(strips - 1, arrived)

        @pl.when(busy(j))
        def _():
            lanes = reach.columns_alive(j, group)
            product(j, y, img, turned, rh, rl, yh, yl, depth, lanes, chans)
            mirror(j).start()
            own_hop(j).start()

        @pl.when(j == ORDER[0])
        def _():
            launch(j)

    def hear(j):
        @pl.when(busy(j))
        def _():
            mirror(j).wait_recv()
            own_hop(j).wait()

    def relay(i):
        j = pick(i, ORDER)

        def one(n):
            u = by_distance(n, group)
            d = rem(s - u + strips, strips)
            alive = jnp.logical_and(reach.rows(j, s), u != s)
            reach.spans(j, u // 2, alive, lambda lanes: hop(j, d, lanes).wait_recv())
            combine(j, u)
            send(j, u)

        each(strips, one)

    def finish(j):
        here = reach.rows(j, s)

        def sent(n):
            d = n + 1
            t = rem(s + d, strips)
            reach.spans(j, t // 2, here, lambda lanes: arrive(j, d, s, lanes).wait_send())
            alive = reach.rows(j, t)
            reach.spans(j, group, alive, lambda lanes: hop(j, d, lanes).wait_send())

        each(strips - 1, sent)

        @pl.when(busy(j))
        def _():
            mirror(j).wait_send()

        def passed(k, lanes):
            part = w.at[j, 0, :, pl.ds(0, lanes)]
            target = sd.at[rem(k, 2) * chans + c, j, :, pl.ds(0, lanes)]
            return remote(part, target, fs.at[j, k], fr.at[j, k], (rem(c + k // 2, chans), s))

        def one(n):
            k = n + 2
            to = rem(c + k // 2, chans)
            reach.spans(j, c, here, lambda lanes: back(j, k, lanes).wait_send())
            reach.spans(j, to, here, lambda lanes: passed(k, lanes).wait_send())
            reach.spans(j, c, here, lambda lanes: passed(k, lanes).wait_recv())

        def own(p):
            def act(lanes):
                part = w.at[j, 0, :, pl.ds(0, lanes)]
                target = sd.at[p * chans + c, j, :, pl.ds(0, lanes)]
                pltpu.make_async_copy(part, target, ls.at[j, p]).wait()

            reach.spans(j, c, here, act)

        each(2, own)
        each(2 * chans - 2, one)

    def step(i):
        @pl.when(i < per - 1)
        def _():
            launch(pick(i + 1, ORDER))

        relay(i)

    each(per, work)
    each(per, hear)
    each(per, step)
    each(per, finish)


def exchange(kernel, ident, outs, buffers, sems, *operands):
    chans = lax.axis_size("chan")
    strips = lax.axis_size("strip")
    return pl.pallas_call(
        functools.partial(kernel, chans, strips),
        out_shape=[jax.ShapeDtypeStruct(shape, jnp.float32) for shape in outs],
        in_specs=[SMEM] * (len(operands) - 2) + [ANY] * 2,
        out_specs=[ANY] * len(outs),
        scratch_shapes=[pltpu.VMEM(*buffer) for buffer in buffers]
        + [pltpu.SemaphoreType.DMA(n) for n in sems],
        compiler_params=pltpu.CompilerParams(
            collective_id=ident, has_side_effects=True, vmem_limit_bytes=62 * 2**20
        ),
    )(*operands)


def couple_kernel(count, last, ints, links, reals, *refs):
    if last:
        field, radial, base, out, pots = refs
    else:
        field, direct, mirror, out, dealt, pots = refs
    channels, height, width = field.shape[1:]
    orders = pots.shape[0]
    partners, extents, firsts, seconds = [2 + n * channels for n in range(4)]
    spacing = 8.0 / count
    row = ints[0] + pl.program_id(0) * height
    row = row + lax.broadcasted_iota(jnp.int32, (height, width), 0)
    col = ints[1] + lax.broadcasted_iota(jnp.int32, (height, width), 1)
    first = row.astype(jnp.float32) * spacing
    second = col.astype(jnp.float32) * spacing
    greater = jnp.maximum(first, second)
    root = jnp.sqrt(greater * greater + 1.0)
    ratio = jnp.minimum(first, second) / root
    pot = 1.0 / root
    for order in range(orders):
        pots[order] = pot
        pot = pot * ratio
    reach = jnp.maximum(row, col)

    def channel(c, carry):
        mine = ints[firsts + c]
        dealt_at = ints[seconds + c]
        if last:
            real_part = radial[0, dealt_at]
            imag_part = radial[1, dealt_at]
        else:
            other = ints[firsts + ints[partners + c]]
            real_part = direct[0, mine] + mirror[0, other]
            imag_part = direct[1, mine] + mirror[1, other]
        for order in range(orders):
            k = links[order, c]
            if not last:
                k = ints[firsts + k]
            c_real = reals[0, order, c]
            c_imag = reals[1, order, c]
            pot = pots[order]
            s_real = pot * field[0, k]
            s_imag = pot * field[1, k]
            real_part = real_part + (c_real * s_real - c_imag * s_imag)
            imag_part = imag_part + (c_real * s_imag + c_imag * s_real)
        live = reach < ints[extents + c]
        real_part = jnp.where(live, real_part, 0.0)
        imag_part = jnp.where(live, imag_part, 0.0)
        if last:
            real_part = 2.0 * real_part - base[0, mine]
            imag_part = 2.0 * imag_part - base[1, mine]
        else:
            dealt[0, dealt_at] = real_part
            dealt[1, dealt_at] = imag_part
        out[0, c] = real_part
        out[1, c] = imag_part
        return carry

    lax.fori_loop(0, channels, channel, 0)


def couple_tiles(count, scalars, orders, last, arrays):
    shape = arrays[0].shape
    height = 32
    block = pl.BlockSpec((2, shape[1], height, shape[3]), lambda n: (0, 0, n, 0))
    outs = 1 if last else 2
    return pl.pallas_call(
        functools.partial(couple_kernel, count, last),
        grid=(shape[2] // height,),
        out_shape=[jax.ShapeDtypeStruct(shape, jnp.float32)] * outs,
        in_specs=[SMEM] * len(scalars) + [block] * len(arrays),
        out_specs=[block] * outs,
        scratch_shapes=[pltpu.VMEM((orders, height, shape[3]), jnp.float32)],
    )(*scalars, *arrays)


FIRST_LEVELS = ((8, 7, 5, 4), (8, 8, 6, 4), (8, 8, 6, 5), (8, 8, 8, 4), (8, 8, 7, 6), (8, 8, 8, 8))
SECOND_LEVELS = ((8, 6, 4, 4), (8, 6, 5, 4), (8, 8, 4, 4), (8, 7, 5, 4), (8, 8, 5, 4), (8, 7, 6, 4), (8, 8, 6, 4), (8, 8, 6, 5), (8, 8, 7, 5), (8, 8, 8, 8))


def deal_kernel(
    per, rows, width, partner, extent, ints, order, mates, choice, choice_next,
    far, keys, lines_of, places,
):
    channels = extent.shape[0]
    chans = channels // per
    c = lax.axis_index("chan")
    ints[0] = lax.axis_index("strip") * rows
    ints[1] = c * width
    for n in range(2 * per):
        far[n] = 0

    def head(i):
        return jnp.minimum(i, partner[i])

    def key(i):
        keys[i] = jnp.where(i < partner[i], extent[i] + extent[partner[i]], -1)

    def before(k, i):
        tie = jnp.logical_and(extent[k] == extent[i], k < i)
        return jnp.logical_or(extent[k] > extent[i], tie)

    def first(i):
        line = i // per
        place = jnp.int32(0)
        for n in range(per):
            place = place + jnp.where(before(line * per + n, i), 1, 0)
        ints[2 + 2 * channels + i] = line * per + place
        far[place] = jnp.maximum(far[place], extent[i])

        @pl.when(line == c)
        def _():
            order[place] = i - line * per

        mine = keys[head(i)]
        rank = jnp.int32(0)
        for k in range(channels):
            tie = jnp.logical_and(keys[k] == mine, k < head(i))
            rank = rank + jnp.where(jnp.logical_or(keys[k] > mine, tie), 1, 0)
        lines_of[i] = jnp.where(rank < chans, rank, 2 * chans - 1 - rank)

    def second(i):
        line = lines_of[i]
        place = jnp.int32(0)
        for k in range(channels):
            ahead = jnp.logical_and(lines_of[k] == line, before(k, i))
            place = place + jnp.where(ahead, 1, 0)
        places[i] = place
        ints[2 + i] = partner[i]
        ints[2 + channels + i] = extent[i]
        ints[2 + 3 * channels + i] = line * per + place
        far[per + place] = jnp.maximum(far[per + place], extent[i])

    def match(i):
        @pl.when(lines_of[i] == c)
        def _():
            mates[places[i]] = places[partner[i]]

    each(channels, key)
    each(channels, first)
    each(channels, second)
    each(channels, match)
    for n, (table, out) in enumerate(((FIRST_LEVELS, choice), (SECOND_LEVELS, choice_next))):
        best = jnp.int32(len(table) - 1)
        for v in reversed(range(len(table) - 1)):
            fits = far[n * per] <= table[v][0] * rows
            for j in range(1, per):
                fits = jnp.logical_and(fits, far[n * per + j] <= table[v][j] * rows)
            best = jnp.where(fits, jnp.int32(v), best)
        out[0] = best


def deal(partner, extent, per, rows, width):
    channels = extent.shape[0]
    sizes = (2 + 4 * channels, per, per, 1, 1)
    scratch = (2 * per, channels, channels, channels)
    return pl.pallas_call(
        functools.partial(deal_kernel, per, rows, width),
        out_shape=[jax.ShapeDtypeStruct((size,), jnp.int32) for size in sizes],
        in_specs=[SMEM] * 2,
        out_specs=[SMEM] * len(sizes),
        scratch_shapes=[pltpu.SMEM((size,), jnp.int32) for size in scratch],
    )(partner, extent)


def sort_kernel(order, x, out, held, loads, stores):
    parts, per = held.shape[:2]
    pieces = [(p, j) for j in range(per) for p in range(parts)]

    def load(p, j):
        return pltpu.make_async_copy(x.at[p, order[j]], held.at[p, j], loads.at[p, j])

    def store(p, j):
        return pltpu.make_async_copy(held.at[p, j], out.at[p, j], stores.at[p, j])

    for p, j in pieces:
        load(p, j).start()
    for p, j in pieces:
        load(p, j).wait()
        store(p, j).start()
    for p, j in pieces:
        store(p, j).wait()


def sort_field(order, x):
    parts, per = x.shape[:2]
    return pl.pallas_call(
        sort_kernel,
        out_shape=jax.ShapeDtypeStruct(x.shape, x.dtype),
        in_specs=[SMEM, ANY],
        out_specs=ANY,
        scratch_shapes=[
            pltpu.VMEM(x.shape, x.dtype),
            pltpu.SemaphoreType.DMA((parts, per)),
            pltpu.SemaphoreType.DMA((parts, per)),
        ],
    )(order, x)


def local(wave_field, radial_op, coupling, couple, partner, extent):
    chans = lax.axis_size("chan")
    strips = lax.axis_size("strip")
    per, rows, grid = wave_field.shape[1:]
    width = grid // chans
    orders = coupling.shape[2]
    tiles = (2 * chans, per, rows, width)
    whole = (2, chans * per, rows, width)
    ints, order, mates, choice, choice_next = deal(partner, extent, per, rows, width)
    scalars = (ints, couple.T, coupling.transpose(0, 2, 1))
    buffers = [
        ((per, grid, width), jnp.float32),
        ((per, grid, width), jnp.float32),
        ((per, width, grid), jnp.float32),
        ((per, strips, rows, width), jnp.float32),
        ((grid, grid), jnp.bfloat16),
        ((grid, grid), jnp.bfloat16),
        ((grid, width), jnp.bfloat16),
        ((grid, width), jnp.bfloat16),
    ]
    one = (per,)
    ring = (per, strips)
    plane = (per, 2 * chans)
    sorted_field = sort_field(order, wave_field).reshape(2 * per, rows, grid)

    def first_call(n):
        def call(x):
            return exchange(
                functools.partial(first_kernel, FIRST_LEVELS[n]),
                n,
                [tiles, tiles, tiles],
                buffers,
                [ring, ring, one, (2 * chans,), (2 * chans,), (2,), (chans,)]
                + [one, ring, ring, plane, plane, one, plane, plane, (per, 2)],
                x,
                radial_op,
            )

        return call

    def second_call(n):
        def call(mates, v):
            return exchange(
                functools.partial(second_kernel, SECOND_LEVELS[n]),
                len(FIRST_LEVELS) + n,
                [tiles, tiles],
                buffers + [((per, rows, grid), jnp.float32)],
                [plane, plane, ring, ring, one, (chans,)]
                + [one, ring, ring, one, one, plane, plane, (per, 2)],
                mates,
                v,
                radial_op,
            )

        return call

    field, mirror, direct = lax.switch(
        choice[0], [first_call(n) for n in range(len(FIRST_LEVELS))], sorted_field
    )
    field = field.reshape(whole)
    first_step, dealt = couple_tiles(
        grid, scalars, orders, False, (field, direct.reshape(whole), mirror.reshape(whole))
    )
    _, radial = lax.switch(
        choice_next[0],
        [second_call(n) for n in range(len(SECOND_LEVELS))],
        mates,
        dealt.reshape(tiles),
    )
    second_step = couple_tiles(
        grid, scalars, orders, True, (first_step, radial.reshape(whole), field)
    )[0]
    return (first_step, second_step)


def dispatch(wave_field, *rest):
    chans = lax.axis_size("chan")
    strips = lax.axis_size("strip")
    per, rows, grid = wave_field.shape[1:]
    width = grid // chans
    aligned = width % 128 == 0 and rows % 64 == 0 and grid % 64 == 0
    if chans == 4 and strips == 8 and per == 4 and aligned:
        return local(wave_field, *rest)
    return general(wave_field, *rest)


def solution(mesh):
    placed = (P(None, "chan", "strip", None), P(), P(), P(), P(), P())
    return jax.shard_map(
        dispatch,
        mesh=mesh,
        in_specs=placed,
        out_specs=(P(None, None, "strip", "chan"), P(None, None, "strip", "chan")),
        check_vma=False,
    )
```
